32 devices in a mesh: fsdp: 16 (over z, x, core), sp: 2 (over y).
Axes of the slice: x: 2, y: 2, z: 4, core: 2. Of those that a mesh axis runs over, the one named last changes fastest.
Arguments:
- patches: float32 [16, 1024, 6144], P('fsdp', 'sp'), may hold values from -6 to 6
- segments: int32 [16, 1024], P('fsdp'), may hold values from 0 to 7, never falling along the last dimension, each value on 1 to 512 neighbouring positions
- w_in: float32 [6144, 768], P('fsdp'), may hold values from -0.078125 to 0.078125
- norm1_gain: float32 [768], P('fsdp'), may hold values from 0.5 to 1.5
- norm1_bias: float32 [768], P('fsdp'), may hold values from -1 to 1
- w_qkv: float32 [768, 2304], P('fsdp'), may hold values from -0.21875 to 0.21875
- w_out: float32 [768, 768], P('fsdp'), may hold values from -0.625 to 0.625
- norm2_gain: float32 [768], P('fsdp'), may hold values from 0.5 to 1.5
- norm2_bias: float32 [768], P('fsdp'), may hold values from -1 to 1
- w_up: float32 [768, 3072], P('fsdp'), may hold values from -0.21875 to 0.21875
- w_down: float32 [3072, 768], P('fsdp'), may hold values from -0.109375 to 0.109375
- cotangent: float32 [16, 1024, 768], P('fsdp', 'sp'), may hold values from -6 to 6
Outputs:
- block_out: float32 [16, 1024, 768], P('fsdp', 'sp')
- grad_patches: float32 [16, 1024, 6144], P('fsdp', 'sp')
- grad_w_in: float32 [6144, 768], P('fsdp')
- grad_norm1_gain: float32 [768], P('fsdp')
- grad_norm1_bias: float32 [768], P('fsdp')
- grad_w_qkv: float32 [768, 2304], P('fsdp')
- grad_w_out: float32 [768, 768], P('fsdp')
- grad_norm2_gain: float32 [768], P('fsdp')
- grad_norm2_bias: float32 [768], P('fsdp')
- grad_w_up: float32 [768, 3072], P('fsdp')
- grad_w_down: float32 [3072, 768], P('fsdp')
The draws below stay inside these ranges and needn't reach their ends.
Inputs may be any that keep to these rules, and one draw needn't show every extreme that they name: `segments`: along each sequence the document numbers never fall; each of the 8 documents has at least one row and at most 512 rows, and some document has exactly 512 rows.
All inputs are finite; a program needn't handle non-finite values.
Results may differ from the reference program's by a relative error of at most 0.0003.
Values sent between devices are 32-bit elements; how exact they have to be, the bound alone decides.
A program may use at most 256 MiB of HBM per device.

```python
import math
import jax
import jax.numpy as jnp
import numpy as np
from jax import lax

D = 768
HEADS = 12
HEAD_DIM = 64
FF = 3072
PATCH = 6144
SEQ_LEN = 1024
DOCS = 8
MOST_DOC = 512
SEQS = 16


def block_scale(own_key, shape, pieces, least, top_value):
    gain = 1.0
    for dim, blocks in pieces:
        steps = jax.random.uniform(jax.random.fold_in(jax.random.fold_in(own_key, 6), dim), (blocks,), jnp.float32, least / len(pieces), top_value / len(pieces))
        gain = gain * jnp.repeat(jnp.exp(steps), shape[dim] // blocks).reshape((-1,) + (1,) * (len(shape) - 1 - dim))
    return gain


def profile(amount, total, bound, slope):
    weights = [(1 << 20) // math.isqrt(grade ** slope) + 1 for grade in range(2, amount + 1)]
    surplus, holding = total - bound - (amount - 1), [1] * (amount - 1)
    while surplus > 0:
        free = [i for i in range(amount - 1) if holding[i] < bound]
        whole, remaining = sum([weights[i] for i in free]), surplus
        for i in free:
            extra = min(bound - holding[i], max(1, remaining * weights[i] // whole), surplus)
            holding[i] = holding[i] + extra
            surplus = surplus - extra
    return np.array([bound] + holding)


def ragged_sizes(key, amount, total, reach, lean):
    if amount == 2:
        one = jax.random.randint(key, (), max(1, total - reach), min(reach, total - 1) + 1)
        return jnp.stack([one, total - one])
    tallies = jnp.asarray(profile(amount, total, reach, lean), jnp.int32)
    twos = (amount - 1) // 2
    giver, taker = tallies[1:1 + 2 * twos:2], tallies[2:2 + 2 * twos:2]
    room = jnp.minimum(giver - 1, reach - taker)
    moved = jax.random.randint(jax.random.fold_in(key, 1), (twos,), 0, 1 << 20) % (room + 1)
    tallies = tallies.at[1:1 + 2 * twos:2].set(giver - moved).at[2:2 + 2 * twos:2].set(taker + moved)
    return tallies[jax.random.permutation(jax.random.fold_in(key, 2), amount)]


def normal_values(stream_key, dims, scale, bound, split=(), kind=jnp.bfloat16):
    array = scale * jax.random.normal(stream_key, dims, jnp.float32)
    if split:
        array = array * block_scale(stream_key, dims, split, -0.22, 0.18)
    return jnp.clip(array, -bound, bound).astype(kind)


def setup_inputs(seed: int = 0) -> dict:
    streams_of = jax.random.split(jax.random.key(seed), 13)
    patches = normal_values(streams_of[0], (SEQS, SEQ_LEN, PATCH), 1.0, 6.0, ((0, 16), (1, 2)), jnp.float32)
    segments = jax.vmap(lambda own: jnp.searchsorted(jnp.cumsum(ragged_sizes(own, DOCS, SEQ_LEN, MOST_DOC, 2)), jnp.arange(SEQ_LEN), side="right"))(jax.random.split(streams_of[1], SEQS)).reshape((SEQS, SEQ_LEN)).astype(jnp.int32)
    w_in = normal_values(streams_of[2], (PATCH, D), PATCH ** -0.5, 0.078125, ((0, 16),), jnp.float32)
    norm1_gain = jnp.clip(1.0 + 0.1 * jax.random.normal(streams_of[3], (D,), jnp.float32), 0.5, 1.5)
    norm1_bias = normal_values(streams_of[4], (D,), 0.2, 1.0, ((0, 16),), jnp.float32)
    w_qkv = normal_values(streams_of[5], (D, 3 * D), D ** -0.5, 0.21875, ((0, 16),), jnp.float32)
    w_out = normal_values(streams_of[6], (D, D), (D // 8) ** -0.5, 0.625, ((0, 16),), jnp.float32)
    norm2_gain = jnp.clip(1.0 + 0.1 * jax.random.normal(streams_of[7], (D,), jnp.float32), 0.5, 1.5)
    norm2_bias = normal_values(streams_of[8], (D,), 0.2, 1.0, ((0, 16),), jnp.float32)
    w_up = normal_values(streams_of[9], (D, FF), D ** -0.5, 0.21875, ((0, 16),), jnp.float32)
    w_down = normal_values(streams_of[10], (FF, D), FF ** -0.5, 0.109375, ((0, 16),), jnp.float32)
    cotangent = normal_values(streams_of[11], (SEQS, SEQ_LEN, D), 1.0, 6.0, ((0, 16), (1, 2)), jnp.float32)
    return dict(patches=patches, segments=segments, w_in=w_in, norm1_gain=norm1_gain, norm1_bias=norm1_bias, w_qkv=w_qkv, w_out=w_out, norm2_gain=norm2_gain, norm2_bias=norm2_bias, w_up=w_up, w_down=w_down, cotangent=cotangent)


@jax.custom_vjp
def low(v):
    return lax.optimization_barrier(v.astype(jnp.bfloat16)).astype(jnp.float32)

@jax.custom_vjp
def low_back(v):
    return v

def low_keep(v):
    return (low(v), None)

def low_pass(kept, grad):
    return (grad,)

def back_keep(v):
    return (v, None)

def back_low(kept, grad):
    return (low(grad),)
low.defvjp(low_keep, low_pass)
low_back.defvjp(back_keep, back_low)
EPSILON = 1e-05

def matmul(left_side, right_side):
    return jnp.dot(left_side, right_side, precision=lax.Precision.HIGHEST, preferred_element_type=jnp.float32)

def layer_norm(values, scaling, offset):
    average = lax.optimization_barrier(jnp.mean(values, axis=-1, keepdims=True))
    centred = values - average
    spread = lax.optimization_barrier(jnp.mean(centred * centred, axis=-1, keepdims=True))
    return centred * lax.rsqrt(spread + EPSILON) * scaling + offset

def attend_sequence(packed):
    queries, key_rows, value_rows, labels = packed
    length = labels.shape[0]
    factor = queries.shape[-1] ** (-0.5)
    scores = jnp.einsum('qhd,khd->hqk', queries, key_rows, precision=lax.Precision.HIGHEST) * factor
    places = jnp.arange(length, dtype=jnp.int32)
    allowed = (labels[:, None] == labels[None, :]) & (places[None, :] <= places[:, None])
    scores = jnp.where(allowed[None], scores, -1e+30)
    weights = jax.nn.softmax(scores, axis=-1)
    return jnp.einsum('hqk,khd->qhd', weights, value_rows, precision=lax.Precision.HIGHEST)

def reference(patches, segments, w_in, norm1_gain, norm1_bias, w_qkv, w_out, norm2_gain, norm2_bias, w_up, w_down, cotangent):
    checked = jax.checkpoint(attend_sequence)

    def forward(patch_data, in_weight, gain_one, offset_one, qkv_weight, out_weight, gain_two, offset_two, up_weight, down_weight):
        seq_count = patch_data.shape[0]
        seq_length = patch_data.shape[1]
        model_width = out_weight.shape[0]
        stream = matmul(patch_data.reshape(-1, patch_data.shape[2]), in_weight)
        normed = layer_norm(stream, gain_one, offset_one)
        projected = matmul(normed, qkv_weight)
        head_shape = (seq_count, seq_length, HEADS, HEAD_DIM)
        queries = projected[:, :model_width].reshape(head_shape)
        key_rows = projected[:, model_width:2 * model_width].reshape(head_shape)
        value_rows = projected[:, 2 * model_width:].reshape(head_shape)
        attended = lax.map(checked, (queries, key_rows, value_rows, segments))
        residual = stream + matmul(attended.reshape(-1, model_width), out_weight)
        normed_two = layer_norm(residual, gain_two, offset_two)
        hidden = jax.nn.gelu(matmul(normed_two, up_weight), approximate=True)
        result = residual + matmul(hidden, down_weight)
        return result.reshape(seq_count, seq_length, model_width)
    block_out, pullback = jax.vjp(forward, patches, w_in, norm1_gain, norm1_bias, w_qkv, w_out, norm2_gain, norm2_bias, w_up, w_down)
    gradients = pullback(cotangent)
    return (block_out, gradients[0], gradients[1], gradients[2], gradients[3], gradients[4], gradients[5], gradients[6], gradients[7], gradients[8], gradients[9])
```

```python
import jax
import jax.numpy as jnp
from jax import lax
from jax.experimental import pallas as pl
from jax.experimental.pallas import tpu as pltpu
from jax.sharding import PartitionSpec as P

HEADS = 12


EPSILON = 1e-05


def matmul(left_side, right_side):
    return jnp.dot(
        left_side, right_side, precision=lax.Precision.HIGH, preferred_element_type=jnp.float32
    )


def matmul_tn(left_side, right_side):
    return lax.dot_general(
        left_side,
        right_side,
        (((0,), (0,)), ((), ())),
        precision=lax.Precision.HIGH,
        preferred_element_type=jnp.float32,
    )


def matmul_nt(left_side, right_side):
    return lax.dot_general(
        left_side,
        right_side,
        (((1,), (1,)), ((), ())),
        precision=lax.Precision.HIGH,
        preferred_element_type=jnp.float32,
    )


def layer_norm(values, scaling, offset):
    average = jnp.mean(values, axis=-1, keepdims=True)
    centred = values - average
    spread = jnp.mean(centred * centred, axis=-1, keepdims=True)
    return centred * lax.rsqrt(spread + EPSILON) * scaling + offset


def gelu_tanh(values):
    return jax.nn.gelu(values, approximate=True)


def scored(queries, key_rows, labels):
    length = labels.shape[0]
    factor = queries.shape[-1] ** (-0.5)
    raw_scores = matmul_nt(queries, key_rows) * factor
    places = jnp.arange(length, dtype=jnp.int32)
    allowed = (labels[:, None] == labels[None, :]) & (places[None, :] <= places[:, None])
    return (raw_scores, allowed, factor)


def attend_one(packed):
    queries, key_rows, value_rows, labels = packed
    raw_scores, allowed, factor = scored(queries, key_rows, labels)
    masked = jnp.where(allowed, raw_scores, -1e30)
    row_max = jnp.max(masked, axis=1, keepdims=True)
    exponent = jnp.exp(masked - row_max)
    summed = jnp.sum(exponent, axis=1, keepdims=True)
    attended = matmul(exponent / summed, value_rows)
    return (attended, (row_max + jnp.log(summed))[:, 0])


def attend_back(packed):
    queries, key_rows, value_rows, attended, log_total, grad_attended, labels = packed
    raw_scores, allowed, factor = scored(queries, key_rows, labels)
    weights = jnp.where(
        allowed, jnp.exp(jnp.where(allowed, raw_scores - log_total[:, None], -1e30)), 0.0
    )
    grad_values = matmul_tn(weights, grad_attended)
    grad_weights = matmul_nt(grad_attended, value_rows)
    row_dot = jnp.sum(grad_attended * attended, axis=1, keepdims=True)
    grad_scores = weights * (grad_weights - row_dot) * factor
    grad_queries = matmul(grad_scores, key_rows)
    grad_keys = matmul_tn(grad_scores, queries)
    return (grad_queries, grad_keys, grad_values)


def to_batch(blocked, heads_local):
    seq_count, length, columns = blocked.shape
    head_dim = columns // heads_local
    return (
        blocked.reshape(seq_count, length, heads_local, head_dim)
        .transpose(0, 2, 1, 3)
        .reshape(seq_count * heads_local, length, head_dim)
    )


def from_batch(blocked, seq_count):
    batch_size, length, head_dim = blocked.shape
    heads_local = batch_size // seq_count
    return (
        blocked.reshape(seq_count, heads_local, length, head_dim)
        .transpose(0, 2, 1, 3)
        .reshape(seq_count, length, heads_local * head_dim)
    )


def shards(
    patches,
    segments,
    w_in,
    norm1_gain,
    norm1_bias,
    w_qkv,
    w_out,
    norm2_gain,
    norm2_bias,
    w_up,
    w_down,
    cotangent,
):
    seq_count, local_len, patch_width = patches.shape
    model_width = w_out.shape[1]
    heads_local = HEADS // lax.axis_size("sp")
    row_count = seq_count * local_len
    norm_params = jnp.stack([norm1_gain, norm1_bias, norm2_gain, norm2_bias])
    gathered = (
        lax.all_gather(w_in, "fsdp", axis=0, tiled=True),
        lax.all_gather(w_qkv, "fsdp", axis=0, tiled=True),
        lax.all_gather(w_out, "fsdp", axis=0, tiled=True),
        lax.all_gather(w_up, "fsdp", axis=0, tiled=True),
        lax.all_gather(w_down, "fsdp", axis=0, tiled=True),
        lax.all_gather(norm_params, "fsdp", axis=1, tiled=True),
    )
    in_full, qkv_full, out_full, up_full, down_full, norm_full = gathered
    patch_rows = patches.reshape(row_count, patch_width)
    stream = matmul(patch_rows, in_full)
    normed, norm1_pull = jax.vjp(layer_norm, stream, norm_full[0], norm_full[1])
    projected = matmul(normed, qkv_full)
    query_tok = projected[:, :model_width].reshape(seq_count, local_len, model_width)
    key_tok = projected[:, model_width : 2 * model_width].reshape(seq_count, local_len, model_width)
    value_tok = projected[:, 2 * model_width :].reshape(seq_count, local_len, model_width)
    query_seq, key_seq, value_seq = (
        lax.all_to_all(query_tok, "sp", split_axis=2, concat_axis=1, tiled=True),
        lax.all_to_all(key_tok, "sp", split_axis=2, concat_axis=1, tiled=True),
        lax.all_to_all(value_tok, "sp", split_axis=2, concat_axis=1, tiled=True),
    )
    labels = jnp.repeat(segments, heads_local, axis=0)
    query_batch = to_batch(query_seq, heads_local)
    key_batch = to_batch(key_seq, heads_local)
    value_batch = to_batch(value_seq, heads_local)
    attended, log_total = lax.map(attend_one, (query_batch, key_batch, value_batch, labels))
    attended_tok = lax.all_to_all(
        from_batch(attended, seq_count), "sp", split_axis=1, concat_axis=2, tiled=True
    )
    attended_rows = attended_tok.reshape(row_count, model_width)
    residual = stream + matmul(attended_rows, out_full)
    normed_two, norm2_pull = jax.vjp(layer_norm, residual, norm_full[2], norm_full[3])
    hidden_pre = matmul(normed_two, up_full)
    hidden, gelu_pull = jax.vjp(gelu_tanh, hidden_pre)
    result = residual + matmul(hidden, down_full)
    block_out = result.reshape(seq_count, local_len, model_width)
    in_back, qkv_back, out_back, up_back, down_back = (
        lax.all_gather(w_in, "fsdp", axis=0, tiled=True),
        lax.all_gather(w_qkv, "fsdp", axis=0, tiled=True),
        lax.all_gather(w_out, "fsdp", axis=0, tiled=True),
        lax.all_gather(w_up, "fsdp", axis=0, tiled=True),
        lax.all_gather(w_down, "fsdp", axis=0, tiled=True),
    )
    grad_rows = cotangent.reshape(row_count, model_width)
    grad_down = matmul_tn(hidden, grad_rows)
    (grad_pre,) = gelu_pull(matmul_nt(grad_rows, down_back))
    grad_up = matmul_tn(normed_two, grad_pre)
    grad_resid_norm, grad_gain_two, grad_offset_two = norm2_pull(matmul_nt(grad_pre, up_back))
    grad_resid = grad_rows + grad_resid_norm
    grad_out = matmul_tn(attended_rows, grad_resid)
    grad_att = matmul_nt(grad_resid, out_back).reshape(seq_count, local_len, model_width)
    grad_att_seq = lax.all_to_all(grad_att, "sp", split_axis=2, concat_axis=1, tiled=True)
    grad_query, grad_key, grad_value = lax.map(
        attend_back,
        (
            query_batch,
            key_batch,
            value_batch,
            attended,
            log_total,
            to_batch(grad_att_seq, heads_local),
            labels,
        ),
    )
    back_query, back_key, back_value = (
        lax.all_to_all(
            from_batch(grad_query, seq_count), "sp", split_axis=1, concat_axis=2, tiled=True
        ),
        lax.all_to_all(
            from_batch(grad_key, seq_count), "sp", split_axis=1, concat_axis=2, tiled=True
        ),
        lax.all_to_all(
            from_batch(grad_value, seq_count), "sp", split_axis=1, concat_axis=2, tiled=True
        ),
    )
    grad_proj = jnp.concatenate([back_query, back_key, back_value], axis=2).reshape(
        row_count, 3 * model_width
    )
    grad_qkv = matmul_tn(normed, grad_proj)
    grad_stream_norm, grad_gain_one, grad_offset_one = norm1_pull(matmul_nt(grad_proj, qkv_back))
    grad_stream = grad_resid + grad_stream_norm
    grad_in = matmul_tn(patch_rows, grad_stream)
    grad_patch = matmul_nt(grad_stream, in_back).reshape(seq_count, local_len, patch_width)
    every_part = (
        lax.psum_scatter(grad_in, "fsdp", scatter_dimension=0, tiled=True),
        lax.psum_scatter(grad_qkv, "fsdp", scatter_dimension=0, tiled=True),
        lax.psum_scatter(grad_out, "fsdp", scatter_dimension=0, tiled=True),
        lax.psum_scatter(grad_up, "fsdp", scatter_dimension=0, tiled=True),
        lax.psum_scatter(grad_down, "fsdp", scatter_dimension=0, tiled=True),
        lax.psum_scatter(
            jnp.stack([grad_gain_one, grad_offset_one, grad_gain_two, grad_offset_two]),
            "fsdp",
            scatter_dimension=1,
            tiled=True,
        ),
    )
    total_in, total_qkv, total_out, total_up, total_down, norm_total = lax.psum(
        (every_part[0], every_part[1], every_part[2], every_part[3], every_part[4], every_part[5]),
        "sp",
    )
    norm_first = norm_total[0:2]
    norm_second = norm_total[2:4]
    return (
        block_out,
        grad_patch,
        total_in,
        norm_first[0],
        norm_first[1],
        total_qkv,
        total_out,
        norm_second[0],
        norm_second[1],
        total_up,
        total_down,
    )


LANES = 128
BLOCK = 256
BF = jnp.bfloat16
F32 = jnp.float32


def halves(values):
    high = values.astype(BF).astype(F32)
    return high, values - high


def roll_half(values):
    return pltpu.roll(values, LANES // 2, 1)


def low_lanes(rows):
    return lax.broadcasted_iota(jnp.int32, (rows, LANES), 1) < LANES // 2


def pair_tiles(values):
    high, low = halves(values)
    first = low_lanes(values.shape[0])
    return (
        jnp.where(first, high, roll_half(low)).astype(BF),
        jnp.where(first, roll_half(high), low).astype(BF),
    )


def spread_tiles(values):
    high, low = halves(values)
    first = low_lanes(values.shape[0])
    high_r, low_r = roll_half(high), roll_half(low)
    return (
        jnp.concatenate([jnp.where(first, high, high_r), jnp.where(first, low, low_r)], axis=1).astype(BF),
        jnp.concatenate([jnp.where(first, high_r, high), jnp.where(first, low_r, low)], axis=1).astype(BF),
    )


def nt(left, right):
    return lax.dot_general(left, right, (((1,), (1,)), ((), ())), preferred_element_type=F32)


def nn(left, right):
    return lax.dot_general(left, right, (((1,), (0,)), ((), ())), preferred_element_type=F32)


def tn(left, right):
    return lax.dot_general(left, right, (((0,), (0,)), ((), ())), preferred_element_type=F32)


def split_bf(values):
    high = values.astype(BF)
    return high, (values - high.astype(F32)).astype(BF)


def forward_kernel(pos_ref, seg_ref, *refs):
    (q_own, k_own, v_own, q_in, k_in, v_in, seg_col, seg_row,
     o_own, o_out, lse_ref, tq, hk, tv, out_s) = refs
    rows = q_own.shape[0]
    own = pl.multiple_of(pos_ref[0] * rows, rows)
    other = pl.multiple_of((1 - pos_ref[0]) * rows, rows)
    for place, q, k, v in ((own, q_own, k_own, v_own), (other, q_in, k_in, v_in)):
        span = pl.ds(place, rows)
        for head, tile in enumerate(pair_tiles(q[...] * 0.125)):
            tq[head, span, :] = jnp.concatenate([tile, tile], axis=1)
        for head, tile in enumerate(spread_tiles(k[...])):
            hk[head, span, :] = tile
        for head, tile in enumerate(pair_tiles(v[...])):
            tv[head, span, :] = tile
    blocks = 2 * rows // BLOCK
    first = low_lanes(BLOCK)

    def query_block(i, carry):
        q_span = pl.ds(pl.multiple_of(i * BLOCK, BLOCK), BLOCK)
        first_label = seg_ref[i * BLOCK]
        start = jnp.int32(0)
        for j in range(blocks):
            start = start + jnp.where((j < i) & (seg_ref[j * BLOCK + BLOCK - 1] < first_label), 1, 0)
        label = seg_col[q_span, :1]
        q_place = i * BLOCK + lax.broadcasted_iota(jnp.int32, (BLOCK, BLOCK), 0)

        def key_block(step, state):
            j = i - step
            k_span = pl.ds(pl.multiple_of(j * BLOCK, BLOCK), BLOCK)
            k_place = j * BLOCK + lax.broadcasted_iota(jnp.int32, (BLOCK, BLOCK), 1)
            allowed = (label == seg_row[j]) & (k_place <= q_place)
            new_state = []
            for head in range(2):
                top, total, acc = state[head]
                scores = nt(tq[head, q_span, :], hk[head, k_span, :])
                scores = jnp.where(allowed, scores, -1e30)
                new_top = jnp.maximum(top, jnp.max(scores, axis=1, keepdims=True))
                weight = jnp.exp(scores - new_top)
                keep = jnp.exp(top - new_top)
                high, low = split_bf(weight)
                values = tv[head, k_span, :]
                new_state.append((
                    new_top,
                    total * keep + jnp.sum(weight, axis=1, keepdims=True),
                    acc * keep + nn(high, values) + nn(low, values),
                ))
            return tuple(new_state)

        init = (
            jnp.full((BLOCK, 1), -1e30, F32),
            jnp.zeros((BLOCK, 1), F32),
            jnp.zeros((BLOCK, LANES), F32),
        )
        state = lax.fori_loop(0, i - start + 1, key_block, (init, init))
        outs, logs = [], []
        for top, total, acc in state:
            outs.append((acc + roll_half(acc)) / total)
            logs.append(jnp.broadcast_to(top + jnp.log(total), (BLOCK, LANES)))
        out_s[q_span, :] = jnp.where(first, outs[0], outs[1])
        lse_ref[q_span, :] = jnp.where(first, logs[0], logs[1])
        return carry

    lax.fori_loop(0, blocks, query_block, 0)
    o_own[...] = out_s[pl.ds(own, rows), :]
    o_out[...] = out_s[pl.ds(other, rows), :]


def attend_forward(own, received, position, labels):
    rows, columns = own.shape
    width = columns // 3
    pairs = width // LANES
    length = 2 * rows

    def part(which):
        return pl.BlockSpec((rows, LANES), lambda g, *_: (0, which * pairs + g))

    whole = pl.BlockSpec((rows, LANES), lambda g, *_: (0, g))
    return pl.pallas_call(
        forward_kernel,
        grid_spec=pltpu.PrefetchScalarGridSpec(
            num_scalar_prefetch=2,
            grid=(pairs,),
            in_specs=[part(0), part(1), part(2), part(0), part(1), part(2),
                      pl.BlockSpec((length, LANES), lambda g, *_: (0, 0)),
                      pl.BlockSpec((length // BLOCK, 1, BLOCK), lambda g, *_: (0, 0, 0))],
            out_specs=[whole, whole, pl.BlockSpec((length, LANES), lambda g, *_: (0, g))],
            scratch_shapes=[
                pltpu.VMEM((2, length, 2 * LANES), BF),
                pltpu.VMEM((2, length, 2 * LANES), BF),
                pltpu.VMEM((2, length, LANES), BF),
                pltpu.VMEM((length, LANES), F32),
            ],
        ),
        out_shape=[
            jax.ShapeDtypeStruct((rows, width), F32),
            jax.ShapeDtypeStruct((rows, width), F32),
            jax.ShapeDtypeStruct((length, width), F32),
        ],
        cost_estimate=pl.CostEstimate(flops=20 * 10**9, bytes_accessed=8 * rows * columns * 3, transcendentals=length * width * 8),
        compiler_params=pltpu.CompilerParams(vmem_limit_bytes=48 * 1024 * 1024),
        name="attend_forward",
    )(position, labels, own, own, own, received, received, received,
      jnp.broadcast_to(labels[:, None], (length, LANES)), labels.reshape(length // BLOCK, 1, BLOCK))


def backward_kernel(pos_ref, seg_ref, *refs):
    (q_own, k_own, v_own, q_in, k_in, v_in, o_own, o_in, g_own, g_in, lse_ref, seg_col, seg_row,
     gq_own, gk_own, gv_own, gq_out, gk_out, gv_out,
     tq, hk, tk, hv, tg, lse_t, delta_t, gq_s, gk_s, gv_s) = refs
    rows = q_own.shape[0]
    length = 2 * rows
    own = pl.multiple_of(pos_ref[0] * rows, rows)
    other = pl.multiple_of((1 - pos_ref[0]) * rows, rows)
    half = LANES // 2
    for place, q, k, v, o, g in ((own, q_own, k_own, v_own, o_own, g_own), (other, q_in, k_in, v_in, o_in, g_in)):
        span = pl.ds(place, rows)
        for head, tile in enumerate(pair_tiles(q[...] * 0.125)):
            tq[head, span, :] = jnp.concatenate([tile, tile], axis=1)
        for head, tile in enumerate(pair_tiles(g[...])):
            tg[head, span, :] = jnp.concatenate([tile, tile], axis=1)
        for head, tile in enumerate(spread_tiles(k[...])):
            hk[head, span, :] = tile
        for head, tile in enumerate(spread_tiles(v[...])):
            hv[head, span, :] = tile
        for head, tile in enumerate(pair_tiles(k[...])):
            tk[head, span, :] = tile
        turned = jnp.transpose(o[...] * g[...])
        for head in range(2):
            delta_t[head, 0:1, span] = jnp.sum(turned[head * half:(head + 1) * half], axis=0, keepdims=True)
    turned = jnp.transpose(lse_ref[...])
    for head in range(2):
        lse_t[head, 0:1, :] = turned[head * half:head * half + 1]
    blocks = length // BLOCK
    first = low_lanes(BLOCK)
    gq_s[...] = jnp.zeros_like(gq_s)

    def key_block(j, carry):
        k_span = pl.ds(pl.multiple_of(j * BLOCK, BLOCK), BLOCK)
        last_label = seg_ref[j * BLOCK + BLOCK - 1]
        count = jnp.int32(1)
        for i in range(blocks):
            count = count + jnp.where((i > j) & (seg_ref[i * BLOCK] <= last_label), 1, 0)
        label = seg_col[k_span, :1]
        k_place = j * BLOCK + lax.broadcasted_iota(jnp.int32, (BLOCK, BLOCK), 0)

        def query_block(step, state):
            i = j + step
            q_span = pl.ds(pl.multiple_of(i * BLOCK, BLOCK), BLOCK)
            q_place = i * BLOCK + lax.broadcasted_iota(jnp.int32, (BLOCK, BLOCK), 1)
            allowed = (label == seg_row[i]) & (k_place <= q_place)
            new_state = []
            for head in range(2):
                grad_k, grad_v = state[head]
                query = tq[head, q_span, :]
                grad = tg[head, q_span, :]
                scores = nt(hk[head, k_span, :], query)
                weight = jnp.exp(jnp.where(allowed, scores - lse_t[head, 0:1, q_span], -1e30))
                grad_weight = nt(hv[head, k_span, :], grad)
                grad_score = weight * (grad_weight - delta_t[head, 0:1, q_span])
                w_high, w_low = split_bf(weight)
                s_high, s_low = split_bf(grad_score)
                grad_v = grad_v + nn(w_high, grad[:, :LANES]) + nn(w_low, grad[:, :LANES])
                grad_k = grad_k + nn(s_high, query[:, :LANES]) + nn(s_low, query[:, :LANES])
                keys = tk[head, k_span, :]
                gq_s[head, q_span, :] += tn(s_high, keys) + tn(s_low, keys)
                new_state.append((grad_k, grad_v))
            return tuple(new_state)

        zero = jnp.zeros((BLOCK, LANES), F32)
        state = lax.fori_loop(0, count, query_block, ((zero, zero), (zero, zero)))
        for slot, store in ((0, gk_s), (1, gv_s)):
            left, right = state[0][slot], state[1][slot]
            store[k_span, :] = jnp.where(first, left + roll_half(left), right + roll_half(right))
        return carry

    lax.fori_loop(0, blocks, key_block, 0)
    wide = low_lanes(rows)
    for place, gq, gk, gv in ((own, gq_own, gk_own, gv_own), (other, gq_out, gk_out, gv_out)):
        span = pl.ds(place, rows)
        left, right = gq_s[0, span, :], gq_s[1, span, :]
        gq[...] = jnp.where(wide, left + roll_half(left), right + roll_half(right)) * 0.125
        gk[...] = gk_s[span, :]
        gv[...] = gv_s[span, :]


def attend_backward(own, received, out_own, out_in, grad_own, grad_in, logs, position, labels):
    rows, columns = own.shape
    width = columns // 3
    pairs = width // LANES
    length = 2 * rows

    def part(which):
        return pl.BlockSpec((rows, LANES), lambda g, *_: (0, which * pairs + g))

    whole = pl.BlockSpec((rows, LANES), lambda g, *_: (0, g))
    outs = pl.pallas_call(
        backward_kernel,
        grid_spec=pltpu.PrefetchScalarGridSpec(
            num_scalar_prefetch=2,
            grid=(pairs,),
            in_specs=[part(0), part(1), part(2), part(0), part(1), part(2), whole, whole, whole, whole,
                      pl.BlockSpec((length, LANES), lambda g, *_: (0, g)),
                      pl.BlockSpec((length, LANES), lambda g, *_: (0, 0)),
                      pl.BlockSpec((length // BLOCK, 1, BLOCK), lambda g, *_: (0, 0, 0))],
            out_specs=[whole] * 6,
            scratch_shapes=[
                pltpu.VMEM((2, length, 2 * LANES), BF),
                pltpu.VMEM((2, length, 2 * LANES), BF),
                pltpu.VMEM((2, length, LANES), BF),
                pltpu.VMEM((2, length, 2 * LANES), BF),
                pltpu.VMEM((2, length, 2 * LANES), BF),
                pltpu.VMEM((2, 8, length), F32),
                pltpu.VMEM((2, 8, length), F32),
                pltpu.VMEM((2, length, LANES), F32),
                pltpu.VMEM((length, LANES), F32),
                pltpu.VMEM((length, LANES), F32),
            ],
        ),
        out_shape=[jax.ShapeDtypeStruct((rows, width), F32)] * 6,
        cost_estimate=pl.CostEstimate(flops=40 * 10**9, bytes_accessed=8 * rows * columns * 5, transcendentals=length * width * 8),
        compiler_params=pltpu.CompilerParams(vmem_limit_bytes=56 * 1024 * 1024),
        name="attend_backward",
    )(position, labels, own, own, own, received, received, received, out_own, out_in, grad_own, grad_in, logs,
      jnp.broadcast_to(labels[:, None], (length, LANES)), labels.reshape(length // BLOCK, 1, BLOCK))
    return outs


def fast_shards(
    patches, segments, w_in, norm1_gain, norm1_bias, w_qkv, w_out, norm2_gain, norm2_bias, w_up, w_down, cotangent
):
    _, rows, patch_width = patches.shape
    width = w_out.shape[1]
    position = lax.axis_index("sp")
    places = position[None].astype(jnp.int32)
    labels = segments[0]
    norm_params = jnp.stack([norm1_gain, norm1_bias, norm2_gain, norm2_bias])
    in_full = lax.all_gather(w_in, "fsdp", axis=0, tiled=True)
    norm_full = lax.all_gather(norm_params, "fsdp", axis=1, tiled=True)
    qkv_full = lax.all_gather(w_qkv, "fsdp", axis=0, tiled=True)
    out_full = lax.all_gather(w_out, "fsdp", axis=0, tiled=True)
    up_full = lax.all_gather(w_up, "fsdp", axis=0, tiled=True)
    down_full = lax.all_gather(w_down, "fsdp", axis=0, tiled=True)
    patch_rows = patches[0]
    stream = matmul(patch_rows, in_full)
    normed, norm1_pull = jax.vjp(layer_norm, stream, norm_full[0], norm_full[1])
    half = width // 2
    by_half = qkv_full.reshape(width, 3, 2, half)
    swap = [(0, 1), (1, 0)]

    def columns_of(which):
        return lax.dynamic_index_in_dim(by_half, which, 2, keepdims=False).reshape(width, 3 * half)

    own_columns = columns_of(position)
    sent_columns = columns_of(1 - position)
    received = lax.ppermute(matmul(normed, sent_columns), "sp", swap)
    own = matmul(normed, own_columns)
    out_own, out_sent, logs = attend_forward(own, received, places, labels)
    out_in = lax.ppermute(out_sent, "sp", swap)

    def whole_rows(mine, theirs):
        return jnp.where(position == 0, jnp.concatenate([mine, theirs], 1), jnp.concatenate([theirs, mine], 1))

    attended_rows = whole_rows(out_own, out_in)
    residual = stream + matmul(attended_rows, out_full)
    normed_two, norm2_pull = jax.vjp(layer_norm, residual, norm_full[2], norm_full[3])
    hidden_pre = matmul(normed_two, up_full)
    hidden, gelu_pull = jax.vjp(gelu_tanh, hidden_pre)
    block_out = residual + matmul(hidden, down_full)
    grad_rows = cotangent[0]
    grad_down = matmul_tn(hidden, grad_rows)
    (grad_pre,) = gelu_pull(matmul_nt(grad_rows, down_full))
    grad_up = matmul_tn(normed_two, grad_pre)
    grad_resid_norm, grad_gain_two, grad_offset_two = norm2_pull(matmul_nt(grad_pre, up_full))
    grad_resid = grad_rows + grad_resid_norm
    grad_out = matmul_tn(attended_rows, grad_resid)
    out_by_half = out_full.reshape(2, half, width)
    grad_sent = matmul_nt(grad_resid, lax.dynamic_index_in_dim(out_by_half, 1 - position, 0, keepdims=False))
    grad_in = lax.ppermute(grad_sent, "sp", swap)
    grad_own = matmul_nt(grad_resid, lax.dynamic_index_in_dim(out_by_half, position, 0, keepdims=False))
    parts = attend_backward(own, received, out_own, out_sent, grad_own, grad_in, logs, places, labels)
    mine = jnp.concatenate(parts[:3], axis=1)
    theirs = lax.ppermute(jnp.concatenate(parts[3:], axis=1), "sp", swap)
    grad_normed = matmul_nt(mine, own_columns) + matmul_nt(theirs, sent_columns)
    grad_proj = whole_rows(mine.reshape(rows, 3, half), theirs.reshape(rows, 3, half))
    low = jnp.where(position == 0, mine, theirs).reshape(rows, 3, 1, half)
    high = jnp.where(position == 0, theirs, mine).reshape(rows, 3, 1, half)
    grad_proj = jnp.concatenate([low, high], axis=2).reshape(rows, 3 * width)
    grad_qkv = matmul_tn(normed, grad_proj)
    grad_stream_norm, grad_gain_one, grad_offset_one = norm1_pull(grad_normed)
    grad_stream = grad_resid + grad_stream_norm
    grad_w_in = matmul_tn(patch_rows, grad_stream)
    grad_patch = matmul_nt(grad_stream, in_full)

    def scattered(value, dimension=0):
        return lax.psum_scatter(value, "fsdp", scatter_dimension=dimension, tiled=True)

    totals = lax.psum(
        (
            scattered(grad_w_in),
            scattered(grad_qkv),
            scattered(grad_out),
            scattered(grad_up),
            scattered(grad_down),
            scattered(jnp.stack([grad_gain_one, grad_offset_one, grad_gain_two, grad_offset_two]), 1),
        ),
        "sp",
    )
    norms = totals[5]
    return (
        block_out[None], grad_patch[None], totals[0], norms[0], norms[1], totals[1], totals[2], norms[2], norms[3],
        totals[3], totals[4],
    )


def solution(mesh):
    sharded = P("fsdp", "sp", None)
    matrix = P("fsdp", None)
    vector = P("fsdp")
    fast = mesh.shape["fsdp"] == 16 and mesh.shape["sp"] == 2
    return jax.shard_map(
        fast_shards if fast else shards,
        mesh=mesh,
        in_specs=(sharded, matrix, matrix, vector, vector, matrix, matrix, vector, vector, matrix, matrix, sharded),
        out_specs=(sharded, sharded, matrix, vector, vector, matrix, matrix, vector, vector, matrix, matrix),
        check_vma=False,
    )
```

```python
import functools

import jax
import jax.numpy as jnp
from jax import lax
from jax.experimental import pallas as pl
from jax.experimental.pallas import tpu as pltpu
from jax.sharding import PartitionSpec as P

HEADS = 12


EPSILON = 1e-05


def matmul(left_side, right_side):
    return jnp.dot(
        left_side, right_side, precision=lax.Precision.HIGH, preferred_element_type=jnp.float32
    )


def matmul_tn(left_side, right_side):
    return lax.dot_general(
        left_side,
        right_side,
        (((0,), (0,)), ((), ())),
        precision=lax.Precision.HIGH,
        preferred_element_type=jnp.float32,
    )


def matmul_nt(left_side, right_side):
    return lax.dot_general(
        left_side,
        right_side,
        (((1,), (1,)), ((), ())),
        precision=lax.Precision.HIGH,
        preferred_element_type=jnp.float32,
    )


def layer_norm(values, scaling, offset):
    average = jnp.mean(values, axis=-1, keepdims=True)
    centred = values - average
    spread = jnp.mean(centred * centred, axis=-1, keepdims=True)
    return centred * lax.rsqrt(spread + EPSILON) * scaling + offset


def gelu_tanh(values):
    return jax.nn.gelu(values, approximate=True)


def scored(queries, key_rows, labels):
    length = labels.shape[0]
    factor = queries.shape[-1] ** (-0.5)
    raw_scores = matmul_nt(queries, key_rows) * factor
    places = jnp.arange(length, dtype=jnp.int32)
    allowed = (labels[:, None] == labels[None, :]) & (places[None, :] <= places[:, None])
    return (raw_scores, allowed, factor)


def attend_one(packed):
    queries, key_rows, value_rows, labels = packed
    raw_scores, allowed, factor = scored(queries, key_rows, labels)
    masked = jnp.where(allowed, raw_scores, -1e30)
    row_max = jnp.max(masked, axis=1, keepdims=True)
    exponent = jnp.exp(masked - row_max)
    summed = jnp.sum(exponent, axis=1, keepdims=True)
    attended = matmul(exponent / summed, value_rows)
    return (attended, (row_max + jnp.log(summed))[:, 0])


def attend_back(packed):
    queries, key_rows, value_rows, attended, log_total, grad_attended, labels = packed
    raw_scores, allowed, factor = scored(queries, key_rows, labels)
    weights = jnp.where(
        allowed, jnp.exp(jnp.where(allowed, raw_scores - log_total[:, None], -1e30)), 0.0
    )
    grad_values = matmul_tn(weights, grad_attended)
    grad_weights = matmul_nt(grad_attended, value_rows)
    row_dot = jnp.sum(grad_attended * attended, axis=1, keepdims=True)
    grad_scores = weights * (grad_weights - row_dot) * factor
    grad_queries = matmul(grad_scores, key_rows)
    grad_keys = matmul_tn(grad_scores, queries)
    return (grad_queries, grad_keys, grad_values)


def to_batch(blocked, heads_local):
    seq_count, length, columns = blocked.shape
    head_dim = columns // heads_local
    return (
        blocked.reshape(seq_count, length, heads_local, head_dim)
        .transpose(0, 2, 1, 3)
        .reshape(seq_count * heads_local, length, head_dim)
    )


def from_batch(blocked, seq_count):
    batch_size, length, head_dim = blocked.shape
    heads_local = batch_size // seq_count
    return (
        blocked.reshape(seq_count, heads_local, length, head_dim)
        .transpose(0, 2, 1, 3)
        .reshape(seq_count, length, heads_local * head_dim)
    )


def shards(
    patches,
    segments,
    w_in,
    norm1_gain,
    norm1_bias,
    w_qkv,
    w_out,
    norm2_gain,
    norm2_bias,
    w_up,
    w_down,
    cotangent,
):
    seq_count, local_len, patch_width = patches.shape
    model_width = w_out.shape[1]
    heads_local = HEADS // lax.axis_size("sp")
    row_count = seq_count * local_len
    norm_params = jnp.stack([norm1_gain, norm1_bias, norm2_gain, norm2_bias])
    gathered = (
        lax.all_gather(w_in, "fsdp", axis=0, tiled=True),
        lax.all_gather(w_qkv, "fsdp", axis=0, tiled=True),
        lax.all_gather(w_out, "fsdp", axis=0, tiled=True),
        lax.all_gather(w_up, "fsdp", axis=0, tiled=True),
        lax.all_gather(w_down, "fsdp", axis=0, tiled=True),
        lax.all_gather(norm_params, "fsdp", axis=1, tiled=True),
    )
    in_full, qkv_full, out_full, up_full, down_full, norm_full = gathered
    patch_rows = patches.reshape(row_count, patch_width)
    stream = matmul(patch_rows, in_full)
    normed, norm1_pull = jax.vjp(layer_norm, stream, norm_full[0], norm_full[1])
    projected = matmul(normed, qkv_full)
    query_tok = projected[:, :model_width].reshape(seq_count, local_len, model_width)
    key_tok = projected[:, model_width : 2 * model_width].reshape(seq_count, local_len, model_width)
    value_tok = projected[:, 2 * model_width :].reshape(seq_count, local_len, model_width)
    query_seq, key_seq, value_seq = (
        lax.all_to_all(query_tok, "sp", split_axis=2, concat_axis=1, tiled=True),
        lax.all_to_all(key_tok, "sp", split_axis=2, concat_axis=1, tiled=True),
        lax.all_to_all(value_tok, "sp", split_axis=2, concat_axis=1, tiled=True),
    )
    labels = jnp.repeat(segments, heads_local, axis=0)
    query_batch = to_batch(query_seq, heads_local)
    key_batch = to_batch(key_seq, heads_local)
    value_batch = to_batch(value_seq, heads_local)
    attended, log_total = lax.map(attend_one, (query_batch, key_batch, value_batch, labels))
    attended_tok = lax.all_to_all(
        from_batch(attended, seq_count), "sp", split_axis=1, concat_axis=2, tiled=True
    )
    attended_rows = attended_tok.reshape(row_count, model_width)
    residual = stream + matmul(attended_rows, out_full)
    normed_two, norm2_pull = jax.vjp(layer_norm, residual, norm_full[2], norm_full[3])
    hidden_pre = matmul(normed_two, up_full)
    hidden, gelu_pull = jax.vjp(gelu_tanh, hidden_pre)
    result = residual + matmul(hidden, down_full)
    block_out = result.reshape(seq_count, local_len, model_width)
    in_back, qkv_back, out_back, up_back, down_back = (
        lax.all_gather(w_in, "fsdp", axis=0, tiled=True),
        lax.all_gather(w_qkv, "fsdp", axis=0, tiled=True),
        lax.all_gather(w_out, "fsdp", axis=0, tiled=True),
        lax.all_gather(w_up, "fsdp", axis=0, tiled=True),
        lax.all_gather(w_down, "fsdp", axis=0, tiled=True),
    )
    grad_rows = cotangent.reshape(row_count, model_width)
    grad_down = matmul_tn(hidden, grad_rows)
    (grad_pre,) = gelu_pull(matmul_nt(grad_rows, down_back))
    grad_up = matmul_tn(normed_two, grad_pre)
    grad_resid_norm, grad_gain_two, grad_offset_two = norm2_pull(matmul_nt(grad_pre, up_back))
    grad_resid = grad_rows + grad_resid_norm
    grad_out = matmul_tn(attended_rows, grad_resid)
    grad_att = matmul_nt(grad_resid, out_back).reshape(seq_count, local_len, model_width)
    grad_att_seq = lax.all_to_all(grad_att, "sp", split_axis=2, concat_axis=1, tiled=True)
    grad_query, grad_key, grad_value = lax.map(
        attend_back,
        (
            query_batch,
            key_batch,
            value_batch,
            attended,
            log_total,
            to_batch(grad_att_seq, heads_local),
            labels,
        ),
    )
    back_query, back_key, back_value = (
        lax.all_to_all(
            from_batch(grad_query, seq_count), "sp", split_axis=1, concat_axis=2, tiled=True
        ),
        lax.all_to_all(
            from_batch(grad_key, seq_count), "sp", split_axis=1, concat_axis=2, tiled=True
        ),
        lax.all_to_all(
            from_batch(grad_value, seq_count), "sp", split_axis=1, concat_axis=2, tiled=True
        ),
    )
    grad_proj = jnp.concatenate([back_query, back_key, back_value], axis=2).reshape(
        row_count, 3 * model_width
    )
    grad_qkv = matmul_tn(normed, grad_proj)
    grad_stream_norm, grad_gain_one, grad_offset_one = norm1_pull(matmul_nt(grad_proj, qkv_back))
    grad_stream = grad_resid + grad_stream_norm
    grad_in = matmul_tn(patch_rows, grad_stream)
    grad_patch = matmul_nt(grad_stream, in_back).reshape(seq_count, local_len, patch_width)
    every_part = (
        lax.psum_scatter(grad_in, "fsdp", scatter_dimension=0, tiled=True),
        lax.psum_scatter(grad_qkv, "fsdp", scatter_dimension=0, tiled=True),
        lax.psum_scatter(grad_out, "fsdp", scatter_dimension=0, tiled=True),
        lax.psum_scatter(grad_up, "fsdp", scatter_dimension=0, tiled=True),
        lax.psum_scatter(grad_down, "fsdp", scatter_dimension=0, tiled=True),
        lax.psum_scatter(
            jnp.stack([grad_gain_one, grad_offset_one, grad_gain_two, grad_offset_two]),
            "fsdp",
            scatter_dimension=1,
            tiled=True,
        ),
    )
    total_in, total_qkv, total_out, total_up, total_down, norm_total = lax.psum(
        (every_part[0], every_part[1], every_part[2], every_part[3], every_part[4], every_part[5]),
        "sp",
    )
    norm_first = norm_total[0:2]
    norm_second = norm_total[2:4]
    return (
        block_out,
        grad_patch,
        total_in,
        norm_first[0],
        norm_first[1],
        total_qkv,
        total_out,
        norm_second[0],
        norm_second[1],
        total_up,
        total_down,
    )


LANES = 128
BLOCK = 256
BF = jnp.bfloat16
F32 = jnp.float32


def halves(values):
    high = values.astype(BF).astype(F32)
    return high, values - high


def roll_half(values):
    return pltpu.roll(values, LANES // 2, 1)


def low_lanes(rows):
    return lax.broadcasted_iota(jnp.int32, (rows, LANES), 1) < LANES // 2


def pair_tiles(values):
    high, low = halves(values)
    first = low_lanes(values.shape[0])
    return (
        jnp.where(first, high, roll_half(low)).astype(BF),
        jnp.where(first, roll_half(high), low).astype(BF),
    )


def spread_tiles(values):
    high, low = halves(values)
    first = low_lanes(values.shape[0])
    high_r, low_r = roll_half(high), roll_half(low)
    return (
        jnp.concatenate([jnp.where(first, high, high_r), jnp.where(first, low, low_r)], axis=1).astype(BF),
        jnp.concatenate([jnp.where(first, high_r, high), jnp.where(first, low_r, low)], axis=1).astype(BF),
    )


def nt(left, right):
    return lax.dot_general(left, right, (((1,), (1,)), ((), ())), preferred_element_type=F32)


def nn(left, right):
    return lax.dot_general(left, right, (((1,), (0,)), ((), ())), preferred_element_type=F32)


def tn(left, right):
    return lax.dot_general(left, right, (((0,), (0,)), ((), ())), preferred_element_type=F32)


def split_bf(values):
    high = values.astype(BF)
    return high, (values - high.astype(F32)).astype(BF)


def forward_kernel(pos_ref, seg_ref, *refs):
    (q_own, k_own, v_own, q_in, k_in, v_in, seg_col, seg_row,
     o_own, o_out, lse_ref, tq, hk, tv, out_s) = refs
    rows = q_own.shape[0]
    own = pl.multiple_of(pos_ref[0] * rows, rows)
    other = pl.multiple_of((1 - pos_ref[0]) * rows, rows)
    for place, q, k, v in ((own, q_own, k_own, v_own), (other, q_in, k_in, v_in)):
        span = pl.ds(place, rows)
        for head, tile in enumerate(pair_tiles(q[...] * 0.125)):
            tq[head, span, :] = jnp.concatenate([tile, tile], axis=1)
        for head, tile in enumerate(spread_tiles(k[...])):
            hk[head, span, :] = tile
        for head, tile in enumerate(pair_tiles(v[...])):
            tv[head, span, :] = tile
    blocks = 2 * rows // BLOCK
    first = low_lanes(BLOCK)

    def query_block(i, carry):
        q_span = pl.ds(pl.multiple_of(i * BLOCK, BLOCK), BLOCK)
        first_label = seg_ref[i * BLOCK]
        start = jnp.int32(0)
        for j in range(blocks):
            start = start + jnp.where((j < i) & (seg_ref[j * BLOCK + BLOCK - 1] < first_label), 1, 0)
        label = seg_col[q_span, :1]
        q_place = i * BLOCK + lax.broadcasted_iota(jnp.int32, (BLOCK, BLOCK), 0)

        def key_block(step, state):
            j = i - step
            k_span = pl.ds(pl.multiple_of(j * BLOCK, BLOCK), BLOCK)
            k_place = j * BLOCK + lax.broadcasted_iota(jnp.int32, (BLOCK, BLOCK), 1)
            allowed = (label == seg_row[j]) & (k_place <= q_place)
            new_state = []
            for head in range(2):
                top, total, acc = state[head]
                scores = nt(tq[head, q_span, :], hk[head, k_span, :])
                scores = jnp.where(allowed, scores, -1e30)
                new_top = jnp.maximum(top, jnp.max(scores, axis=1, keepdims=True))
                weight = jnp.exp(scores - new_top)
                keep = jnp.exp(top - new_top)
                high, low = split_bf(weight)
                values = tv[head, k_span, :]
                new_state.append((
                    new_top,
                    total * keep + jnp.sum(weight, axis=1, keepdims=True),
                    acc * keep + nn(high, values) + nn(low, values),
                ))
            return tuple(new_state)

        init = (
            jnp.full((BLOCK, 1), -1e30, F32),
            jnp.zeros((BLOCK, 1), F32),
            jnp.zeros((BLOCK, LANES), F32),
        )
        state = lax.fori_loop(0, i - start + 1, key_block, (init, init))
        outs, logs = [], []
        for top, total, acc in state:
            outs.append((acc + roll_half(acc)) / total)
            logs.append(jnp.broadcast_to(top + jnp.log(total), (BLOCK, LANES)))
        out_s[q_span, :] = jnp.where(first, outs[0], outs[1])
        lse_ref[q_span, :] = jnp.where(first, logs[0], logs[1])
        return carry

    lax.fori_loop(0, blocks, query_block, 0)
    o_own[...] = out_s[pl.ds(own, rows), :]
    o_out[...] = out_s[pl.ds(other, rows), :]


def attend_forward(own, received, position, labels):
    rows, columns = own.shape
    width = columns // 3
    pairs = width // LANES
    length = 2 * rows

    def part(which):
        return pl.BlockSpec((rows, LANES), lambda g, *_: (0, which * pairs + g))

    whole = pl.BlockSpec((rows, LANES), lambda g, *_: (0, g))
    return pl.pallas_call(
        forward_kernel,
        grid_spec=pltpu.PrefetchScalarGridSpec(
            num_scalar_prefetch=2,
            grid=(pairs,),
            in_specs=[part(0), part(1), part(2), part(0), part(1), part(2),
                      pl.BlockSpec((length, LANES), lambda g, *_: (0, 0)),
                      pl.BlockSpec((length // BLOCK, 1, BLOCK), lambda g, *_: (0, 0, 0))],
            out_specs=[whole, whole, pl.BlockSpec((length, LANES), lambda g, *_: (0, g))],
            scratch_shapes=[
                pltpu.VMEM((2, length, 2 * LANES), BF),
                pltpu.VMEM((2, length, 2 * LANES), BF),
                pltpu.VMEM((2, length, LANES), BF),
                pltpu.VMEM((length, LANES), F32),
            ],
        ),
        out_shape=[
            jax.ShapeDtypeStruct((rows, width), F32),
            jax.ShapeDtypeStruct((rows, width), F32),
            jax.ShapeDtypeStruct((length, width), F32),
        ],
        cost_estimate=pl.CostEstimate(flops=20 * 10**9, bytes_accessed=8 * rows * columns * 3, transcendentals=length * width * 8),
        compiler_params=pltpu.CompilerParams(vmem_limit_bytes=48 * 1024 * 1024),
        name="attend_forward",
    )(position, labels, own, own, own, received, received, received,
      jnp.broadcast_to(labels[:, None], (length, LANES)), labels.reshape(length // BLOCK, 1, BLOCK))


def backward_kernel(pos_ref, seg_ref, *refs):
    (q_own, k_own, v_own, q_in, k_in, v_in, o_own, o_in, g_own, g_in, lse_ref, seg_col, seg_row,
     gq_own, gk_own, gv_own, gq_out, gk_out, gv_out,
     tq, hk, tk, hv, tg, lse_t, delta_t, gq_s, gk_s, gv_s) = refs
    rows = q_own.shape[0]
    length = 2 * rows
    own = pl.multiple_of(pos_ref[0] * rows, rows)
    other = pl.multiple_of((1 - pos_ref[0]) * rows, rows)
    half = LANES // 2
    for place, q, k, v, o, g in ((own, q_own, k_own, v_own, o_own, g_own), (other, q_in, k_in, v_in, o_in, g_in)):
        span = pl.ds(place, rows)
        for head, tile in enumerate(pair_tiles(q[...] * 0.125)):
            tq[head, span, :] = jnp.concatenate([tile, tile], axis=1)
        for head, tile in enumerate(pair_tiles(g[...])):
            tg[head, span, :] = jnp.concatenate([tile, tile], axis=1)
        for head, tile in enumerate(spread_tiles(k[...])):
            hk[head, span, :] = tile
        for head, tile in enumerate(spread_tiles(v[...])):
            hv[head, span, :] = tile
        for head, tile in enumerate(pair_tiles(k[...])):
            tk[head, span, :] = tile
        turned = jnp.transpose(o[...] * g[...])
        for head in range(2):
            delta_t[head, 0:1, span] = jnp.sum(turned[head * half:(head + 1) * half], axis=0, keepdims=True)
    turned = jnp.transpose(lse_ref[...])
    for head in range(2):
        lse_t[head, 0:1, :] = turned[head * half:head * half + 1]
    blocks = length // BLOCK
    first = low_lanes(BLOCK)
    gq_s[...] = jnp.zeros_like(gq_s)

    def key_block(j, carry):
        k_span = pl.ds(pl.multiple_of(j * BLOCK, BLOCK), BLOCK)
        last_label = seg_ref[j * BLOCK + BLOCK - 1]
        count = jnp.int32(1)
        for i in range(blocks):
            count = count + jnp.where((i > j) & (seg_ref[i * BLOCK] <= last_label), 1, 0)
        label = seg_col[k_span, :1]
        k_place = j * BLOCK + lax.broadcasted_iota(jnp.int32, (BLOCK, BLOCK), 0)

        def query_block(step, state):
            i = j + step
            q_span = pl.ds(pl.multiple_of(i * BLOCK, BLOCK), BLOCK)
            q_place = i * BLOCK + lax.broadcasted_iota(jnp.int32, (BLOCK, BLOCK), 1)
            allowed = (label == seg_row[i]) & (k_place <= q_place)
            new_state = []
            for head in range(2):
                grad_k, grad_v = state[head]
                query = tq[head, q_span, :]
                grad = tg[head, q_span, :]
                scores = nt(hk[head, k_span, :], query)
                weight = jnp.exp(jnp.where(allowed, scores - lse_t[head, 0:1, q_span], -1e30))
                grad_weight = nt(hv[head, k_span, :], grad)
                grad_score = weight * (grad_weight - delta_t[head, 0:1, q_span])
                w_high, w_low = split_bf(weight)
                s_high, s_low = split_bf(grad_score)
                grad_v = grad_v + nn(w_high, grad[:, :LANES]) + nn(w_low, grad[:, :LANES])
                grad_k = grad_k + nn(s_high, query[:, :LANES]) + nn(s_low, query[:, :LANES])
                keys = tk[head, k_span, :]
                gq_s[head, q_span, :] += tn(s_high, keys) + tn(s_low, keys)
                new_state.append((grad_k, grad_v))
            return tuple(new_state)

        zero = jnp.zeros((BLOCK, LANES), F32)
        state = lax.fori_loop(0, count, query_block, ((zero, zero), (zero, zero)))
        for slot, store in ((0, gk_s), (1, gv_s)):
            left, right = state[0][slot], state[1][slot]
            store[k_span, :] = jnp.where(first, left + roll_half(left), right + roll_half(right))
        return carry

    lax.fori_loop(0, blocks, key_block, 0)
    wide = low_lanes(rows)
    for place, gq, gk, gv in ((own, gq_own, gk_own, gv_own), (other, gq_out, gk_out, gv_out)):
        span = pl.ds(place, rows)
        left, right = gq_s[0, span, :], gq_s[1, span, :]
        gq[...] = jnp.where(wide, left + roll_half(left), right + roll_half(right)) * 0.125
        gk[...] = gk_s[span, :]
        gv[...] = gv_s[span, :]


def attend_backward(own, received, out_own, out_in, grad_own, grad_in, logs, position, labels):
    rows, columns = own.shape
    width = columns // 3
    pairs = width // LANES
    length = 2 * rows

    def part(which):
        return pl.BlockSpec((rows, LANES), lambda g, *_: (0, which * pairs + g))

    whole = pl.BlockSpec((rows, LANES), lambda g, *_: (0, g))
    outs = pl.pallas_call(
        backward_kernel,
        grid_spec=pltpu.PrefetchScalarGridSpec(
            num_scalar_prefetch=2,
            grid=(pairs,),
            in_specs=[part(0), part(1), part(2), part(0), part(1), part(2), whole, whole, whole, whole,
                      pl.BlockSpec((length, LANES), lambda g, *_: (0, g)),
                      pl.BlockSpec((length, LANES), lambda g, *_: (0, 0)),
                      pl.BlockSpec((length // BLOCK, 1, BLOCK), lambda g, *_: (0, 0, 0))],
            out_specs=[whole] * 6,
            scratch_shapes=[
                pltpu.VMEM((2, length, 2 * LANES), BF),
                pltpu.VMEM((2, length, 2 * LANES), BF),
                pltpu.VMEM((2, length, LANES), BF),
                pltpu.VMEM((2, length, 2 * LANES), BF),
                pltpu.VMEM((2, length, 2 * LANES), BF),
                pltpu.VMEM((2, 8, length), F32),
                pltpu.VMEM((2, 8, length), F32),
                pltpu.VMEM((2, length, LANES), F32),
                pltpu.VMEM((length, LANES), F32),
                pltpu.VMEM((length, LANES), F32),
            ],
        ),
        out_shape=[jax.ShapeDtypeStruct((rows, width), F32)] * 6,
        cost_estimate=pl.CostEstimate(flops=40 * 10**9, bytes_accessed=8 * rows * columns * 5, transcendentals=length * width * 8),
        compiler_params=pltpu.CompilerParams(vmem_limit_bytes=56 * 1024 * 1024),
        name="attend_backward",
    )(position, labels, own, own, own, received, received, received, out_own, out_in, grad_own, grad_in, logs,
      jnp.broadcast_to(labels[:, None], (length, LANES)), labels.reshape(length // BLOCK, 1, BLOCK))
    return outs


MESH = pl.DeviceIdType.MESH
PIECE = 48


def scatter_kernel(plan, *refs):
    count = len(plan)
    units = sum(plan)
    pairs = units // 2
    turned, grads = refs[:count], refs[count:2 * count]
    stream_ref, weight_ref, norms_ref, extra_ref = refs[2 * count:2 * count + 4]
    total_ref, patch_ref, norm_total_ref, extra_total_ref = refs[2 * count + 4:2 * count + 8]
    (t_buf, g_buf, g_high, g_low, part, s_high, s_low, w_buf, p_buf, land_a, n_x, n_z, n_y, y_y, y_x, y_z, done,
     v_c, v_x, v_y, v_z, extra_in,
     load_sem, w_sem, p_sem, a_sem, nx_sem, nz_sem, ny_sem, yy_sem, yx_sem, yz_sem, ye_sem, v_sem, o_sem) = refs[2 * count + 8:]
    fsdp = lax.axis_index("fsdp")
    row = lax.axis_index("sp")
    z, x, core = fsdp // 4, (fsdp // 2) % 2, fsdp % 2
    half = PIECE // 2

    def device(z_at, x_at, core_at, row_at):
        return ((z_at * 2 + x_at) * 2 + core_at, row_at)

    sibling = device(z, x, 1 - core, row)
    beside = device(z, 1 - x, core, row)
    across = device(z, x, core, 1 - row)
    along = [device((z + step) % 4, x, core, row) for step in (1, 2, 3)]

    barrier = pltpu.get_barrier_semaphore()
    for peer in [sibling, beside, across] + along:
        pl.semaphore_signal(barrier, inc=1, device_id=peer, device_id_type=MESH)

    def remote(source, target, sems, index, peer):
        return pltpu.make_async_remote_copy(
            src_ref=source, dst_ref=target, send_sem=sems.at[(0,) + index], recv_sem=sems.at[(1,) + index],
            device_id=peer, device_id_type=MESH,
        )

    def loads(unit, slot, act):
        base = 0
        for which in range(count):
            first, last = base, base + plan[which]
            base = last

            @pl.when((unit >= first) & (unit < last))
            def _(which=which, first=first):
                j = unit - first
                for side in range(2):
                    rows_ref = turned[which]
                    source = rows_ref.at[:, side, j] if rows_ref.shape[2] > 1 else rows_ref.at[:, side, 0]
                    act(pltpu.make_async_copy(source, t_buf.at[slot, side], load_sem.at[slot, side]))
                grad = grads[which]
                width = g_buf.shape[2]
                if grad.shape[1] > width:
                    grad = grad.at[:, pl.ds(pl.multiple_of(j * width, width), width)]
                act(pltpu.make_async_copy(grad, g_buf.at[slot], load_sem.at[slot, 2]))

    def start(copy):
        copy.start()

    def wait(copy):
        copy.wait()

    def weight_copy(block, slot):
        return pltpu.make_async_copy(weight_ref.at[block], w_buf.at[slot], w_sem.at[slot])

    def patch_copy(block, slot):
        columns = w_buf.shape[1]
        return pltpu.make_async_copy(
            p_buf.at[slot], patch_ref.at[:, pl.ds(pl.multiple_of(block * columns, columns), columns)], p_sem.at[slot]
        )

    def core_copy(unit, slot):
        return remote(part.at[slot, 1 - core], land_a.at[unit], a_sem, (unit,), sibling)

    def nx_copy(p):
        return remote(land_a.at[2 * p, :, 1 - x], n_x.at[p], nx_sem, (p,), beside)

    def nz_copy(p, step):
        return remote(n_x.at[p, (z + step + 1) % 4], n_z.at[p, step], nz_sem, (p, step), along[step])

    def ny_copy(p):
        return remote(n_x.at[p, z], n_y.at[p], ny_sem, (p,), across)

    def yy_copy(p):
        return remote(
            land_a.at[2 * p + 1, :, :, pl.ds(pl.multiple_of((1 - row) * half, half), half)], y_y.at[p], yy_sem, (p,), across
        )

    def yx_copy(p):
        return remote(y_y.at[p, :, 1 - x], y_x.at[p], yx_sem, (p,), beside)

    def yz_copy(p, step):
        return remote(y_x.at[p, (z + step + 1) % 4], y_z.at[p, step], yz_sem, (p, step), along[step])

    def ye_copy(p):
        place = pl.ds(pl.multiple_of(row * half, half), half)
        return remote(y_x.at[p, z], done.at[2 * p + 1, place], ye_sem, (p,), across)

    loads(0, 0, start)
    weight_copy(0, 0).start()
    s_high[...] = stream_ref[...].astype(BF)
    s_low[...] = (stream_ref[...] - s_high[...].astype(F32)).astype(BF)
    pl.semaphore_wait(barrier, 6)

    v_copies = [
        remote(norms_ref, v_c, v_sem, (0,), sibling),
        remote(v_c, v_x, v_sem, (1,), beside),
        remote(v_x, v_y, v_sem, (2,), across),
    ] + [remote(v_y, v_z.at[step], v_sem, (3 + step,), along[step]) for step in range(3)]
    v_copies[0].start()
    extra_copy = remote(extra_ref, extra_in, v_sem, (6,), across)
    extra_copy.start()

    def compute(unit, slot):
        loads(unit, slot, wait)

        @pl.when(unit + 1 < units)
        def _():
            loads(unit + 1, 1 - slot, start)

        @pl.when(unit >= 2)
        def _():
            core_copy(unit - 2, slot).wait_send()

        grad = g_buf[slot]
        g_high[...] = grad.astype(BF)
        g_low[...] = (grad - g_high[...].astype(F32)).astype(BF)

        def side_of(turn, carry):
            side = jnp.where(turn == 0, 1 - core, core)
            high, low = split_bf(t_buf[slot, side].reshape(8 * PIECE, t_buf.shape[4]))
            product = nn(high, g_high[...]) + nn(high, g_low[...]) + nn(low, g_high[...])
            part[slot, side] = product.reshape(4, 2, PIECE, product.shape[1])

            @pl.when(turn == 0)
            def _():
                core_copy(unit, slot).start()

            return carry

        lax.fori_loop(0, 2, side_of, 0)

    def patch_block(block, slot):
        weight_copy(block, slot).wait()

        @pl.when(block + 1 < weight_ref.shape[0])
        def _():
            weight_copy(block + 1, 1 - slot).start()

        @pl.when(block >= 2)
        def _():
            patch_copy(block - 2, slot).wait()

        high, low = split_bf(w_buf[slot])
        p_buf[slot] = nt(s_high[...], high) + nt(s_high[...], low) + nt(s_low[...], high)
        patch_copy(block, slot).start()

    def loop(number, body):
        def step(i, carry):
            body(i)
            return carry

        lax.fori_loop(0, number, step, 0)

    def after_core(unit, slot):
        core_copy(unit, slot).wait_recv()

        def add(i):
            for b in range(2):
                land_a[unit, i, b] = land_a[unit, i, b] + part[slot, core, i, b]

        loop(4, add)

    def iteration(p, carry):
        @pl.when(p < pairs)
        def _():
            compute(2 * p, 0)
            compute(2 * p + 1, 1)
            after_core(2 * p, 0)
            nx_copy(p).start()
            after_core(2 * p + 1, 1)
            yy_copy(p).start()

        q = p - 1

        @pl.when((q >= 0) & (q < pairs))
        def _():
            nx_copy(q).wait_recv()

            def add_n(i):
                n_x[q, i] = n_x[q, i] + land_a[2 * q, i, x]

            loop(4, add_n)
            for step in range(3):
                nz_copy(q, step).start()
            yy_copy(q).wait_recv()
            own = pl.ds(pl.multiple_of(row * half, half), half)

            def add_y(i):
                for b in range(2):
                    y_y[q, i, b] = y_y[q, i, b] + land_a[2 * q + 1, i, b, own]

            loop(4, add_y)
            yx_copy(q).start()

        @pl.when(p < pairs)
        def _():
            patch_block(2 * p, 0)
            patch_block(2 * p + 1, 1)

        r = p - 2

        @pl.when((r >= 0) & (r < pairs))
        def _():
            for step in range(3):
                nz_copy(r, step).wait_recv()
            n_x[r, z] = n_x[r, z] + n_z[r, 0] + n_z[r, 1] + n_z[r, 2]
            ny_copy(r).start()
            yx_copy(r).wait_recv()

            def add_x(i):
                y_x[r, i] = y_x[r, i] + y_y[r, i, x]

            loop(4, add_x)
            for step in range(3):
                yz_copy(r, step).start()

        s = p - 3

        @pl.when((s >= 0) & (s < pairs))
        def _():
            ny_copy(s).wait_recv()
            done[2 * s] = n_x[s, z] + n_y[s]
            for step in range(3):
                yz_copy(s, step).wait_recv()
            total = y_x[s, z] + y_z[s, 0] + y_z[s, 1] + y_z[s, 2]
            y_x[s, z] = total
            done[2 * s + 1, pl.ds(pl.multiple_of(row * half, half), half)] = total
            ye_copy(s).start()

        @pl.when(p == 0)
        def _():
            v_copies[0].wait_recv()
            v_c[...] = v_c[...] + norms_ref[...]
            v_copies[1].start()

        @pl.when(p == 1)
        def _():
            v_copies[1].wait_recv()
            v_x[...] = v_x[...] + v_c[...]
            v_copies[2].start()

        @pl.when(p == 2)
        def _():
            v_copies[2].wait_recv()
            v_y[...] = v_y[...] + v_x[...]
            for step in range(3):
                v_copies[3 + step].start()

        @pl.when(p == 3)
        def _():
            for step in range(3):
                v_copies[3 + step].wait_recv()
            norm_total_ref[...] = v_y[...] + v_z[0] + v_z[1] + v_z[2]
            extra_copy.wait_recv()
            extra_total_ref[...] = extra_ref[...] + extra_in[...]

        return carry

    lax.fori_loop(0, pairs + 3, iteration, 0)

    def finish(p):
        ye_copy(p).wait()
        nx_copy(p).wait_send()
        ny_copy(p).wait_send()
        yy_copy(p).wait_send()
        yx_copy(p).wait_send()
        for step in range(3):
            nz_copy(p, step).wait_send()
            yz_copy(p, step).wait_send()

    loop(pairs, finish)
    out = pltpu.make_async_copy(done, total_ref, o_sem)
    out.start()
    for copy in v_copies + [extra_copy]:
        copy.wait_send()
    core_copy(units - 2, 0).wait_send()
    core_copy(units - 1, 1).wait_send()
    blocks = weight_ref.shape[0]
    patch_copy(blocks - 2, 0).wait()
    patch_copy(blocks - 1, 1).wait()
    out.wait()


def reduce_gradients(turned, grads, grad_stream, weight, norms, extra):
    rows, width = grad_stream.shape
    plan, views = [], []
    for left, right in zip(turned, grads):
        tall = left.shape[0] // (16 * PIECE)
        plan.append(tall * (right.shape[1] // width))
        views.append(left.reshape(8, 2, tall, PIECE, rows))
    units = sum(plan)
    pairs = units // 2
    owners = 16
    block = weight.shape[0] // owners
    half = PIECE // 2
    dma = pltpu.SemaphoreType.DMA
    any_space = pl.BlockSpec(memory_space=pl.ANY)
    vmem = pl.BlockSpec(memory_space=pltpu.VMEM)
    flops = 6 * rows * width * (units * 16 * PIECE + weight.shape[0])
    return pl.pallas_call(
        functools.partial(scatter_kernel, tuple(plan)),
        out_shape=[
            jax.ShapeDtypeStruct((units, PIECE, width), F32),
            jax.ShapeDtypeStruct((rows, weight.shape[0]), F32),
            jax.ShapeDtypeStruct(norms.shape, F32),
            jax.ShapeDtypeStruct(extra.shape, F32),
        ],
        in_specs=[any_space] * (2 * len(plan)) + [vmem, any_space, vmem, vmem],
        out_specs=[any_space, any_space, vmem, vmem],
        scratch_shapes=[
            pltpu.VMEM((2, 2, 8, PIECE, rows), F32),
            pltpu.VMEM((2, rows, width), F32),
            pltpu.VMEM((rows, width), BF),
            pltpu.VMEM((rows, width), BF),
            pltpu.VMEM((2, 2, 4, 2, PIECE, width), F32),
            pltpu.VMEM((rows, width), BF),
            pltpu.VMEM((rows, width), BF),
            pltpu.VMEM((2, block, width), F32),
            pltpu.VMEM((2, rows, block), F32),
            pltpu.VMEM((units, 4, 2, PIECE, width), F32),
            pltpu.VMEM((pairs, 4, PIECE, width), F32),
            pltpu.VMEM((pairs, 3, PIECE, width), F32),
            pltpu.VMEM((pairs, PIECE, width), F32),
            pltpu.VMEM((pairs, 4, 2, half, width), F32),
            pltpu.VMEM((pairs, 4, half, width), F32),
            pltpu.VMEM((pairs, 3, half, width), F32),
            pltpu.VMEM((units, PIECE, width), F32),
            pltpu.VMEM(norms.shape, F32),
            pltpu.VMEM(norms.shape, F32),
            pltpu.VMEM(norms.shape, F32),
            pltpu.VMEM((3,) + norms.shape, F32),
            pltpu.VMEM(extra.shape, F32),
            dma((2, 3)), dma((2,)), dma((2,)),
            dma((2, units)), dma((2, pairs)), dma((2, pairs, 3)), dma((2, pairs)),
            dma((2, pairs)), dma((2, pairs)), dma((2, pairs, 3)), dma((2, pairs)),
            dma((2, 7)), dma,
        ],
        cost_estimate=pl.CostEstimate(flops=flops, bytes_accessed=120 * 10**6, transcendentals=0),
        compiler_params=pltpu.CompilerParams(
            collective_id=0, has_side_effects=True, vmem_limit_bytes=67043328
        ),
        name="reduce_gradients",
    )(*views, *grads, grad_stream, weight.reshape(owners, block, width), norms, extra)


def fast_shards(
    patches, segments, w_in, norm1_gain, norm1_bias, w_qkv, w_out, norm2_gain, norm2_bias, w_up, w_down, cotangent
):
    _, rows, patch_width = patches.shape
    width = w_out.shape[1]
    position = lax.axis_index("sp")
    places = position[None].astype(jnp.int32)
    labels = segments[0]
    norm_params = jnp.stack([norm1_gain, norm1_bias, norm2_gain, norm2_bias])
    in_full = lax.all_gather(w_in, "fsdp", axis=0, tiled=True)
    norm_full = lax.all_gather(norm_params, "fsdp", axis=1, tiled=True)
    qkv_full = lax.all_gather(w_qkv, "fsdp", axis=0, tiled=True)
    out_full = lax.all_gather(w_out, "fsdp", axis=0, tiled=True)
    up_full = lax.all_gather(w_up, "fsdp", axis=0, tiled=True)
    down_full = lax.all_gather(w_down, "fsdp", axis=0, tiled=True)
    patch_rows = patches[0]
    stream = matmul(patch_rows, in_full)
    normed, norm1_pull = jax.vjp(layer_norm, stream, norm_full[0], norm_full[1])
    half = width // 2
    by_half = qkv_full.reshape(width, 3, 2, half)
    swap = [(0, 1), (1, 0)]

    def columns_of(which):
        return lax.dynamic_index_in_dim(by_half, which, 2, keepdims=False).reshape(width, 3 * half)

    own_columns = columns_of(position)
    sent_columns = columns_of(1 - position)
    received = lax.ppermute(matmul(normed, sent_columns), "sp", swap)
    own = matmul(normed, own_columns)
    out_own, out_sent, logs = attend_forward(own, received, places, labels)
    out_in = lax.ppermute(out_sent, "sp", swap)

    def whole_rows(mine, theirs):
        return jnp.where(position == 0, jnp.concatenate([mine, theirs], 1), jnp.concatenate([theirs, mine], 1))

    attended_rows = whole_rows(out_own, out_in)
    residual = stream + matmul(attended_rows, out_full)
    normed_two, norm2_pull = jax.vjp(layer_norm, residual, norm_full[2], norm_full[3])
    hidden_pre = matmul(normed_two, up_full)
    hidden, gelu_pull = jax.vjp(gelu_tanh, hidden_pre)
    block_out = residual + matmul(hidden, down_full)
    grad_rows = cotangent[0]
    grad_down = matmul_tn(hidden, grad_rows)
    down_part = lax.psum_scatter(grad_down, "fsdp", scatter_dimension=0, tiled=True)
    later_rows, _ = lax.optimization_barrier((grad_rows, grad_down))
    (grad_pre,) = gelu_pull(matmul_nt(later_rows, down_full))
    grad_resid_norm, grad_gain_two, grad_offset_two = norm2_pull(matmul_nt(grad_pre, up_full))
    grad_resid = grad_rows + grad_resid_norm
    out_by_half = out_full.reshape(2, half, width)
    grad_sent = matmul_nt(grad_resid, lax.dynamic_index_in_dim(out_by_half, 1 - position, 0, keepdims=False))
    grad_in = lax.ppermute(grad_sent, "sp", swap)
    grad_own = matmul_nt(grad_resid, lax.dynamic_index_in_dim(out_by_half, position, 0, keepdims=False))
    parts = attend_backward(own, received, out_own, out_sent, grad_own, grad_in, logs, places, labels)
    mine = jnp.concatenate(parts[:3], axis=1)
    theirs = lax.ppermute(jnp.concatenate(parts[3:], axis=1), "sp", swap)
    grad_normed = matmul_nt(mine, own_columns) + matmul_nt(theirs, sent_columns)
    low = jnp.where(position == 0, mine, theirs).reshape(rows, 3, 1, half)
    high = jnp.where(position == 0, theirs, mine).reshape(rows, 3, 1, half)
    grad_proj = jnp.concatenate([low, high], axis=2).reshape(rows, 3 * width)
    grad_stream_norm, grad_gain_one, grad_offset_one = norm1_pull(grad_normed)
    grad_stream = grad_resid + grad_stream_norm
    vectors = jnp.stack([grad_gain_one, grad_offset_one, grad_gain_two, grad_offset_two] + [jnp.zeros_like(grad_gain_one)] * 4)
    pieces, grad_patch, vector_sums, total_down = reduce_gradients(
        [normed_two.T, attended_rows.T, normed.T, patch_rows.T],
        [grad_pre, grad_resid, grad_proj, grad_stream],
        grad_stream, in_full, vectors, down_part,
    )
    own_part = w_out.shape[0]
    vector_sums = lax.dynamic_slice(vector_sums, (0, lax.axis_index("fsdp") * own_part), (4, own_part))

    def across(first, last):
        return jnp.concatenate([pieces[i] for i in range(first, last)], axis=1)

    return (
        block_out[None], grad_patch[None], pieces[8:16].reshape(8 * PIECE, width), vector_sums[0], vector_sums[1],
        across(5, 8), pieces[4], vector_sums[2], vector_sums[3], across(0, 4), total_down,
    )


def solution(mesh):
    sharded = P("fsdp", "sp", None)
    matrix = P("fsdp", None)
    vector = P("fsdp")
    fast = mesh.shape["fsdp"] == 16 and mesh.shape["sp"] == 2
    return jax.shard_map(
        fast_shards if fast else shards,
        mesh=mesh,
        in_specs=(sharded, matrix, matrix, vector, vector, matrix, matrix, vector, vector, matrix, matrix, sharded),
        out_specs=(sharded, sharded, matrix, vector, vector, matrix, matrix, vector, vector, matrix, matrix),
        check_vma=False,
    )
```

```python
import functools

import jax
import jax.numpy as jnp
from jax import lax
from jax.experimental import pallas as pl
from jax.experimental.pallas import tpu as pltpu
from jax.sharding import PartitionSpec as P

HEADS = 12


EPSILON = 1e-05


def matmul(left_side, right_side):
    return jnp.dot(
        left_side, right_side, precision=lax.Precision.HIGH, preferred_element_type=jnp.float32
    )


def matmul_tn(left_side, right_side):
    return lax.dot_general(
        left_side,
        right_side,
        (((0,), (0,)), ((), ())),
        precision=lax.Precision.HIGH,
        preferred_element_type=jnp.float32,
    )


def matmul_nt(left_side, right_side):
    return lax.dot_general(
        left_side,
        right_side,
        (((1,), (1,)), ((), ())),
        precision=lax.Precision.HIGH,
        preferred_element_type=jnp.float32,
    )


def layer_norm(values, scaling, offset):
    average = jnp.mean(values, axis=-1, keepdims=True)
    centred = values - average
    spread = jnp.mean(centred * centred, axis=-1, keepdims=True)
    return centred * lax.rsqrt(spread + EPSILON) * scaling + offset


def gelu_tanh(values):
    return jax.nn.gelu(values, approximate=True)


def scored(queries, key_rows, labels):
    length = labels.shape[0]
    factor = queries.shape[-1] ** (-0.5)
    raw_scores = matmul_nt(queries, key_rows) * factor
    places = jnp.arange(length, dtype=jnp.int32)
    allowed = (labels[:, None] == labels[None, :]) & (places[None, :] <= places[:, None])
    return (raw_scores, allowed, factor)


def attend_one(packed):
    queries, key_rows, value_rows, labels = packed
    raw_scores, allowed, factor = scored(queries, key_rows, labels)
    masked = jnp.where(allowed, raw_scores, -1e30)
    row_max = jnp.max(masked, axis=1, keepdims=True)
    exponent = jnp.exp(masked - row_max)
    summed = jnp.sum(exponent, axis=1, keepdims=True)
    attended = matmul(exponent / summed, value_rows)
    return (attended, (row_max + jnp.log(summed))[:, 0])


def attend_back(packed):
    queries, key_rows, value_rows, attended, log_total, grad_attended, labels = packed
    raw_scores, allowed, factor = scored(queries, key_rows, labels)
    weights = jnp.where(
        allowed, jnp.exp(jnp.where(allowed, raw_scores - log_total[:, None], -1e30)), 0.0
    )
    grad_values = matmul_tn(weights, grad_attended)
    grad_weights = matmul_nt(grad_attended, value_rows)
    row_dot = jnp.sum(grad_attended * attended, axis=1, keepdims=True)
    grad_scores = weights * (grad_weights - row_dot) * factor
    grad_queries = matmul(grad_scores, key_rows)
    grad_keys = matmul_tn(grad_scores, queries)
    return (grad_queries, grad_keys, grad_values)


def to_batch(blocked, heads_local):
    seq_count, length, columns = blocked.shape
    head_dim = columns // heads_local
    return (
        blocked.reshape(seq_count, length, heads_local, head_dim)
        .transpose(0, 2, 1, 3)
        .reshape(seq_count * heads_local, length, head_dim)
    )


def from_batch(blocked, seq_count):
    batch_size, length, head_dim = blocked.shape
    heads_local = batch_size // seq_count
    return (
        blocked.reshape(seq_count, heads_local, length, head_dim)
        .transpose(0, 2, 1, 3)
        .reshape(seq_count, length, heads_local * head_dim)
    )


def shards(
    patches,
    segments,
    w_in,
    norm1_gain,
    norm1_bias,
    w_qkv,
    w_out,
    norm2_gain,
    norm2_bias,
    w_up,
    w_down,
    cotangent,
):
    seq_count, local_len, patch_width = patches.shape
    model_width = w_out.shape[1]
    heads_local = HEADS // lax.axis_size("sp")
    row_count = seq_count * local_len
    norm_params = jnp.stack([norm1_gain, norm1_bias, norm2_gain, norm2_bias])
    gathered = (
        lax.all_gather(w_in, "fsdp", axis=0, tiled=True),
        lax.all_gather(w_qkv, "fsdp", axis=0, tiled=True),
        lax.all_gather(w_out, "fsdp", axis=0, tiled=True),
        lax.all_gather(w_up, "fsdp", axis=0, tiled=True),
        lax.all_gather(w_down, "fsdp", axis=0, tiled=True),
        lax.all_gather(norm_params, "fsdp", axis=1, tiled=True),
    )
    in_full, qkv_full, out_full, up_full, down_full, norm_full = gathered
    patch_rows = patches.reshape(row_count, patch_width)
    stream = matmul(patch_rows, in_full)
    normed, norm1_pull = jax.vjp(layer_norm, stream, norm_full[0], norm_full[1])
    projected = matmul(normed, qkv_full)
    query_tok = projected[:, :model_width].reshape(seq_count, local_len, model_width)
    key_tok = projected[:, model_width : 2 * model_width].reshape(seq_count, local_len, model_width)
    value_tok = projected[:, 2 * model_width :].reshape(seq_count, local_len, model_width)
    query_seq, key_seq, value_seq = (
        lax.all_to_all(query_tok, "sp", split_axis=2, concat_axis=1, tiled=True),
        lax.all_to_all(key_tok, "sp", split_axis=2, concat_axis=1, tiled=True),
        lax.all_to_all(value_tok, "sp", split_axis=2, concat_axis=1, tiled=True),
    )
    labels = jnp.repeat(segments, heads_local, axis=0)
    query_batch = to_batch(query_seq, heads_local)
    key_batch = to_batch(key_seq, heads_local)
    value_batch = to_batch(value_seq, heads_local)
    attended, log_total = lax.map(attend_one, (query_batch, key_batch, value_batch, labels))
    attended_tok = lax.all_to_all(
        from_batch(attended, seq_count), "sp", split_axis=1, concat_axis=2, tiled=True
    )
    attended_rows = attended_tok.reshape(row_count, model_width)
    residual = stream + matmul(attended_rows, out_full)
    normed_two, norm2_pull = jax.vjp(layer_norm, residual, norm_full[2], norm_full[3])
    hidden_pre = matmul(normed_two, up_full)
    hidden, gelu_pull = jax.vjp(gelu_tanh, hidden_pre)
    result = residual + matmul(hidden, down_full)
    block_out = result.reshape(seq_count, local_len, model_width)
    in_back, qkv_back, out_back, up_back, down_back = (
        lax.all_gather(w_in, "fsdp", axis=0, tiled=True),
        lax.all_gather(w_qkv, "fsdp", axis=0, tiled=True),
        lax.all_gather(w_out, "fsdp", axis=0, tiled=True),
        lax.all_gather(w_up, "fsdp", axis=0, tiled=True),
        lax.all_gather(w_down, "fsdp", axis=0, tiled=True),
    )
    grad_rows = cotangent.reshape(row_count, model_width)
    grad_down = matmul_tn(hidden, grad_rows)
    (grad_pre,) = gelu_pull(matmul_nt(grad_rows, down_back))
    grad_up = matmul_tn(normed_two, grad_pre)
    grad_resid_norm, grad_gain_two, grad_offset_two = norm2_pull(matmul_nt(grad_pre, up_back))
    grad_resid = grad_rows + grad_resid_norm
    grad_out = matmul_tn(attended_rows, grad_resid)
    grad_att = matmul_nt(grad_resid, out_back).reshape(seq_count, local_len, model_width)
    grad_att_seq = lax.all_to_all(grad_att, "sp", split_axis=2, concat_axis=1, tiled=True)
    grad_query, grad_key, grad_value = lax.map(
        attend_back,
        (
            query_batch,
            key_batch,
            value_batch,
            attended,
            log_total,
            to_batch(grad_att_seq, heads_local),
            labels,
        ),
    )
    back_query, back_key, back_value = (
        lax.all_to_all(
            from_batch(grad_query, seq_count), "sp", split_axis=1, concat_axis=2, tiled=True
        ),
        lax.all_to_all(
            from_batch(grad_key, seq_count), "sp", split_axis=1, concat_axis=2, tiled=True
        ),
        lax.all_to_all(
            from_batch(grad_value, seq_count), "sp", split_axis=1, concat_axis=2, tiled=True
        ),
    )
    grad_proj = jnp.concatenate([back_query, back_key, back_value], axis=2).reshape(
        row_count, 3 * model_width
    )
    grad_qkv = matmul_tn(normed, grad_proj)
    grad_stream_norm, grad_gain_one, grad_offset_one = norm1_pull(matmul_nt(grad_proj, qkv_back))
    grad_stream = grad_resid + grad_stream_norm
    grad_in = matmul_tn(patch_rows, grad_stream)
    grad_patch = matmul_nt(grad_stream, in_back).reshape(seq_count, local_len, patch_width)
    every_part = (
        lax.psum_scatter(grad_in, "fsdp", scatter_dimension=0, tiled=True),
        lax.psum_scatter(grad_qkv, "fsdp", scatter_dimension=0, tiled=True),
        lax.psum_scatter(grad_out, "fsdp", scatter_dimension=0, tiled=True),
        lax.psum_scatter(grad_up, "fsdp", scatter_dimension=0, tiled=True),
        lax.psum_scatter(grad_down, "fsdp", scatter_dimension=0, tiled=True),
        lax.psum_scatter(
            jnp.stack([grad_gain_one, grad_offset_one, grad_gain_two, grad_offset_two]),
            "fsdp",
            scatter_dimension=1,
            tiled=True,
        ),
    )
    total_in, total_qkv, total_out, total_up, total_down, norm_total = lax.psum(
        (every_part[0], every_part[1], every_part[2], every_part[3], every_part[4], every_part[5]),
        "sp",
    )
    norm_first = norm_total[0:2]
    norm_second = norm_total[2:4]
    return (
        block_out,
        grad_patch,
        total_in,
        norm_first[0],
        norm_first[1],
        total_qkv,
        total_out,
        norm_second[0],
        norm_second[1],
        total_up,
        total_down,
    )


LANES = 128
BLOCK = 256
BF = jnp.bfloat16
F32 = jnp.float32


def halves(values):
    high = values.astype(BF).astype(F32)
    return high, values - high


def roll_half(values):
    return pltpu.roll(values, LANES // 2, 1)


def low_lanes(rows):
    return lax.broadcasted_iota(jnp.int32, (rows, LANES), 1) < LANES // 2


def pair_tiles(values):
    high, low = halves(values)
    first = low_lanes(values.shape[0])
    return (
        jnp.where(first, high, roll_half(low)).astype(BF),
        jnp.where(first, roll_half(high), low).astype(BF),
    )


def spread_tiles(values):
    high, low = halves(values)
    first = low_lanes(values.shape[0])
    high_r, low_r = roll_half(high), roll_half(low)
    return (
        jnp.concatenate([jnp.where(first, high, high_r), jnp.where(first, low, low_r)], axis=1).astype(BF),
        jnp.concatenate([jnp.where(first, high_r, high), jnp.where(first, low_r, low)], axis=1).astype(BF),
    )


def nt(left, right):
    return lax.dot_general(left, right, (((1,), (1,)), ((), ())), preferred_element_type=F32)


def nn(left, right):
    return lax.dot_general(left, right, (((1,), (0,)), ((), ())), preferred_element_type=F32)


def tn(left, right):
    return lax.dot_general(left, right, (((0,), (0,)), ((), ())), preferred_element_type=F32)


def split_bf(values):
    high = values.astype(BF)
    return high, (values - high.astype(F32)).astype(BF)


def forward_kernel(pos_ref, seg_ref, *refs):
    (own_ref, in_ref, seg_col, seg_row,
     o_own, o_out, lse_ref, tq, hk, tv, out_s) = refs
    rows = own_ref.shape[0]
    own = pl.multiple_of(pos_ref[0] * rows, rows)
    other = pl.multiple_of((1 - pos_ref[0]) * rows, rows)
    for place, ref in ((own, own_ref), (other, in_ref)):
        span = pl.ds(place, rows)
        q, k, v = (ref.at[:, i * LANES:(i + 1) * LANES] for i in range(3))
        for head, tile in enumerate(pair_tiles(q[...] * 0.125)):
            tq[head, span, :] = jnp.concatenate([tile, tile], axis=1)
        for head, tile in enumerate(spread_tiles(k[...])):
            hk[head, span, :] = tile
        for head, tile in enumerate(pair_tiles(v[...])):
            tv[head, span, :] = tile
    blocks = 2 * rows // BLOCK
    first = low_lanes(BLOCK)

    def query_block(i, carry):
        q_span = pl.ds(pl.multiple_of(i * BLOCK, BLOCK), BLOCK)
        first_label = seg_ref[i * BLOCK]
        start = jnp.int32(0)
        for j in range(blocks):
            start = start + jnp.where((j < i) & (seg_ref[j * BLOCK + BLOCK - 1] < first_label), 1, 0)
        label = seg_col[q_span, :1]
        q_place = i * BLOCK + lax.broadcasted_iota(jnp.int32, (BLOCK, BLOCK), 0)

        def key_block(step, state):
            j = i - step
            k_span = pl.ds(pl.multiple_of(j * BLOCK, BLOCK), BLOCK)
            k_place = j * BLOCK + lax.broadcasted_iota(jnp.int32, (BLOCK, BLOCK), 1)
            allowed = (label == seg_row[j]) & (k_place <= q_place)
            new_state = []
            for head in range(2):
                top, total, acc = state[head]
                scores = nt(tq[head, q_span, :], hk[head, k_span, :])
                scores = jnp.where(allowed, scores, -1e30)
                new_top = jnp.maximum(top, jnp.max(scores, axis=1, keepdims=True))
                weight = jnp.exp(scores - new_top)
                keep = jnp.exp(top - new_top)
                high, low = split_bf(weight)
                values = tv[head, k_span, :]
                new_state.append((
                    new_top,
                    total * keep + jnp.sum(weight, axis=1, keepdims=True),
                    acc * keep + nn(high, values) + nn(low, values),
                ))
            return tuple(new_state)

        init = (
            jnp.full((BLOCK, 1), -1e30, F32),
            jnp.zeros((BLOCK, 1), F32),
            jnp.zeros((BLOCK, LANES), F32),
        )
        state = lax.fori_loop(0, i - start + 1, key_block, (init, init))
        outs, logs = [], []
        for top, total, acc in state:
            outs.append((acc + roll_half(acc)) / total)
            logs.append(jnp.broadcast_to(top + jnp.log(total), (BLOCK, LANES)))
        out_s[q_span, :] = jnp.where(first, outs[0], outs[1])
        lse_ref[q_span, :] = jnp.where(first, logs[0], logs[1])
        return carry

    lax.fori_loop(0, blocks, query_block, 0)
    o_own[...] = out_s[pl.ds(own, rows), :]
    o_out[...] = out_s[pl.ds(other, rows), :]


def attend_forward(own, received, position, labels, labels_wide, labels_row):
    rows = own.shape[0]
    length = 2 * rows
    smem = pl.BlockSpec(memory_space=pltpu.SMEM)
    vmem = pl.BlockSpec(memory_space=pltpu.VMEM)
    return pl.pallas_call(
        forward_kernel,
        in_specs=[smem, smem] + [vmem] * 4,
        out_specs=[vmem] * 3,
        scratch_shapes=[
            pltpu.VMEM((2, length, 2 * LANES), BF),
            pltpu.VMEM((2, length, 2 * LANES), BF),
            pltpu.VMEM((2, length, LANES), BF),
            pltpu.VMEM((length, LANES), F32),
        ],
        out_shape=[
            jax.ShapeDtypeStruct((rows, LANES), F32),
            jax.ShapeDtypeStruct((rows, LANES), F32),
            jax.ShapeDtypeStruct((length, LANES), F32),
        ],
        cost_estimate=pl.CostEstimate(flops=6 * 10**9, bytes_accessed=28 * rows * LANES, transcendentals=length * length),
        compiler_params=pltpu.CompilerParams(vmem_limit_bytes=32 * 1024 * 1024),
        name="attend_forward",
    )(position, labels, own, received, labels_wide, labels_row)


def backward_kernel(pos_ref, seg_ref, *refs):
    (own_ref, in_ref, o_own, o_in, g_own, g_in, lse_ref, seg_col, seg_row,
     grad_own, grad_out,
     tq, hk, tk, hv, tg, lse_t, delta_t, gq_s, gk_s, gv_s) = refs
    rows = own_ref.shape[0]
    length = 2 * rows
    own = pl.multiple_of(pos_ref[0] * rows, rows)
    other = pl.multiple_of((1 - pos_ref[0]) * rows, rows)
    half = LANES // 2
    for place, ref, o, g in ((own, own_ref, o_own, g_own), (other, in_ref, o_in, g_in)):
        span = pl.ds(place, rows)
        q, k, v = (ref.at[:, i * LANES:(i + 1) * LANES] for i in range(3))
        for head, tile in enumerate(pair_tiles(q[...] * 0.125)):
            tq[head, span, :] = jnp.concatenate([tile, tile], axis=1)
        for head, tile in enumerate(pair_tiles(g[...])):
            tg[head, span, :] = jnp.concatenate([tile, tile], axis=1)
        for head, tile in enumerate(spread_tiles(k[...])):
            hk[head, span, :] = tile
        for head, tile in enumerate(spread_tiles(v[...])):
            hv[head, span, :] = tile
        for head, tile in enumerate(pair_tiles(k[...])):
            tk[head, span, :] = tile
        turned = jnp.transpose(o[...] * g[...])
        for head in range(2):
            delta_t[head, 0:1, span] = jnp.sum(turned[head * half:(head + 1) * half], axis=0, keepdims=True)
    turned = jnp.transpose(lse_ref[...])
    for head in range(2):
        lse_t[head, 0:1, :] = turned[head * half:head * half + 1]
    blocks = length // BLOCK
    first = low_lanes(BLOCK)
    gq_s[...] = jnp.zeros_like(gq_s)

    def key_block(j, carry):
        k_span = pl.ds(pl.multiple_of(j * BLOCK, BLOCK), BLOCK)
        last_label = seg_ref[j * BLOCK + BLOCK - 1]
        count = jnp.int32(1)
        for i in range(blocks):
            count = count + jnp.where((i > j) & (seg_ref[i * BLOCK] <= last_label), 1, 0)
        label = seg_col[k_span, :1]
        k_place = j * BLOCK + lax.broadcasted_iota(jnp.int32, (BLOCK, BLOCK), 0)

        def query_block(step, state):
            i = j + step
            q_span = pl.ds(pl.multiple_of(i * BLOCK, BLOCK), BLOCK)
            q_place = i * BLOCK + lax.broadcasted_iota(jnp.int32, (BLOCK, BLOCK), 1)
            allowed = (label == seg_row[i]) & (k_place <= q_place)
            new_state = []
            for head in range(2):
                grad_k, grad_v = state[head]
                query = tq[head, q_span, :]
                grad = tg[head, q_span, :]
                scores = nt(hk[head, k_span, :], query)
                weight = jnp.exp(jnp.where(allowed, scores - lse_t[head, 0:1, q_span], -1e30))
                grad_weight = nt(hv[head, k_span, :], grad)
                grad_score = weight * (grad_weight - delta_t[head, 0:1, q_span])
                w_high, w_low = split_bf(weight)
                s_high, s_low = split_bf(grad_score)
                grad_v = grad_v + nn(w_high, grad[:, :LANES]) + nn(w_low, grad[:, :LANES])
                grad_k = grad_k + nn(s_high, query[:, :LANES]) + nn(s_low, query[:, :LANES])
                keys = tk[head, k_span, :]
                gq_s[head, q_span, :] += tn(s_high, keys) + tn(s_low, keys)
                new_state.append((grad_k, grad_v))
            return tuple(new_state)

        zero = jnp.zeros((BLOCK, LANES), F32)
        state = lax.fori_loop(0, count, query_block, ((zero, zero), (zero, zero)))
        for slot, store in ((0, gk_s), (1, gv_s)):
            left, right = state[0][slot], state[1][slot]
            store[k_span, :] = jnp.where(first, left + roll_half(left), right + roll_half(right))
        return carry

    lax.fori_loop(0, blocks, key_block, 0)
    wide = low_lanes(rows)
    for place, ref in ((own, grad_own), (other, grad_out)):
        span = pl.ds(place, rows)
        left, right = gq_s[0, span, :], gq_s[1, span, :]
        ref[:, :LANES] = jnp.where(wide, left + roll_half(left), right + roll_half(right)) * 0.125
        ref[:, LANES:2 * LANES] = gk_s[span, :]
        ref[:, 2 * LANES:] = gv_s[span, :]


def attend_backward(own, received, out_own, out_in, grad_own, grad_in, logs, position, labels, labels_wide, labels_row):
    rows = own.shape[0]
    length = 2 * rows
    smem = pl.BlockSpec(memory_space=pltpu.SMEM)
    vmem = pl.BlockSpec(memory_space=pltpu.VMEM)
    return pl.pallas_call(
        backward_kernel,
        in_specs=[smem, smem] + [vmem] * 9,
        out_specs=[vmem] * 2,
        scratch_shapes=[
            pltpu.VMEM((2, length, 2 * LANES), BF),
            pltpu.VMEM((2, length, 2 * LANES), BF),
            pltpu.VMEM((2, length, LANES), BF),
            pltpu.VMEM((2, length, 2 * LANES), BF),
            pltpu.VMEM((2, length, 2 * LANES), BF),
            pltpu.VMEM((2, 8, length), F32),
            pltpu.VMEM((2, 8, length), F32),
            pltpu.VMEM((2, length, LANES), F32),
            pltpu.VMEM((length, LANES), F32),
            pltpu.VMEM((length, LANES), F32),
        ],
        out_shape=[jax.ShapeDtypeStruct((rows, 3 * LANES), F32)] * 2,
        cost_estimate=pl.CostEstimate(flops=13 * 10**9, bytes_accessed=60 * rows * LANES, transcendentals=length * length),
        compiler_params=pltpu.CompilerParams(vmem_limit_bytes=40 * 1024 * 1024),
        name="attend_backward",
    )(position, labels, own, received, out_own, out_in, grad_own, grad_in, logs, labels_wide, labels_row)


MESH = pl.DeviceIdType.MESH
PIECE = 48


def scatter_kernel(plan, groups, *refs):
    count = len(plan)
    units = sum(plan)
    pairs = units // 2
    turned, refs = refs[:count], refs[count:]
    grads = []
    for group in groups:
        grads.append(refs[:group] if group > 1 else refs[0])
        refs = refs[group:]
    stream_ref, weight_ref, norms_ref, extra_ref, total_ref, patch_ref, norm_total_ref, extra_total_ref = refs[:8]
    (t_buf, g_buf, g_high, g_low, part, s_high, s_low, w_buf, p_buf, land_a, n_x, n_z, n_y, y_y, y_x, y_z, done,
     v_c, v_x, v_y, v_z, extra_in,
     load_sem, w_sem, p_sem, a_sem, nx_sem, nz_sem, ny_sem, yy_sem, yx_sem, yz_sem, ye_sem, v_sem, o_sem) = refs[8:]
    fsdp = lax.axis_index("fsdp")
    row = lax.axis_index("sp")
    z, x, core = fsdp // 4, (fsdp // 2) % 2, fsdp % 2
    half = PIECE // 2

    def device(z_at, x_at, core_at, row_at):
        return ((z_at * 2 + x_at) * 2 + core_at, row_at)

    sibling = device(z, x, 1 - core, row)
    beside = device(z, 1 - x, core, row)
    across = device(z, x, core, 1 - row)
    along = [device((z + step) % 4, x, core, row) for step in (1, 2, 3)]

    barrier = pltpu.get_barrier_semaphore()
    for peer in [sibling, beside, across] + along:
        pl.semaphore_signal(barrier, inc=1, device_id=peer, device_id_type=MESH)

    def remote(source, target, sems, index, peer):
        return pltpu.make_async_remote_copy(
            src_ref=source, dst_ref=target, send_sem=sems.at[(0,) + index], recv_sem=sems.at[(1,) + index],
            device_id=peer, device_id_type=MESH,
        )

    def loads(unit, slot, act):
        base = 0
        for which in range(count):
            first, last = base, base + plan[which]
            base = last

            @pl.when((unit >= first) & (unit < last))
            def _(which=which, first=first):
                j = unit - first
                for side in range(2):
                    rows_ref = turned[which]
                    source = rows_ref.at[:, side, j] if rows_ref.shape[2] > 1 else rows_ref.at[:, side, 0]
                    act(pltpu.make_async_copy(source, t_buf.at[slot, side], load_sem.at[slot, side]))
                grad = grads[which]
                width = g_buf.shape[2]
                if groups[which] > 1:
                    parts = groups[which] // 2
                    for unit_at in range(plan[which]):
                        @pl.when(j == unit_at)
                        def _(unit_at=unit_at):
                            for place in range(2):
                                side, part = divmod(2 * unit_at + place, parts)
                                for mine in range(2):
                                    @pl.when((row == side) == (mine == 1))
                                    def _(place=place, part=part, mine=mine):
                                        act(pltpu.make_async_copy(
                                            grad[part if mine else parts + part],
                                            g_buf.at[slot, :, pl.ds(place * (width // 2), width // 2)],
                                            load_sem.at[slot, 2 + place],
                                        ))
                    return
                if grad.shape[1] > width:
                    grad = grad.at[:, pl.ds(pl.multiple_of(j * width, width), width)]
                act(pltpu.make_async_copy(grad, g_buf.at[slot], load_sem.at[slot, 2]))

    def start(copy):
        copy.start()

    def wait(copy):
        copy.wait()

    def weight_copy(block, slot):
        return pltpu.make_async_copy(weight_ref.at[block], w_buf.at[slot], w_sem.at[slot])

    def patch_copy(block, slot):
        columns = w_buf.shape[1]
        return pltpu.make_async_copy(
            p_buf.at[slot], patch_ref.at[:, pl.ds(pl.multiple_of(block * columns, columns), columns)], p_sem.at[slot]
        )

    def core_copy(unit, slot):
        return remote(part.at[slot, 1 - core], land_a.at[unit], a_sem, (unit,), sibling)

    def nx_copy(p):
        return remote(land_a.at[2 * p, :, 1 - x], n_x.at[p], nx_sem, (p,), beside)

    def nz_copy(p, step):
        return remote(n_x.at[p, (z + step + 1) % 4], n_z.at[p, step], nz_sem, (p, step), along[step])

    def ny_copy(p):
        return remote(n_x.at[p, z], n_y.at[p], ny_sem, (p,), across)

    def yy_copy(p):
        return remote(
            land_a.at[2 * p + 1, :, :, pl.ds(pl.multiple_of((1 - row) * half, half), half)], y_y.at[p], yy_sem, (p,), across
        )

    def yx_copy(p):
        return remote(y_y.at[p, :, 1 - x], y_x.at[p], yx_sem, (p,), beside)

    def yz_copy(p, step):
        return remote(y_x.at[p, (z + step + 1) % 4], y_z.at[p, step], yz_sem, (p, step), along[step])

    def ye_copy(p):
        place = pl.ds(pl.multiple_of(row * half, half), half)
        return remote(y_x.at[p, z], done.at[2 * p + 1, place], ye_sem, (p,), across)

    loads(0, 0, start)
    weight_copy(0, 0).start()
    s_high[...] = stream_ref[...].astype(BF)
    s_low[...] = (stream_ref[...] - s_high[...].astype(F32)).astype(BF)
    pl.semaphore_wait(barrier, 6)

    v_copies = [
        remote(norms_ref, v_c, v_sem, (0,), sibling),
        remote(v_c, v_x, v_sem, (1,), beside),
        remote(v_x, v_y, v_sem, (2,), across),
    ] + [remote(v_y, v_z.at[step], v_sem, (3 + step,), along[step]) for step in range(3)]
    v_copies[0].start()
    extra_copy = remote(extra_ref, extra_in, v_sem, (6,), across)
    extra_copy.start()

    def compute(unit, slot):
        loads(unit, slot, wait)

        @pl.when(unit + 1 < units)
        def _():
            loads(unit + 1, 1 - slot, start)

        @pl.when(unit >= 2)
        def _():
            core_copy(unit - 2, slot).wait_send()

        grad = g_buf[slot]
        g_high[...] = grad.astype(BF)
        g_low[...] = (grad - g_high[...].astype(F32)).astype(BF)

        def side_of(turn, carry):
            side = jnp.where(turn == 0, 1 - core, core)
            high, low = split_bf(t_buf[slot, side].reshape(8 * PIECE, t_buf.shape[4]))
            product = nn(high, g_high[...]) + nn(high, g_low[...]) + nn(low, g_high[...])
            part[slot, side] = product.reshape(4, 2, PIECE, product.shape[1])

            @pl.when(turn == 0)
            def _():
                core_copy(unit, slot).start()

            return carry

        lax.fori_loop(0, 2, side_of, 0)

    def patch_block(block, slot):
        weight_copy(block, slot).wait()

        @pl.when(block + 1 < weight_ref.shape[0])
        def _():
            weight_copy(block + 1, 1 - slot).start()

        @pl.when(block >= 2)
        def _():
            patch_copy(block - 2, slot).wait()

        high, low = split_bf(w_buf[slot])
        p_buf[slot] = nt(s_high[...], high) + nt(s_high[...], low) + nt(s_low[...], high)
        patch_copy(block, slot).start()

    def loop(number, body):
        def step(i, carry):
            body(i)
            return carry

        lax.fori_loop(0, number, step, 0)

    def after_core(unit, slot):
        core_copy(unit, slot).wait_recv()

        def add(i):
            for b in range(2):
                land_a[unit, i, b] = land_a[unit, i, b] + part[slot, core, i, b]

        loop(4, add)

    def iteration(p, carry):
        @pl.when(p < pairs)
        def _():
            compute(2 * p, 0)
            compute(2 * p + 1, 1)
            after_core(2 * p, 0)
            nx_copy(p).start()
            after_core(2 * p + 1, 1)
            yy_copy(p).start()

        q = p - 1

        @pl.when((q >= 0) & (q < pairs))
        def _():
            nx_copy(q).wait_recv()

            def add_n(i):
                n_x[q, i] = n_x[q, i] + land_a[2 * q, i, x]

            loop(4, add_n)
            for step in range(3):
                nz_copy(q, step).start()
            yy_copy(q).wait_recv()
            own = pl.ds(pl.multiple_of(row * half, half), half)

            def add_y(i):
                for b in range(2):
                    y_y[q, i, b] = y_y[q, i, b] + land_a[2 * q + 1, i, b, own]

            loop(4, add_y)
            yx_copy(q).start()

        @pl.when(p < pairs)
        def _():
            patch_block(2 * p, 0)
            patch_block(2 * p + 1, 1)

        r = p - 2

        @pl.when((r >= 0) & (r < pairs))
        def _():
            for step in range(3):
                nz_copy(r, step).wait_recv()
            n_x[r, z] = n_x[r, z] + n_z[r, 0] + n_z[r, 1] + n_z[r, 2]
            ny_copy(r).start()
            yx_copy(r).wait_recv()

            def add_x(i):
                y_x[r, i] = y_x[r, i] + y_y[r, i, x]

            loop(4, add_x)
            for step in range(3):
                yz_copy(r, step).start()

        s = p - 3

        @pl.when((s >= 0) & (s < pairs))
        def _():
            ny_copy(s).wait_recv()
            done[2 * s] = n_x[s, z] + n_y[s]
            for step in range(3):
                yz_copy(s, step).wait_recv()
            total = y_x[s, z] + y_z[s, 0] + y_z[s, 1] + y_z[s, 2]
            y_x[s, z] = total
            done[2 * s + 1, pl.ds(pl.multiple_of(row * half, half), half)] = total
            ye_copy(s).start()

        @pl.when(p == 0)
        def _():
            v_copies[0].wait_recv()
            v_c[...] = v_c[...] + norms_ref[...]
            v_copies[1].start()

        @pl.when(p == 1)
        def _():
            v_copies[1].wait_recv()
            v_x[...] = v_x[...] + v_c[...]
            v_copies[2].start()

        @pl.when(p == 2)
        def _():
            v_copies[2].wait_recv()
            v_y[...] = v_y[...] + v_x[...]
            for step in range(3):
                v_copies[3 + step].start()

        @pl.when(p == 3)
        def _():
            for step in range(3):
                v_copies[3 + step].wait_recv()
            norm_total_ref[...] = v_y[...] + v_z[0] + v_z[1] + v_z[2]
            extra_copy.wait_recv()
            extra_total_ref[...] = extra_ref[...] + extra_in[...]

        return carry

    lax.fori_loop(0, pairs + 3, iteration, 0)

    def finish(p):
        ye_copy(p).wait()
        nx_copy(p).wait_send()
        ny_copy(p).wait_send()
        yy_copy(p).wait_send()
        yx_copy(p).wait_send()
        for step in range(3):
            nz_copy(p, step).wait_send()
            yz_copy(p, step).wait_send()

    loop(pairs, finish)
    out = pltpu.make_async_copy(done, total_ref, o_sem)
    out.start()
    for copy in v_copies + [extra_copy]:
        copy.wait_send()
    core_copy(units - 2, 0).wait_send()
    core_copy(units - 1, 1).wait_send()
    blocks = weight_ref.shape[0]
    patch_copy(blocks - 2, 0).wait()
    patch_copy(blocks - 1, 1).wait()
    out.wait()


def reduce_gradients(turned, grads, grad_stream, weight, norms, extra):
    rows, width = grad_stream.shape
    plan, views = [], []
    flat, groups = [], []
    for left, right in zip(turned, grads):
        tall = left.shape[0] // (16 * PIECE)
        parts = list(right) if isinstance(right, (tuple, list)) else [right]
        flat += parts
        groups.append(len(parts))
        plan.append(tall * (sum(part.shape[1] for part in parts) // width))
        views.append(left.reshape(8, 2, tall, PIECE, rows))
    units = sum(plan)
    pairs = units // 2
    owners = 16
    block = weight.shape[0] // owners
    assert units == owners
    half = PIECE // 2
    dma = pltpu.SemaphoreType.DMA
    any_space = pl.BlockSpec(memory_space=pl.ANY)
    vmem = pl.BlockSpec(memory_space=pltpu.VMEM)
    flops = 6 * rows * width * (units * 16 * PIECE + weight.shape[0])
    return pl.pallas_call(
        functools.partial(scatter_kernel, tuple(plan), tuple(groups)),
        out_shape=[
            jax.ShapeDtypeStruct((units, PIECE, width), F32),
            jax.ShapeDtypeStruct((rows, weight.shape[0]), F32),
            jax.ShapeDtypeStruct(norms.shape, F32),
            jax.ShapeDtypeStruct(extra.shape, F32),
        ],
        in_specs=[any_space] * (len(views) + len(flat)) + [vmem, any_space, vmem, vmem],
        out_specs=[any_space, any_space, vmem, vmem],
        scratch_shapes=[
            pltpu.VMEM((2, 2, 8, PIECE, rows), F32),
            pltpu.VMEM((2, rows, width), F32),
            pltpu.VMEM((rows, width), BF),
            pltpu.VMEM((rows, width), BF),
            pltpu.VMEM((2, 2, 4, 2, PIECE, width), F32),
            pltpu.VMEM((rows, width), BF),
            pltpu.VMEM((rows, width), BF),
            pltpu.VMEM((2, block, width), F32),
            pltpu.VMEM((2, rows, block), F32),
            pltpu.VMEM((units, 4, 2, PIECE, width), F32),
            pltpu.VMEM((pairs, 4, PIECE, width), F32),
            pltpu.VMEM((pairs, 3, PIECE, width), F32),
            pltpu.VMEM((pairs, PIECE, width), F32),
            pltpu.VMEM((pairs, 4, 2, half, width), F32),
            pltpu.VMEM((pairs, 4, half, width), F32),
            pltpu.VMEM((pairs, 3, half, width), F32),
            pltpu.VMEM((units, PIECE, width), F32),
            pltpu.VMEM(norms.shape, F32),
            pltpu.VMEM(norms.shape, F32),
            pltpu.VMEM(norms.shape, F32),
            pltpu.VMEM((3,) + norms.shape, F32),
            pltpu.VMEM(extra.shape, F32),
            dma((2, 4)), dma((2,)), dma((2,)),
            dma((2, units)), dma((2, pairs)), dma((2, pairs, 3)), dma((2, pairs)),
            dma((2, pairs)), dma((2, pairs)), dma((2, pairs, 3)), dma((2, pairs)),
            dma((2, 7)), dma,
        ],
        cost_estimate=pl.CostEstimate(flops=flops, bytes_accessed=120 * 10**6, transcendentals=0),
        compiler_params=pltpu.CompilerParams(
            collective_id=0, has_side_effects=True, vmem_limit_bytes=67043328
        ),
        name="reduce_gradients",
    )(*views, *flat, grad_stream, weight.reshape(owners, block, width), norms, extra)


CUT_ROWS = 128
CUT_COLUMNS = 128
NARROW = 384


def three(product, left, right):
    return product(left[0], right[0]) + product(left[0], right[1]) + product(left[1], right[0])


def normalized(values):
    average = jnp.mean(values, axis=-1, keepdims=True)
    centred = values - average
    spread = jnp.mean(centred * centred, axis=-1, keepdims=True)
    scale = lax.rsqrt(spread + EPSILON)
    return centred * scale, scale


def gather_kernel(patch_ref, in_ref, qkv_ref, out_ref, vector_ref,
                  stream_ref, normed_ref, turned_ref, patch_turned_ref, in_full, qkv_full, out_full, vectors_ref,
                  sent_0, sent_1, sent_2,
                  patch_buf, in_buf, qkv_buf, out_buf, turn_buf, acc, v_c, v_x, v_z, sent_buf,
                  z_sem, x_sem, y_sem, c_sem, v_sem, own_sem, patch_sem, turn_sem, full_sem, last_sem):
    fsdp = lax.axis_index("fsdp")
    row = lax.axis_index("sp")
    z, x, core = fsdp // 4, (fsdp // 2) % 2, fsdp % 2
    block, width = in_ref.shape
    across_count = width // CUT_COLUMNS
    in_units = (block // CUT_ROWS) * across_count
    narrow = NARROW
    out_units = width // narrow
    units = in_units + qkv_ref.shape[1] // narrow + out_units

    def device(z_at, x_at, core_at, row_at):
        return ((z_at * 2 + x_at) * 2 + core_at, row_at)

    sibling = device(z, x, 1 - core, row)
    beside = device(z, 1 - x, core, row)
    across = device(z, x, core, 1 - row)
    along = [device((z + step) % 4, x, core, row) for step in (1, 2, 3)]
    barrier = pltpu.get_barrier_semaphore()
    for peer in [sibling, beside, across] + along:
        pl.semaphore_signal(barrier, inc=1, device_id=peer, device_id_type=MESH)

    def remote(source, target, sems, index, peer):
        return pltpu.make_async_remote_copy(
            src_ref=source, dst_ref=target, send_sem=sems.at[(0,) + index], recv_sem=sems.at[(1,) + index],
            device_id=peer, device_id_type=MESH,
        )

    patch_copy = pltpu.make_async_copy(patch_ref, patch_buf, patch_sem)

    def span(first, size, step=None):
        return pl.ds(pl.multiple_of(first, step or size), size)

    def places(kind, unit, part):
        if kind == "in":
            j, column = unit // across_count, unit % across_count
            columns = span(column * CUT_COLUMNS, CUT_COLUMNS)
            base, rows, edge = j * CUT_ROWS, CUT_ROWS, 40
        else:
            rows, edge = out_ref.shape[0], 16
            first = in_units if kind == "qkv" else units - out_units
            base, columns = 0, span((unit - first) * narrow, narrow)
        if part is None:
            return span(base, rows, 8), columns
        which, side = part
        if which == 0:
            return span(base + side * (rows - edge), edge, 8), columns
        return span(base + side * edge, rows - edge, 8), columns

    sources = {"in": (in_ref, in_buf), "qkv": (qkv_ref, qkv_buf), "out": (out_ref, out_buf)}

    def each_kind(unit, act):
        ranges = (("in", 0, in_units), ("qkv", in_units, units - out_units), ("out", units - out_units, units))
        for kind, first, last in ranges:
            @pl.when((unit >= first) & (unit < last))
            def _(kind=kind):
                act(kind)

    own_copies = []
    for kind, firsts in (("in", range(0, block, CUT_ROWS)), ("qkv", (0,)), ("out", (0,))):
        source, buf = sources[kind]
        for first in firsts:
            rows = places(kind, first // CUT_ROWS * across_count if kind == "in" else in_units, (1, row))[0]
            own_copies.append(
                pltpu.make_async_copy(source.at[rows], buf.at[z, x, core, rows], own_sem.at[len(own_copies)])
            )

    def z_copy(kind, unit, step):
        source, buf = sources[kind]
        at = places(kind, unit, (1, row))
        return remote(source.at[at], buf.at[(z, x, core) + at], z_sem, (unit, step), along[step])

    def x_copy(kind, unit):
        ref = sources[kind][1].at[(slice(None), x, core) + places(kind, unit, (1, row))]
        return remote(ref, ref, x_sem, (unit,), beside)

    def y_copy(kind, unit):
        ref = sources[kind][1].at[(slice(None), slice(None), core) + places(kind, unit, (0, row))]
        return remote(ref, ref, y_sem, (unit,), across)

    def c_copy(kind, unit, index):
        part = (1, row) if index == 0 else (0, 1 - row)
        ref = sources[kind][1].at[(slice(None), slice(None), core) + places(kind, unit, part)]
        return remote(ref, ref, c_sem, (unit, index), sibling)

    def z_stage(unit):
        def act(kind):
            for step in range(3):
                z_copy(kind, unit, step).start()

        each_kind(unit, act)

    def x_stage(unit):
        def act(kind):
            for step in range(3):
                z_copy(kind, unit, step).wait_recv()
            x_copy(kind, unit).start()

        each_kind(unit, act)

    def spread_stage(unit):
        def act(kind):
            x_copy(kind, unit).wait_recv()
            y_copy(kind, unit).start()
            c_copy(kind, unit, 0).start()

        each_kind(unit, act)

    def y_stage(unit):
        def act(kind):
            y_copy(kind, unit).wait_recv()
            c_copy(kind, unit, 1).start()

        each_kind(unit, act)

    def ready(unit):
        def act(kind):
            c_copy(kind, unit, 0).wait_recv()
            c_copy(kind, unit, 1).wait_recv()
            full_copy(kind, unit).start()

        each_kind(unit, act)

    def full_copy(kind, unit):
        at = (slice(None), slice(None), slice(None)) + places(kind, unit, None)
        full = {"in": in_full, "qkv": qkv_full, "out": out_full}[kind]
        return pltpu.make_async_copy(sources[kind][1].at[at], full.at[at], full_sem.at[unit])

    def multiply(unit):
        j, column = unit // across_count, unit % across_count
        columns = span(column * CUT_COLUMNS, CUT_COLUMNS)
        rows = span(j * CUT_ROWS, CUT_ROWS)

        def step(pair, carry):
            first = pair * 2 * block + j * CUT_ROWS
            left = jnp.concatenate(
                [patch_buf[:, span(first, CUT_ROWS)], patch_buf[:, span(first + block, CUT_ROWS)]], axis=1
            )
            right = in_buf[pair // 2, pair % 2, :, rows, columns].reshape(2 * CUT_ROWS, CUT_COLUMNS)
            acc[:, columns] = acc[:, columns] + three(nn, split_bf(left), split_bf(right))
            return carry

        lax.fori_loop(0, 8, step, 0)

    tiles = patch_ref.shape[1] // LANES
    each = turn_buf.shape[0]

    def turn_copy(tile, slot):
        return pltpu.make_async_copy(turn_buf.at[slot], patch_turned_ref.at[span(tile * LANES, LANES)], turn_sem.at[slot])

    def turn(group):
        for slot in range(each):
            @pl.when(group > 0)
            def _(slot=slot):
                turn_copy((group - 1) * each + slot, slot).wait()

            turn_buf[slot] = jnp.transpose(patch_buf[:, span((group * each + slot) * LANES, LANES)])
            turn_copy(group * each + slot, slot).start()

    pl.semaphore_wait(barrier, 6)
    z_stage(jnp.int32(0))
    z_stage(jnp.int32(1))
    for copy in own_copies:
        copy.start()
    patch_copy.start()
    v_copies = [
        remote(vector_ref, v_c, v_sem, (0,), sibling),
        remote(v_c, v_x, v_sem, (1,), beside),
    ] + [remote(v_x, v_z.at[step], v_sem, (2 + step,), along[step]) for step in range(3)]
    v_copies[0].start()
    acc[...] = jnp.zeros_like(acc)
    for copy in own_copies:
        copy.wait()

    def iteration(t, carry):
        z_stage(t + 2)
        x_stage(t)
        spread_stage(t - 2)
        y_stage(t - 4)

        @pl.when(t == 0)
        def _():
            patch_copy.wait()
            v_copies[0].wait_recv()
            v_c[...] = v_c[...] + vector_ref[...]
            v_copies[1].start()

        @pl.when(t == 1)
        def _():
            v_copies[1].wait_recv()
            v_x[...] = v_x[...] + v_c[...]
            for step in range(3):
                v_copies[2 + step].start()

        @pl.when(t == 2)
        def _():
            for step in range(3):
                v_copies[2 + step].wait_recv()
            vectors_ref[...] = v_x[...] + v_z[0] + v_z[1] + v_z[2]

        @pl.when(t < tiles // each)
        def _():
            turn(t)

        ready(t - 5)

        @pl.when((t >= 5) & (t < in_units + 5))
        def _():
            multiply(t - 5)

        @pl.when(t == in_units + 5)
        def _():
            stream = acc[...]
            stream_ref[...] = stream
            zhat, _ = normalized(stream)
            acc[...] = zhat * vectors_ref[0:1, :] + vectors_ref[1:2, :]
            normed_ref[...] = acc[...]
            turned_ref[...] = jnp.transpose(acc[...])

        return carry

    lax.fori_loop(0, units + 5, iteration, 0)
    left = split_bf(acc[...])
    group_width = sent_0.shape[1]
    last = []
    for group, ref in enumerate((sent_0, sent_1, sent_2)):
        columns = span((1 - row) * 3 * group_width + group * group_width, group_width)
        right = qkv_buf[:, :, :, :, columns].reshape(width, group_width)
        sent_buf[group] = three(nn, left, split_bf(right))
        copy = pltpu.make_async_copy(sent_buf.at[group], ref, last_sem.at[group])
        copy.start()
        last.append(copy)

    def finish(unit, carry):
        def act(kind):
            for step in range(3):
                z_copy(kind, unit, step).wait_send()
            x_copy(kind, unit).wait_send()
            y_copy(kind, unit).wait_send()
            c_copy(kind, unit, 0).wait_send()
            c_copy(kind, unit, 1).wait_send()
            full_copy(kind, unit).wait()

        each_kind(unit, act)
        return carry

    lax.fori_loop(0, units, finish, 0)
    for copy in v_copies:
        copy.wait_send()
    for slot in range(each):
        turn_copy(tiles - each + slot, slot).wait()
    for copy in last:
        copy.wait()


def gather_stream(patch_rows, w_in, w_qkv, w_out, vectors):
    rows, patch_width = patch_rows.shape
    block, width = w_in.shape
    piece, columns = w_qkv.shape
    group = columns // 6
    any_space = pl.BlockSpec(memory_space=pl.ANY)
    vmem = pl.BlockSpec(memory_space=pltpu.VMEM)
    dma = pltpu.SemaphoreType.DMA
    units = (block // CUT_ROWS) * (width // CUT_COLUMNS) + (columns + width) // NARROW
    owners = (4, 2, 2)

    def array(*shape):
        return jax.ShapeDtypeStruct(shape, F32)

    return pl.pallas_call(
        gather_kernel,
        out_shape=[
            array(rows, width), array(rows, width), array(width, rows), array(patch_width, rows),
            array(*owners, block, width), array(*owners, piece, columns), array(*owners, piece, width),
            array(*vectors.shape), array(rows, group), array(rows, group), array(rows, group),
        ],
        in_specs=[any_space] * 4 + [vmem],
        out_specs=[vmem, vmem, vmem] + [any_space] * 4 + [vmem] + [any_space] * 3,
        scratch_shapes=[
            pltpu.VMEM((rows, patch_width), F32),
            pltpu.VMEM(owners + (block, width), F32),
            pltpu.VMEM(owners + (piece, columns), F32),
            pltpu.VMEM(owners + (piece, width), F32),
            pltpu.VMEM((4, LANES, rows), F32),
            pltpu.VMEM((rows, width), F32),
            pltpu.VMEM(vectors.shape, F32),
            pltpu.VMEM(vectors.shape, F32),
            pltpu.VMEM((3,) + vectors.shape, F32),
            pltpu.VMEM((3, rows, group), F32),
            dma((2, units, 3)), dma((2, units)), dma((2, units)), dma((2, units, 2)), dma((2, 5)),
            dma((block // CUT_ROWS + 2,)), dma, dma((4,)), dma((units,)), dma((3,)),
        ],
        cost_estimate=pl.CostEstimate(flops=6 * rows * patch_width * width, bytes_accessed=90 * 10**6, transcendentals=0),
        compiler_params=pltpu.CompilerParams(collective_id=1, has_side_effects=True, vmem_limit_bytes=67043328),
        name="gather_stream",
    )(patch_rows, w_in, w_qkv, w_out, vectors)


def own_kernel(pos_ref, normed_ref, weight_ref, *outs):
    step = pl.program_id(0)
    weight = weight_ref[...].reshape(normed_ref.shape[1], weight_ref.shape[4])
    product = three(nn, split_bf(normed_ref[...]), split_bf(weight))
    for i, ref in enumerate(outs):
        @pl.when(step == i)
        def _(ref=ref):
            ref[...] = product


def project_own(position, normed, qkv_full):
    rows, width = normed.shape
    owners, columns = qkv_full.shape[:4], qkv_full.shape[4]
    group = columns // 6
    return pl.pallas_call(
        own_kernel,
        grid_spec=pltpu.PrefetchScalarGridSpec(
            num_scalar_prefetch=1,
            grid=(3,),
            in_specs=[
                pl.BlockSpec((rows, width), lambda g, pos: (0, 0)),
                pl.BlockSpec(owners + (group,), lambda g, pos: (0, 0, 0, 0, pos[0] * 3 + g)),
            ],
            out_specs=[pl.BlockSpec((rows, group), lambda g, pos: (0, 0))] * 3,
        ),
        out_shape=[jax.ShapeDtypeStruct((rows, group), F32)] * 3,
        cost_estimate=pl.CostEstimate(flops=3 * rows * width * columns, bytes_accessed=8 * 10**6, transcendentals=0),
        compiler_params=pltpu.CompilerParams(vmem_limit_bytes=40 * 1024 * 1024),
        name="project_own",
    )(position, normed, qkv_full)


def gelu_and_slope(values):
    root = 0.7978845608028654
    square = values * values
    bent = jnp.tanh(root * (values + 0.044715 * values * square))
    half = 0.5 + 0.5 * bent
    slope = half + 0.5 * values * (1.0 - bent * bent) * (root * (1.0 + 0.134145 * square))
    return values * half, slope


def norm_back(grad, values, gain):
    zhat, scale = normalized(values)
    scaled = grad * gain
    back = scale * (
        scaled - jnp.mean(scaled, axis=-1, keepdims=True) - zhat * jnp.mean(scaled * zhat, axis=-1, keepdims=True)
    )
    return back, jnp.sum(grad * zhat, axis=0, keepdims=True), jnp.sum(grad, axis=0, keepdims=True)


def middle_kernel(pos_ref, *refs):
    own_parts, in_parts = refs[0:3], refs[3:6]
    (stream_ref, cot_ref, out_ref, vectors_ref, up_ref, down_ref,
     block_ref, grad_pre_ref, grad_down_ref, grad_resid_ref, turned_ref, attended_ref) = refs[6:18]
    sent_refs, own_refs, sums_ref = refs[18:21], refs[21:24], refs[24]
    residual, norm_high, norm_low, cot_high, cot_low, grad_norm = refs[25:]
    step = pl.program_id(0)
    width = out_ref.shape[0]
    half = width // 2
    own = pl.ds(pl.multiple_of(pos_ref[0] * half, half), half)
    other = pl.ds(pl.multiple_of((1 - pos_ref[0]) * half, half), half)

    @pl.when(step == 0)
    def _():
        total = stream_ref[...]
        for span, parts in ((own, own_parts), (other, in_parts)):
            left = jnp.concatenate([part[...] for part in parts], axis=1)
            attended_ref[span, :] = jnp.transpose(left)
            total = total + three(nn, split_bf(left), split_bf(out_ref[span, :]))
        residual[...] = total
        block_ref[...] = total
        zhat, _ = normalized(total)
        normed = zhat * vectors_ref[2:3, :] + vectors_ref[3:4, :]
        turned_ref[...] = jnp.transpose(normed)
        norm_high[...], norm_low[...] = split_bf(normed)
        cot_high[...], cot_low[...] = split_bf(cot_ref[...])
        grad_norm[...] = jnp.zeros_like(grad_norm)

    up = split_bf(up_ref[...].reshape(width, width))
    hidden, slope = gelu_and_slope(three(nn, (norm_high[...], norm_low[...]), up))
    down = split_bf(down_ref[...].reshape(width, width))
    cot = (cot_high[...], cot_low[...])
    grad_pre = three(nt, cot, down) * slope
    grad_pre_ref[...] = grad_pre
    parts = split_bf(hidden)
    block_ref[...] = block_ref[...] + three(nn, parts, down)
    grad_down_ref[...] = three(tn, parts, cot).reshape(grad_down_ref.shape)
    grad_norm[...] = grad_norm[...] + three(nt, split_bf(grad_pre), up)

    @pl.when(step == pl.num_programs(0) - 1)
    def _():
        back, gain, offset = norm_back(grad_norm[...], residual[...], vectors_ref[2:3, :])
        grad = cot_ref[...] + back
        grad_resid_ref[...] = grad
        sums_ref[...] = jnp.zeros_like(sums_ref)
        sums_ref[2:3, :] = gain
        sums_ref[3:4, :] = offset
        left = split_bf(grad)
        for span, outs in ((other, sent_refs), (own, own_refs)):
            product = three(nt, left, split_bf(out_ref[span, :]))
            for i, ref in enumerate(outs):
                ref[...] = product[:, i * LANES:(i + 1) * LANES]


def middle(position, out_own, out_in, stream, cotangent, w_out, vectors, weights):
    rows, width = stream.shape
    owners, stacked = weights.shape[0], weights.shape[1]
    piece = width // owners
    steps = stacked // piece // 2
    whole = lambda *shape: pl.BlockSpec(shape, lambda j, *_: (0,) * len(shape))
    array = lambda *shape: jax.ShapeDtypeStruct(shape, F32)
    head = whole(rows, LANES)
    return pl.pallas_call(
        middle_kernel,
        grid_spec=pltpu.PrefetchScalarGridSpec(
            num_scalar_prefetch=1,
            grid=(steps,),
            in_specs=[head] * 6 + [
                whole(rows, width), whole(rows, width), whole(width, width), whole(*vectors.shape),
                pl.BlockSpec((owners, piece, width), lambda j, *_: (0, j, 0)),
                pl.BlockSpec((owners, piece, width), lambda j, *_: (0, steps + j, 0)),
            ],
            out_specs=[
                whole(rows, width),
                pl.BlockSpec((rows, width), lambda j, *_: (0, j)),
                pl.BlockSpec((owners, piece, width), lambda j, *_: (0, j, 0)),
                whole(rows, width), whole(width, rows), whole(width, rows),
            ] + [head] * 6 + [whole(*vectors.shape)],
            scratch_shapes=[
                pltpu.VMEM((rows, width), F32),
                pltpu.VMEM((rows, width), BF), pltpu.VMEM((rows, width), BF),
                pltpu.VMEM((rows, width), BF), pltpu.VMEM((rows, width), BF),
                pltpu.VMEM((rows, width), F32),
            ],
        ),
        out_shape=[
            array(rows, width), array(rows, steps * width), array(owners, steps * piece, width),
            array(rows, width), array(width, rows), array(width, rows),
        ] + [array(rows, LANES)] * 6 + [array(*vectors.shape)],
        cost_estimate=pl.CostEstimate(
            flops=6 * rows * width * width * (5 * steps + 2), bytes_accessed=60 * 10**6, transcendentals=rows * steps * width
        ),
        compiler_params=pltpu.CompilerParams(vmem_limit_bytes=62 * 1024 * 1024),
        name="feed_forward",
    )(position, *out_own, *out_in, stream, cotangent, w_out, vectors, weights, weights)


def partial_kernel(pos_ref, g0, g1, g2, weight_ref, out_ref):
    width = out_ref.shape[1]
    weight = weight_ref[...].reshape(width, weight_ref.shape[4])
    left = jnp.concatenate([g0[...], g1[...], g2[...]], axis=1)
    out_ref[...] = three(nt, split_bf(left), split_bf(weight))


def grad_normed_part(position, grads, qkv_full):
    rows = grads[0].shape[0]
    owners, columns = qkv_full.shape[:4], qkv_full.shape[4]
    width = owners[0] * owners[1] * owners[2] * owners[3]
    part = pl.BlockSpec((rows, columns // 6), lambda i, pos: (0, 0))
    return pl.pallas_call(
        partial_kernel,
        grid_spec=pltpu.PrefetchScalarGridSpec(
            num_scalar_prefetch=1,
            grid=(1,),
            in_specs=[part] * 3 + [pl.BlockSpec(owners + (columns // 2,), lambda i, pos: (0, 0, 0, 0, pos[0]))],
            out_specs=pl.BlockSpec((rows, width), lambda i, pos: (0, 0)),
        ),
        out_shape=jax.ShapeDtypeStruct((rows, width), F32),
        cost_estimate=pl.CostEstimate(flops=3 * rows * width * columns, bytes_accessed=8 * 10**6, transcendentals=0),
        compiler_params=pltpu.CompilerParams(vmem_limit_bytes=40 * 1024 * 1024),
        name="grad_normed_part",
    )(position, *grads, qkv_full)


def stream_kernel(pos_ref, g0, g1, g2, weight_ref, part_ref, stream_ref, resid_ref, vectors_ref, before_ref, out_ref, sums_ref):
    width = out_ref.shape[1]
    weight = weight_ref[...].reshape(width, weight_ref.shape[4])
    left = jnp.concatenate([g0[...], g1[...], g2[...]], axis=1)
    grad = part_ref[...] + three(nt, split_bf(left), split_bf(weight))
    back, gain, offset = norm_back(grad, stream_ref[...], vectors_ref[0:1, :])
    out_ref[...] = resid_ref[...] + back
    sums_ref[...] = before_ref[...]
    sums_ref[0:1, :] = gain
    sums_ref[1:2, :] = offset


def grad_of_stream(position, grads, qkv_full, part, stream, grad_resid, vectors, sums):
    rows, width = stream.shape
    owners, columns = qkv_full.shape[:4], qkv_full.shape[4]
    whole = lambda *shape: pl.BlockSpec(shape, lambda i, pos: (0,) * len(shape))
    return pl.pallas_call(
        stream_kernel,
        grid_spec=pltpu.PrefetchScalarGridSpec(
            num_scalar_prefetch=1,
            grid=(1,),
            in_specs=[whole(rows, columns // 6)] * 3
            + [pl.BlockSpec(owners + (columns // 2,), lambda i, pos: (0, 0, 0, 0, 1 - pos[0]))]
            + [whole(rows, width)] * 3 + [whole(*vectors.shape)] * 2,
            out_specs=[whole(rows, width), whole(*vectors.shape)],
        ),
        out_shape=[jax.ShapeDtypeStruct((rows, width), F32), jax.ShapeDtypeStruct(vectors.shape, F32)],
        cost_estimate=pl.CostEstimate(flops=3 * rows * width * columns, bytes_accessed=14 * 10**6, transcendentals=0),
        compiler_params=pltpu.CompilerParams(vmem_limit_bytes=48 * 1024 * 1024),
        name="grad_of_stream",
    )(position, *grads, qkv_full, part, stream, grad_resid, vectors, sums)


def fast_shards(
    patches, segments, w_in, norm1_gain, norm1_bias, w_qkv, w_out, norm2_gain, norm2_bias, w_up, w_down, cotangent
):
    _, rows, patch_width = patches.shape
    piece, width = w_out.shape
    hidden = w_up.shape[1]
    owners = lax.axis_size("fsdp")
    position = lax.axis_index("sp")
    index = lax.axis_index("fsdp")
    places = position[None].astype(jnp.int32)
    labels = segments[0]
    length = labels.shape[0]
    labels_wide = jnp.broadcast_to(labels[:, None], (length, LANES))
    labels_row = labels.reshape(length // BLOCK, 1, BLOCK)
    blocks = hidden // width
    swap = [(0, 1), (1, 0)]

    qkv_own = w_qkv.reshape(piece, 3, 2, 3, LANES).transpose(0, 2, 3, 1, 4).reshape(piece, 3 * width)
    vectors_own = lax.dynamic_update_slice(
        jnp.zeros((8, width), F32),
        jnp.concatenate([jnp.stack([norm1_gain, norm1_bias, norm2_gain, norm2_bias]), jnp.zeros((4, piece), F32)]),
        (0, index * piece),
    )
    (stream, normed, normed_turned, patches_turned, in_full, qkv_full, out_full, vectors, *sent) = gather_stream(
        patches[0], w_in, qkv_own, w_out, vectors_own
    )
    up_own = w_up.reshape(piece, owners, blocks, piece).transpose(2, 0, 1, 3).reshape(blocks * piece, width)
    stacked = jnp.concatenate([up_own, w_down], axis=0)
    stacked, _ = lax.optimization_barrier((stacked, vectors))
    weights = lax.all_gather(stacked, "fsdp", axis=0, tiled=True).reshape(owners, 2 * blocks * piece, width)
    received = [lax.ppermute(part, "sp", swap) for part in sent]
    own = project_own(places, normed, qkv_full)
    attended = [attend_forward(a, b, places, labels, labels_wide, labels_row) for a, b in zip(own, received)]
    out_in = [lax.ppermute(part[1], "sp", swap) for part in attended]
    (block_out, grad_pre, grad_down, grad_resid, normed_two_turned, attended_turned,
     *grads) = middle(
        places, [part[0] for part in attended], out_in, stream, cotangent[0], out_full.reshape(width, width), vectors, weights
    )
    grad_sent, grad_own, sums = grads[:3], grads[3:6], grads[6]
    down_part = lax.psum_scatter(
        grad_down.reshape(hidden, width), "fsdp", scatter_dimension=0, tiled=True
    )
    grad_in = [lax.ppermute(part, "sp", swap) for part in grad_sent]
    both = [
        attend_backward(own[i], received[i], attended[i][0], attended[i][1], grad_own[i], grad_in[i], attended[i][2],
                        places, labels, labels_wide, labels_row)
        for i in range(3)
    ]
    mine = [pair[0] for pair in both]
    theirs = [lax.ppermute(pair[1], "sp", swap) for pair in both]
    part = grad_normed_part(places, mine, qkv_full)
    grad_stream, sums = grad_of_stream(places, theirs, qkv_full, part, stream, grad_resid, vectors, sums)
    pieces, grad_patch, vector_sums, total_down = reduce_gradients(
        [normed_two_turned, attended_turned, normed_turned, patches_turned],
        [grad_pre, grad_resid, mine + theirs, grad_stream],
        grad_stream, in_full.reshape(owners * in_full.shape[3], width), sums, down_part,
    )
    vector_sums = lax.dynamic_slice(vector_sums, (0, index * piece), (4, piece))
    grad_up = pieces[:blocks].reshape(blocks, piece, owners, piece).transpose(1, 2, 0, 3).reshape(piece, hidden)
    first = blocks + 1
    grad_qkv = jnp.concatenate([pieces[first + i] for i in range(3)], axis=1)
    grad_qkv = grad_qkv.reshape(piece, 2, 3, 3, LANES).transpose(0, 3, 1, 2, 4).reshape(piece, 3 * width)
    grad_w_in = pieces[first + 3:].reshape(w_in.shape)
    return (
        block_out[None], grad_patch[None], grad_w_in, vector_sums[0], vector_sums[1],
        grad_qkv, pieces[blocks], vector_sums[2], vector_sums[3], grad_up, total_down,
    )


def solution(mesh):
    sharded = P("fsdp", "sp", None)
    matrix = P("fsdp", None)
    vector = P("fsdp")
    fast = mesh.shape["fsdp"] == 16 and mesh.shape["sp"] == 2
    return jax.shard_map(
        fast_shards if fast else shards,
        mesh=mesh,
        in_specs=(sharded, matrix, matrix, vector, vector, matrix, matrix, vector, vector, matrix, matrix, sharded),
        out_specs=(sharded, sharded, matrix, vector, vector, matrix, matrix, vector, vector, matrix, matrix),
        check_vma=False,
    )
```

```python
import functools

import jax
import jax.numpy as jnp
from jax import lax
from jax.experimental import pallas as pl
from jax.experimental.pallas import tpu as pltpu
from jax.sharding import PartitionSpec as P

HEADS = 12


EPSILON = 1e-05


def matmul(left_side, right_side):
    return jnp.dot(
        left_side, right_side, precision=lax.Precision.HIGH, preferred_element_type=jnp.float32
    )


def matmul_tn(left_side, right_side):
    return lax.dot_general(
        left_side,
        right_side,
        (((0,), (0,)), ((), ())),
        precision=lax.Precision.HIGH,
        preferred_element_type=jnp.float32,
    )


def matmul_nt(left_side, right_side):
    return lax.dot_general(
        left_side,
        right_side,
        (((1,), (1,)), ((), ())),
        precision=lax.Precision.HIGH,
        preferred_element_type=jnp.float32,
    )


def layer_norm(values, scaling, offset):
    average = jnp.mean(values, axis=-1, keepdims=True)
    centred = values - average
    spread = jnp.mean(centred * centred, axis=-1, keepdims=True)
    return centred * lax.rsqrt(spread + EPSILON) * scaling + offset


def gelu_tanh(values):
    return jax.nn.gelu(values, approximate=True)


def scored(queries, key_rows, labels):
    length = labels.shape[0]
    factor = queries.shape[-1] ** (-0.5)
    raw_scores = matmul_nt(queries, key_rows) * factor
    places = jnp.arange(length, dtype=jnp.int32)
    allowed = (labels[:, None] == labels[None, :]) & (places[None, :] <= places[:, None])
    return (raw_scores, allowed, factor)


def attend_one(packed):
    queries, key_rows, value_rows, labels = packed
    raw_scores, allowed, factor = scored(queries, key_rows, labels)
    masked = jnp.where(allowed, raw_scores, -1e30)
    row_max = jnp.max(masked, axis=1, keepdims=True)
    exponent = jnp.exp(masked - row_max)
    summed = jnp.sum(exponent, axis=1, keepdims=True)
    attended = matmul(exponent / summed, value_rows)
    return (attended, (row_max + jnp.log(summed))[:, 0])


def attend_back(packed):
    queries, key_rows, value_rows, attended, log_total, grad_attended, labels = packed
    raw_scores, allowed, factor = scored(queries, key_rows, labels)
    weights = jnp.where(
        allowed, jnp.exp(jnp.where(allowed, raw_scores - log_total[:, None], -1e30)), 0.0
    )
    grad_values = matmul_tn(weights, grad_attended)
    grad_weights = matmul_nt(grad_attended, value_rows)
    row_dot = jnp.sum(grad_attended * attended, axis=1, keepdims=True)
    grad_scores = weights * (grad_weights - row_dot) * factor
    grad_queries = matmul(grad_scores, key_rows)
    grad_keys = matmul_tn(grad_scores, queries)
    return (grad_queries, grad_keys, grad_values)


def to_batch(blocked, heads_local):
    seq_count, length, columns = blocked.shape
    head_dim = columns // heads_local
    return (
        blocked.reshape(seq_count, length, heads_local, head_dim)
        .transpose(0, 2, 1, 3)
        .reshape(seq_count * heads_local, length, head_dim)
    )


def from_batch(blocked, seq_count):
    batch_size, length, head_dim = blocked.shape
    heads_local = batch_size // seq_count
    return (
        blocked.reshape(seq_count, heads_local, length, head_dim)
        .transpose(0, 2, 1, 3)
        .reshape(seq_count, length, heads_local * head_dim)
    )


def shards(
    patches,
    segments,
    w_in,
    norm1_gain,
    norm1_bias,
    w_qkv,
    w_out,
    norm2_gain,
    norm2_bias,
    w_up,
    w_down,
    cotangent,
):
    seq_count, local_len, patch_width = patches.shape
    model_width = w_out.shape[1]
    heads_local = HEADS // lax.axis_size("sp")
    row_count = seq_count * local_len
    norm_params = jnp.stack([norm1_gain, norm1_bias, norm2_gain, norm2_bias])
    gathered = (
        lax.all_gather(w_in, "fsdp", axis=0, tiled=True),
        lax.all_gather(w_qkv, "fsdp", axis=0, tiled=True),
        lax.all_gather(w_out, "fsdp", axis=0, tiled=True),
        lax.all_gather(w_up, "fsdp", axis=0, tiled=True),
        lax.all_gather(w_down, "fsdp", axis=0, tiled=True),
        lax.all_gather(norm_params, "fsdp", axis=1, tiled=True),
    )
    in_full, qkv_full, out_full, up_full, down_full, norm_full = gathered
    patch_rows = patches.reshape(row_count, patch_width)
    stream = matmul(patch_rows, in_full)
    normed, norm1_pull = jax.vjp(layer_norm, stream, norm_full[0], norm_full[1])
    projected = matmul(normed, qkv_full)
    query_tok = projected[:, :model_width].reshape(seq_count, local_len, model_width)
    key_tok = projected[:, model_width : 2 * model_width].reshape(seq_count, local_len, model_width)
    value_tok = projected[:, 2 * model_width :].reshape(seq_count, local_len, model_width)
    query_seq, key_seq, value_seq = (
        lax.all_to_all(query_tok, "sp", split_axis=2, concat_axis=1, tiled=True),
        lax.all_to_all(key_tok, "sp", split_axis=2, concat_axis=1, tiled=True),
        lax.all_to_all(value_tok, "sp", split_axis=2, concat_axis=1, tiled=True),
    )
    labels = jnp.repeat(segments, heads_local, axis=0)
    query_batch = to_batch(query_seq, heads_local)
    key_batch = to_batch(key_seq, heads_local)
    value_batch = to_batch(value_seq, heads_local)
    attended, log_total = lax.map(attend_one, (query_batch, key_batch, value_batch, labels))
    attended_tok = lax.all_to_all(
        from_batch(attended, seq_count), "sp", split_axis=1, concat_axis=2, tiled=True
    )
    attended_rows = attended_tok.reshape(row_count, model_width)
    residual = stream + matmul(attended_rows, out_full)
    normed_two, norm2_pull = jax.vjp(layer_norm, residual, norm_full[2], norm_full[3])
    hidden_pre = matmul(normed_two, up_full)
    hidden, gelu_pull = jax.vjp(gelu_tanh, hidden_pre)
    result = residual + matmul(hidden, down_full)
    block_out = result.reshape(seq_count, local_len, model_width)
    in_back, qkv_back, out_back, up_back, down_back = (
        lax.all_gather(w_in, "fsdp", axis=0, tiled=True),
        lax.all_gather(w_qkv, "fsdp", axis=0, tiled=True),
        lax.all_gather(w_out, "fsdp", axis=0, tiled=True),
        lax.all_gather(w_up, "fsdp", axis=0, tiled=True),
        lax.all_gather(w_down, "fsdp", axis=0, tiled=True),
    )
    grad_rows = cotangent.reshape(row_count, model_width)
    grad_down = matmul_tn(hidden, grad_rows)
    (grad_pre,) = gelu_pull(matmul_nt(grad_rows, down_back))
    grad_up = matmul_tn(normed_two, grad_pre)
    grad_resid_norm, grad_gain_two, grad_offset_two = norm2_pull(matmul_nt(grad_pre, up_back))
    grad_resid = grad_rows + grad_resid_norm
    grad_out = matmul_tn(attended_rows, grad_resid)
    grad_att = matmul_nt(grad_resid, out_back).reshape(seq_count, local_len, model_width)
    grad_att_seq = lax.all_to_all(grad_att, "sp", split_axis=2, concat_axis=1, tiled=True)
    grad_query, grad_key, grad_value = lax.map(
        attend_back,
        (
            query_batch,
            key_batch,
            value_batch,
            attended,
            log_total,
            to_batch(grad_att_seq, heads_local),
            labels,
        ),
    )
    back_query, back_key, back_value = (
        lax.all_to_all(
            from_batch(grad_query, seq_count), "sp", split_axis=1, concat_axis=2, tiled=True
        ),
        lax.all_to_all(
            from_batch(grad_key, seq_count), "sp", split_axis=1, concat_axis=2, tiled=True
        ),
        lax.all_to_all(
            from_batch(grad_value, seq_count), "sp", split_axis=1, concat_axis=2, tiled=True
        ),
    )
    grad_proj = jnp.concatenate([back_query, back_key, back_value], axis=2).reshape(
        row_count, 3 * model_width
    )
    grad_qkv = matmul_tn(normed, grad_proj)
    grad_stream_norm, grad_gain_one, grad_offset_one = norm1_pull(matmul_nt(grad_proj, qkv_back))
    grad_stream = grad_resid + grad_stream_norm
    grad_in = matmul_tn(patch_rows, grad_stream)
    grad_patch = matmul_nt(grad_stream, in_back).reshape(seq_count, local_len, patch_width)
    every_part = (
        lax.psum_scatter(grad_in, "fsdp", scatter_dimension=0, tiled=True),
        lax.psum_scatter(grad_qkv, "fsdp", scatter_dimension=0, tiled=True),
        lax.psum_scatter(grad_out, "fsdp", scatter_dimension=0, tiled=True),
        lax.psum_scatter(grad_up, "fsdp", scatter_dimension=0, tiled=True),
        lax.psum_scatter(grad_down, "fsdp", scatter_dimension=0, tiled=True),
        lax.psum_scatter(
            jnp.stack([grad_gain_one, grad_offset_one, grad_gain_two, grad_offset_two]),
            "fsdp",
            scatter_dimension=1,
            tiled=True,
        ),
    )
    total_in, total_qkv, total_out, total_up, total_down, norm_total = lax.psum(
        (every_part[0], every_part[1], every_part[2], every_part[3], every_part[4], every_part[5]),
        "sp",
    )
    norm_first = norm_total[0:2]
    norm_second = norm_total[2:4]
    return (
        block_out,
        grad_patch,
        total_in,
        norm_first[0],
        norm_first[1],
        total_qkv,
        total_out,
        norm_second[0],
        norm_second[1],
        total_up,
        total_down,
    )


LANES = 128
BLOCK = 256
BF = jnp.bfloat16
F32 = jnp.float32


def halves(values):
    high = values.astype(BF).astype(F32)
    return high, values - high


def roll_half(values):
    return pltpu.roll(values, LANES // 2, 1)


def low_lanes(rows):
    return lax.broadcasted_iota(jnp.int32, (rows, LANES), 1) < LANES // 2


def pair_tiles(values):
    high, low = halves(values)
    first = low_lanes(values.shape[0])
    return (
        jnp.where(first, high, roll_half(low)).astype(BF),
        jnp.where(first, roll_half(high), low).astype(BF),
    )


def spread_tiles(values):
    high, low = halves(values)
    first = low_lanes(values.shape[0])
    high_r, low_r = roll_half(high), roll_half(low)
    return (
        jnp.concatenate([jnp.where(first, high, high_r), jnp.where(first, low, low_r)], axis=1).astype(BF),
        jnp.concatenate([jnp.where(first, high_r, high), jnp.where(first, low_r, low)], axis=1).astype(BF),
    )


def nt(left, right):
    return lax.dot_general(left, right, (((1,), (1,)), ((), ())), preferred_element_type=F32)


def nn(left, right):
    return lax.dot_general(left, right, (((1,), (0,)), ((), ())), preferred_element_type=F32)


def tn(left, right):
    return lax.dot_general(left, right, (((0,), (0,)), ((), ())), preferred_element_type=F32)


def split_bf(values):
    high = values.astype(BF)
    return high, (values - high.astype(F32)).astype(BF)


def forward_kernel(pos_ref, seg_ref, *refs):
    (own_ref, in_ref, seg_col, seg_row,
     o_own, o_out, lse_ref, tq, hk, tv, out_s) = refs
    rows = own_ref.shape[0]
    own = pl.multiple_of(pos_ref[0] * rows, rows)
    other = pl.multiple_of((1 - pos_ref[0]) * rows, rows)
    for place, ref in ((own, own_ref), (other, in_ref)):
        span = pl.ds(place, rows)
        q, k, v = (ref.at[:, i * LANES:(i + 1) * LANES] for i in range(3))
        for head, tile in enumerate(pair_tiles(q[...] * 0.125)):
            tq[head, span, :] = jnp.concatenate([tile, tile], axis=1)
        for head, tile in enumerate(spread_tiles(k[...])):
            hk[head, span, :] = tile
        for head, tile in enumerate(pair_tiles(v[...])):
            tv[head, span, :] = tile
    blocks = 2 * rows // BLOCK
    first = low_lanes(BLOCK)

    def query_block(i, carry):
        q_span = pl.ds(pl.multiple_of(i * BLOCK, BLOCK), BLOCK)
        first_label = seg_ref[i * BLOCK]
        start = jnp.int32(0)
        for j in range(blocks):
            start = start + jnp.where((j < i) & (seg_ref[j * BLOCK + BLOCK - 1] < first_label), 1, 0)
        label = seg_col[q_span, :1]
        q_place = i * BLOCK + lax.broadcasted_iota(jnp.int32, (BLOCK, BLOCK), 0)

        def key_block(step, state):
            j = i - step
            k_span = pl.ds(pl.multiple_of(j * BLOCK, BLOCK), BLOCK)
            k_place = j * BLOCK + lax.broadcasted_iota(jnp.int32, (BLOCK, BLOCK), 1)
            allowed = (label == seg_row[j]) & (k_place <= q_place)
            new_state = []
            for head in range(2):
                top, total, acc = state[head]
                scores = nt(tq[head, q_span, :], hk[head, k_span, :])
                scores = jnp.where(allowed, scores, -1e30)
                new_top = jnp.maximum(top, jnp.max(scores, axis=1, keepdims=True))
                weight = jnp.exp(scores - new_top)
                keep = jnp.exp(top - new_top)
                high, low = split_bf(weight)
                values = tv[head, k_span, :]
                new_state.append((
                    new_top,
                    total * keep + jnp.sum(weight, axis=1, keepdims=True),
                    acc * keep + nn(high, values) + nn(low, values),
                ))
            return tuple(new_state)

        init = (
            jnp.full((BLOCK, 1), -1e30, F32),
            jnp.zeros((BLOCK, 1), F32),
            jnp.zeros((BLOCK, LANES), F32),
        )
        state = lax.fori_loop(0, i - start + 1, key_block, (init, init))
        outs, logs = [], []
        for top, total, acc in state:
            outs.append((acc + roll_half(acc)) / total)
            logs.append(jnp.broadcast_to(top + jnp.log(total), (BLOCK, LANES)))
        out_s[q_span, :] = jnp.where(first, outs[0], outs[1])
        lse_ref[q_span, :] = jnp.where(first, logs[0], logs[1])
        return carry

    lax.fori_loop(0, blocks, query_block, 0)
    o_own[...] = out_s[pl.ds(own, rows), :]
    o_out[...] = out_s[pl.ds(other, rows), :]


def attend_forward(own, received, position, labels, labels_wide, labels_row):
    rows = own.shape[0]
    length = 2 * rows
    smem = pl.BlockSpec(memory_space=pltpu.SMEM)
    vmem = pl.BlockSpec(memory_space=pltpu.VMEM)
    return pl.pallas_call(
        forward_kernel,
        in_specs=[smem, smem] + [vmem] * 4,
        out_specs=[vmem] * 3,
        scratch_shapes=[
            pltpu.VMEM((2, length, 2 * LANES), BF),
            pltpu.VMEM((2, length, 2 * LANES), BF),
            pltpu.VMEM((2, length, LANES), BF),
            pltpu.VMEM((length, LANES), F32),
        ],
        out_shape=[
            jax.ShapeDtypeStruct((rows, LANES), F32),
            jax.ShapeDtypeStruct((rows, LANES), F32),
            jax.ShapeDtypeStruct((length, LANES), F32),
        ],
        cost_estimate=pl.CostEstimate(flops=6 * 10**9, bytes_accessed=28 * rows * LANES, transcendentals=length * length),
        compiler_params=pltpu.CompilerParams(vmem_limit_bytes=32 * 1024 * 1024),
        name="attend_forward",
    )(position, labels, own, received, labels_wide, labels_row)


def backward_kernel(pos_ref, seg_ref, *refs):
    (own_ref, in_ref, o_own, o_in, g_own, g_in, lse_ref, seg_col, seg_row,
     grad_own, grad_out,
     tq, hk, tk, hv, tg, lse_t, delta_t, gq_s, gk_s, gv_s) = refs
    rows = own_ref.shape[0]
    length = 2 * rows
    own = pl.multiple_of(pos_ref[0] * rows, rows)
    other = pl.multiple_of((1 - pos_ref[0]) * rows, rows)
    half = LANES // 2
    for place, ref, o, g in ((own, own_ref, o_own, g_own), (other, in_ref, o_in, g_in)):
        span = pl.ds(place, rows)
        q, k, v = (ref.at[:, i * LANES:(i + 1) * LANES] for i in range(3))
        for head, tile in enumerate(pair_tiles(q[...] * 0.125)):
            tq[head, span, :] = jnp.concatenate([tile, tile], axis=1)
        for head, tile in enumerate(pair_tiles(g[...])):
            tg[head, span, :] = jnp.concatenate([tile, tile], axis=1)
        for head, tile in enumerate(spread_tiles(k[...])):
            hk[head, span, :] = tile
        for head, tile in enumerate(spread_tiles(v[...])):
            hv[head, span, :] = tile
        for head, tile in enumerate(pair_tiles(k[...])):
            tk[head, span, :] = tile
        turned = jnp.transpose(o[...] * g[...])
        for head in range(2):
            delta_t[head, 0:1, span] = jnp.sum(turned[head * half:(head + 1) * half], axis=0, keepdims=True)
    turned = jnp.transpose(lse_ref[...])
    for head in range(2):
        lse_t[head, 0:1, :] = turned[head * half:head * half + 1]
    blocks = length // BLOCK
    first = low_lanes(BLOCK)
    gq_s[...] = jnp.zeros_like(gq_s)

    def key_block(j, carry):
        k_span = pl.ds(pl.multiple_of(j * BLOCK, BLOCK), BLOCK)
        last_label = seg_ref[j * BLOCK + BLOCK - 1]
        count = jnp.int32(1)
        for i in range(blocks):
            count = count + jnp.where((i > j) & (seg_ref[i * BLOCK] <= last_label), 1, 0)
        label = seg_col[k_span, :1]
        k_place = j * BLOCK + lax.broadcasted_iota(jnp.int32, (BLOCK, BLOCK), 0)

        def query_block(step, state):
            i = j + step
            q_span = pl.ds(pl.multiple_of(i * BLOCK, BLOCK), BLOCK)
            q_place = i * BLOCK + lax.broadcasted_iota(jnp.int32, (BLOCK, BLOCK), 1)
            allowed = (label == seg_row[i]) & (k_place <= q_place)
            new_state = []
            for head in range(2):
                grad_k, grad_v = state[head]
                query = tq[head, q_span, :]
                grad = tg[head, q_span, :]
                scores = nt(hk[head, k_span, :], query)
                weight = jnp.exp(jnp.where(allowed, scores - lse_t[head, 0:1, q_span], -1e30))
                grad_weight = nt(hv[head, k_span, :], grad)
                grad_score = weight * (grad_weight - delta_t[head, 0:1, q_span])
                w_high, w_low = split_bf(weight)
                s_high, s_low = split_bf(grad_score)
                grad_v = grad_v + nn(w_high, grad[:, :LANES]) + nn(w_low, grad[:, :LANES])
                grad_k = grad_k + nn(s_high, query[:, :LANES]) + nn(s_low, query[:, :LANES])
                keys = tk[head, k_span, :]
                gq_s[head, q_span, :] += tn(s_high, keys) + tn(s_low, keys)
                new_state.append((grad_k, grad_v))
            return tuple(new_state)

        zero = jnp.zeros((BLOCK, LANES), F32)
        state = lax.fori_loop(0, count, query_block, ((zero, zero), (zero, zero)))
        for slot, store in ((0, gk_s), (1, gv_s)):
            left, right = state[0][slot], state[1][slot]
            store[k_span, :] = jnp.where(first, left + roll_half(left), right + roll_half(right))
        return carry

    lax.fori_loop(0, blocks, key_block, 0)
    wide = low_lanes(rows)
    for place, ref in ((own, grad_own), (other, grad_out)):
        span = pl.ds(place, rows)
        left, right = gq_s[0, span, :], gq_s[1, span, :]
        ref[:, :LANES] = jnp.where(wide, left + roll_half(left), right + roll_half(right)) * 0.125
        ref[:, LANES:2 * LANES] = gk_s[span, :]
        ref[:, 2 * LANES:] = gv_s[span, :]


def attend_backward(own, received, out_own, out_in, grad_own, grad_in, logs, position, labels, labels_wide, labels_row):
    rows = own.shape[0]
    length = 2 * rows
    smem = pl.BlockSpec(memory_space=pltpu.SMEM)
    vmem = pl.BlockSpec(memory_space=pltpu.VMEM)
    return pl.pallas_call(
        backward_kernel,
        in_specs=[smem, smem] + [vmem] * 9,
        out_specs=[vmem] * 2,
        scratch_shapes=[
            pltpu.VMEM((2, length, 2 * LANES), BF),
            pltpu.VMEM((2, length, 2 * LANES), BF),
            pltpu.VMEM((2, length, LANES), BF),
            pltpu.VMEM((2, length, 2 * LANES), BF),
            pltpu.VMEM((2, length, 2 * LANES), BF),
            pltpu.VMEM((2, 8, length), F32),
            pltpu.VMEM((2, 8, length), F32),
            pltpu.VMEM((2, length, LANES), F32),
            pltpu.VMEM((length, LANES), F32),
            pltpu.VMEM((length, LANES), F32),
        ],
        out_shape=[jax.ShapeDtypeStruct((rows, 3 * LANES), F32)] * 2,
        cost_estimate=pl.CostEstimate(flops=13 * 10**9, bytes_accessed=60 * rows * LANES, transcendentals=length * length),
        compiler_params=pltpu.CompilerParams(vmem_limit_bytes=40 * 1024 * 1024),
        name="attend_backward",
    )(position, labels, own, received, out_own, out_in, grad_own, grad_in, logs, labels_wide, labels_row)


MESH = pl.DeviceIdType.MESH
PIECE = 48
FLAT_PAIRS = 2


def back_kernel(plan, *refs):
    up_units, out_units, qkv_units, in_units = plan
    units = sum(plan)
    pairs = units // 2
    first_qkv = up_units + out_units
    first_in = first_qkv + qkv_units
    (up_turned, out_turned, qkv_turned, in_turned, grad_pre, grad_resid, mine_0, mine_1, mine_2, got_0, sent_1, sent_2,
     qkv_ref, stream_ref, weight_ref, vectors_ref, sums_ref,
     up_total, out_total, qkv_total, in_total, patch_ref, norm_total_ref, got_1, got_2,
     t_buf, g_buf, g_high, g_low, part, s_high, s_low, w_buf, p_buf, q_buf, acc, land_a, n_x, n_z, n_y, y_y, y_x, y_z, done,
     v_own, v_c, v_x, v_y, v_z,
     load_sem, w_sem, p_sem, q_sem, norm_sem, swap_sem,
     a_sem, nx_sem, nz_sem, ny_sem, yy_sem, yx_sem, yz_sem, ye_sem, v_sem, o_sem) = refs
    mine, got = (mine_0, mine_1, mine_2), (got_0, got_1, got_2)
    width = g_buf.shape[2]
    fsdp = lax.axis_index("fsdp")
    row = lax.axis_index("sp")
    z, x, core = fsdp // 4, (fsdp // 2) % 2, fsdp % 2
    half = PIECE // 2

    def device(z_at, x_at, core_at, row_at):
        return ((z_at * 2 + x_at) * 2 + core_at, row_at)

    sibling = device(z, x, 1 - core, row)
    beside = device(z, 1 - x, core, row)
    across = device(z, x, core, 1 - row)
    along = [device((z + step) % 4, x, core, row) for step in (1, 2, 3)]

    barrier = pltpu.get_barrier_semaphore()
    for peer in [sibling, beside, across] + along:
        pl.semaphore_signal(barrier, inc=1, device_id=peer, device_id_type=MESH)

    def remote(source, target, sems, index, peer):
        return pltpu.make_async_remote_copy(
            src_ref=source, dst_ref=target, send_sem=sems.at[(0,) + index], recv_sem=sems.at[(1,) + index],
            device_id=peer, device_id_type=MESH,
        )

    def span(first, size):
        return pl.ds(pl.multiple_of(first, size), size)

    def loop(number, body):
        def step(i, carry):
            body(i)
            return carry

        lax.fori_loop(0, number, step, 0)

    def start(copy):
        copy.start()

    def wait(copy):
        copy.wait()

    def loads(unit, slot, act):
        def left(view):
            for side in range(2):
                act(pltpu.make_async_copy(view.at[:, side], t_buf.at[slot, side], load_sem.at[slot, side]))

        def right(source):
            act(pltpu.make_async_copy(source, g_buf.at[slot], load_sem.at[slot, 2]))

        @pl.when(unit < up_units)
        def _():
            left(up_turned)
            right(grad_pre.at[:, span(unit * width, width)])

        @pl.when((unit >= up_units) & (unit < first_qkv))
        def _():
            left(out_turned)
            right(grad_resid.at[:, span((unit - up_units) * width, width)])

        @pl.when((unit >= first_qkv) & (unit < first_in))
        def _():
            left(qkv_turned)
            for j in range(qkv_units):
                kind, side = divmod(j, 2)
                for sources, own in ((mine, True), (got, False)):
                    @pl.when((unit == first_qkv + j) & ((row == side) == own))
                    def _(kind=kind, sources=sources):
                        for i, source in enumerate(sources):
                            act(pltpu.make_async_copy(
                                source.at[:, kind * LANES:(kind + 1) * LANES],
                                g_buf.at[slot, :, i * LANES:(i + 1) * LANES],
                                load_sem.at[slot, 2 + i],
                            ))

        @pl.when(unit >= first_in)
        def _():
            j = (unit - first_in) // 2
            for side in range(2):
                act(pltpu.make_async_copy(in_turned.at[:, side, j], t_buf.at[slot, side], load_sem.at[slot, side]))

    def weight_copy(block, slot):
        return pltpu.make_async_copy(weight_ref.at[block], w_buf.at[slot], w_sem.at[slot])

    def patch_copy(block, slot):
        columns = w_buf.shape[1]
        return pltpu.make_async_copy(p_buf.at[slot], patch_ref.at[:, span(block * columns, columns)], p_sem.at[slot])

    def q_copy(j):
        return pltpu.make_async_copy(qkv_ref.at[:, :, :, :, span(j * width, width)], q_buf, q_sem)

    rows = stream_ref.shape[0]
    cut = w_buf.shape[1]
    norm_copies = [
        pltpu.make_async_copy(stream_ref.at[:, 0:width], p_buf.at[0], norm_sem.at[0]),
        pltpu.make_async_copy(stream_ref.at[:, width:], p_buf.at[1], norm_sem.at[1]),
        pltpu.make_async_copy(grad_resid.at[0:cut], w_buf.at[0], norm_sem.at[2]),
        pltpu.make_async_copy(grad_resid.at[cut:], w_buf.at[1, 0:rows - cut], norm_sem.at[3]),
    ]
    swap_copies = [
        remote(sent_1, got_1, swap_sem, (0,), across),
        remote(sent_2, got_2, swap_sem, (1,), across),
    ]

    def core_copy(unit, slot):
        return remote(part.at[slot, 1 - core], land_a.at[unit], a_sem, (unit,), sibling)

    def nx_copy(unit, n):
        return remote(land_a.at[unit, :, 1 - x], n_x.at[n], nx_sem, (n,), beside)

    def nz_copy(n, step):
        return remote(n_x.at[n, (z + step + 1) % 4], n_z.at[n, step], nz_sem, (n, step), along[step])

    def ny_copy(n):
        return remote(n_x.at[n, z], n_y.at[n], ny_sem, (n,), across)

    def yy_copy(unit, p):
        return remote(land_a.at[unit, :, :, span((1 - row) * half, half)], y_y.at[p], yy_sem, (p,), across)

    def yx_copy(p):
        return remote(y_y.at[p, :, 1 - x], y_x.at[p], yx_sem, (p,), beside)

    def yz_copy(p, step):
        return remote(y_x.at[p, (z + step + 1) % 4], y_z.at[p, step], yz_sem, (p, step), along[step])

    def ye_copy(unit, p):
        return remote(y_x.at[p, z], done.at[unit, span(row * half, half)], ye_sem, (p,), across)

    def flat_number(pair):
        return pairs + pair

    def other_number(pair):
        return pair - FLAT_PAIRS

    def odd(pair, flat, other):
        @pl.when(pair < FLAT_PAIRS)
        def _():
            flat(2 * pair + 1, flat_number(pair))

        @pl.when(pair >= FLAT_PAIRS)
        def _():
            other(2 * pair + 1, other_number(pair))

    v_copies = [
        remote(v_own, v_c, v_sem, (0,), sibling),
        remote(v_c, v_x, v_sem, (1,), beside),
        remote(v_x, v_y, v_sem, (2,), across),
    ] + [remote(v_y, v_z.at[step], v_sem, (3 + step,), along[step]) for step in range(3)]

    loads(jnp.int32(0), 0, start)
    q_copy(0).start()
    for copy in norm_copies:
        copy.start()
    pl.semaphore_wait(barrier, 6)
    for copy in swap_copies:
        copy.start()

    def norm_backward():
        for copy in norm_copies:
            copy.wait()
        values = jnp.concatenate([p_buf[0], p_buf[1]], axis=1)
        back, gain, offset = norm_back(acc[...], values, vectors_ref[0:1, :])
        v_own[...] = sums_ref[...]
        v_own[0:1, :] = gain
        v_own[1:2, :] = offset
        acc[...] = back
        acc[0:cut, :] = acc[0:cut, :] + w_buf[0]
        acc[cut:, :] = acc[cut:, :] + w_buf[1, 0:rows - cut]
        s_high[...] = acc[...].astype(BF)
        s_low[...] = (acc[...] - s_high[...].astype(F32)).astype(BF)
        weight_copy(0, 0).start()
        v_copies[0].start()

    def compute(unit, slot):
        loads(unit, slot, wait)

        @pl.when(unit + 1 < units)
        def _():
            loads(unit + 1, 1 - slot, start)

        @pl.when(unit >= 2)
        def _():
            core_copy(unit - 2, slot).wait_send()

        @pl.when(unit < first_in)
        def _():
            grad = g_buf[slot]
            g_high[...] = grad.astype(BF)
            g_low[...] = (grad - g_high[...].astype(F32)).astype(BF)

        @pl.when(unit >= first_in)
        def _():
            columns = span(((unit - first_in) % 2) * width, width)
            g_high[...] = s_high[:, columns]
            g_low[...] = s_low[:, columns]

        def side_of(turn, carry):
            side = jnp.where(turn == 0, 1 - core, core)
            high, low = split_bf(t_buf[slot, side].reshape(8 * PIECE, t_buf.shape[4]))
            product = nn(high, g_high[...]) + nn(high, g_low[...]) + nn(low, g_high[...])
            part[slot, side] = product.reshape(4, 2, PIECE, product.shape[1])

            @pl.when(turn == 0)
            def _():
                core_copy(unit, slot).start()

            return carry

        lax.fori_loop(0, 2, side_of, 0)

        @pl.when((unit >= first_qkv) & (unit < first_in))
        def _():
            j = unit - first_qkv
            q_copy(j).wait()
            weight = split_bf(q_buf[...].reshape(acc.shape[1], width))
            acc[...] = acc[...] + three(nt, (g_high[...], g_low[...]), weight)

            @pl.when(j + 1 < qkv_units)
            def _():
                q_copy(j + 1).start()

    def patch_block(block, slot):
        weight_copy(block, slot).wait()

        @pl.when(block + 1 < weight_ref.shape[0])
        def _():
            weight_copy(block + 1, 1 - slot).start()

        @pl.when(block >= 2)
        def _():
            patch_copy(block - 2, slot).wait()

        p_buf[slot] = three(nt, (s_high[...], s_low[...]), split_bf(w_buf[slot]))
        patch_copy(block, slot).start()

    def after_core(unit, slot):
        core_copy(unit, slot).wait_recv()

        def add(i):
            for b in range(2):
                land_a[unit, i, b] = land_a[unit, i, b] + part[slot, core, i, b]

        loop(4, add)

    def flat_x(unit, n):
        nx_copy(unit, n).wait_recv()

        def add(i):
            n_x[n, i] = n_x[n, i] + land_a[unit, i, x]

        loop(4, add)
        for step in range(3):
            nz_copy(n, step).start()

    def flat_z(unit, n):
        for step in range(3):
            nz_copy(n, step).wait_recv()
        n_x[n, z] = n_x[n, z] + n_z[n, 0] + n_z[n, 1] + n_z[n, 2]
        ny_copy(n).start()

    def flat_y(unit, n):
        ny_copy(n).wait_recv()
        done[unit] = n_x[n, z] + n_y[n]

    def other_y(unit, p):
        yy_copy(unit, p).wait_recv()
        own = span(row * half, half)

        def add(i):
            for b in range(2):
                y_y[p, i, b] = y_y[p, i, b] + land_a[unit, i, b, own]

        loop(4, add)
        yx_copy(p).start()

    def other_x(unit, p):
        yx_copy(p).wait_recv()

        def add(i):
            y_x[p, i] = y_x[p, i] + y_y[p, i, x]

        loop(4, add)
        for step in range(3):
            yz_copy(p, step).start()

    def other_z(unit, p):
        for step in range(3):
            yz_copy(p, step).wait_recv()
        total = y_x[p, z] + y_z[p, 0] + y_z[p, 1] + y_z[p, 2]
        y_x[p, z] = total
        done[unit, span(row * half, half)] = total
        ye_copy(unit, p).start()

    acc[...] = jnp.zeros_like(acc)

    def iteration(p, carry):
        @pl.when(p == first_qkv // 2 - 1)
        def _():
            for copy in swap_copies:
                copy.wait_recv()

        @pl.when(p < pairs)
        def _():
            compute(2 * p, 0)
            compute(2 * p + 1, 1)
            after_core(2 * p, 0)
            nx_copy(2 * p, p).start()
            after_core(2 * p + 1, 1)
            odd(p, lambda unit, n: nx_copy(unit, n).start(), lambda unit, i: yy_copy(unit, i).start())

        @pl.when(p == first_in // 2 - 1)
        def _():
            norm_backward()

        q = p - 1

        @pl.when((q >= 0) & (q < pairs))
        def _():
            flat_x(2 * q, q)
            odd(q, flat_x, other_y)

        @pl.when((p >= first_in // 2) & (p < pairs))
        def _():
            patch_block(2 * p - first_in, 0)
            patch_block(2 * p - first_in + 1, 1)

        r = p - 2

        @pl.when((r >= 0) & (r < pairs))
        def _():
            flat_z(2 * r, r)
            odd(r, flat_z, other_x)

        s = p - 3

        @pl.when((s >= 0) & (s < pairs))
        def _():
            flat_y(2 * s, s)
            odd(s, flat_y, other_z)

        turn = p - first_in // 2

        @pl.when(turn == 0)
        def _():
            v_copies[0].wait_recv()
            v_c[...] = v_c[...] + v_own[...]
            v_copies[1].start()

        @pl.when(turn == 1)
        def _():
            v_copies[1].wait_recv()
            v_x[...] = v_x[...] + v_c[...]
            v_copies[2].start()

        @pl.when(turn == 2)
        def _():
            v_copies[2].wait_recv()
            v_y[...] = v_y[...] + v_x[...]
            for step in range(3):
                v_copies[3 + step].start()

        @pl.when(turn == 3)
        def _():
            for step in range(3):
                v_copies[3 + step].wait_recv()
            norm_total_ref[...] = v_y[...] + v_z[0] + v_z[1] + v_z[2]

        return carry

    lax.fori_loop(0, pairs + 3, iteration, 0)

    def flat_end(unit, n):
        nx_copy(unit, n).wait_send()
        ny_copy(n).wait_send()
        for step in range(3):
            nz_copy(n, step).wait_send()

    def other_end(unit, p):
        ye_copy(unit, p).wait()
        yy_copy(unit, p).wait_send()
        yx_copy(p).wait_send()
        for step in range(3):
            yz_copy(p, step).wait_send()

    def finish(p):
        flat_end(2 * p, p)
        odd(p, flat_end, other_end)

    loop(pairs, finish)

    def out_copy(unit, act):
        @pl.when(unit < up_units)
        def _():
            act(pltpu.make_async_copy(done.at[unit], up_total.at[:, span(unit * width, width)], o_sem.at[unit]))

        @pl.when((unit >= up_units) & (unit < first_qkv))
        def _():
            act(pltpu.make_async_copy(done.at[unit], out_total.at[:, span((unit - up_units) * width, width)], o_sem.at[unit]))

        @pl.when((unit >= first_qkv) & (unit < first_in))
        def _():
            act(pltpu.make_async_copy(done.at[unit], qkv_total.at[:, span((unit - first_qkv) * width, width)], o_sem.at[unit]))

        @pl.when(unit >= first_in)
        def _():
            j = unit - first_in
            act(pltpu.make_async_copy(
                done.at[unit], in_total.at[span((j // 2) * PIECE, PIECE), span((j % 2) * width, width)], o_sem.at[unit]
            ))

    loop(units, lambda unit: out_copy(unit, start))
    for copy in v_copies + swap_copies:
        copy.wait_send()
    core_copy(units - 2, 0).wait_send()
    core_copy(units - 1, 1).wait_send()
    blocks = weight_ref.shape[0]
    patch_copy(blocks - 2, 0).wait()
    patch_copy(blocks - 1, 1).wait()
    loop(units, lambda unit: out_copy(unit, wait))


def back_and_reduce(turned, grad_pre, grad_resid, mine, got, sent, qkv_full, stream, weights, vectors, sums):
    rows, full = stream.shape
    width = full // 2
    owners, block, _ = weights.shape
    piece = full // owners
    columns = [grad_pre.shape[1], full, qkv_full.shape[4], full]
    plan = [c // width for c in columns]
    plan[3] *= block // piece
    views = [left.reshape(8, 2, piece, rows) for left in turned[:3]] + [turned[3].reshape(8, 2, block // piece, piece, rows)]
    units = sum(plan)
    pairs = units // 2
    flats, others = pairs + FLAT_PAIRS, pairs - FLAT_PAIRS
    assert piece == PIECE and plan[3] == owners and (plan[0] + plan[1]) % 2 == 0 and plan[2] == 6
    half = PIECE // 2
    dma = pltpu.SemaphoreType.DMA
    any_space = pl.BlockSpec(memory_space=pl.ANY)
    vmem = pl.BlockSpec(memory_space=pltpu.VMEM)

    def array(*shape):
        return jax.ShapeDtypeStruct(shape, F32)

    return pl.pallas_call(
        functools.partial(back_kernel, tuple(plan)),
        out_shape=[
            array(piece, columns[0]), array(piece, full), array(piece, columns[2]), array(block, full),
            array(rows, owners * block), array(*vectors.shape), array(*got.shape), array(*got.shape),
        ],
        in_specs=[any_space] * 15 + [vmem, vmem],
        out_specs=[any_space] * 5 + [vmem, any_space, any_space],
        scratch_shapes=[
            pltpu.VMEM((2, 2, 8, PIECE, rows), F32),
            pltpu.VMEM((2, rows, width), F32),
            pltpu.VMEM((rows, width), BF),
            pltpu.VMEM((rows, width), BF),
            pltpu.VMEM((2, 2, 4, 2, PIECE, width), F32),
            pltpu.VMEM((rows, full), BF),
            pltpu.VMEM((rows, full), BF),
            pltpu.VMEM((2, block, full), F32),
            pltpu.VMEM((2, rows, block), F32),
            pltpu.VMEM((4, 2, 2, PIECE, width), F32),
            pltpu.VMEM((rows, full), F32),
            pltpu.VMEM((units, 4, 2, PIECE, width), F32),
            pltpu.VMEM((flats, 4, PIECE, width), F32),
            pltpu.VMEM((flats, 3, PIECE, width), F32),
            pltpu.VMEM((flats, PIECE, width), F32),
            pltpu.VMEM((others, 4, 2, half, width), F32),
            pltpu.VMEM((others, 4, half, width), F32),
            pltpu.VMEM((others, 3, half, width), F32),
            pltpu.VMEM((units, PIECE, width), F32),
            pltpu.VMEM(vectors.shape, F32),
            pltpu.VMEM(vectors.shape, F32),
            pltpu.VMEM(vectors.shape, F32),
            pltpu.VMEM(vectors.shape, F32),
            pltpu.VMEM((3,) + vectors.shape, F32),
            dma((2, 5)), dma((2,)), dma((2,)), dma, dma((4,)), dma((2, 2)),
            dma((2, units)), dma((2, flats)), dma((2, flats, 3)), dma((2, flats)),
            dma((2, others)), dma((2, others)), dma((2, others, 3)), dma((2, others)),
            dma((2, 6)), dma((units,)),
        ],
        cost_estimate=pl.CostEstimate(
            flops=6 * rows * full * (units * 8 * PIECE + owners * block), bytes_accessed=130 * 10**6, transcendentals=0
        ),
        compiler_params=pltpu.CompilerParams(
            collective_id=0, has_side_effects=True, vmem_limit_bytes=67043328
        ),
        name="back_and_reduce",
    )(*views, grad_pre, grad_resid, *mine, got, *sent, qkv_full, stream, weights, vectors, sums)[:6]


CUT_ROWS = 128
CUT_COLUMNS = 128
NARROW = 384


def three(product, left, right):
    return product(left[0], right[0]) + product(left[0], right[1]) + product(left[1], right[0])


def normalized(values):
    average = jnp.mean(values, axis=-1, keepdims=True)
    centred = values - average
    spread = jnp.mean(centred * centred, axis=-1, keepdims=True)
    scale = lax.rsqrt(spread + EPSILON)
    return centred * scale, scale


def gather_kernel(patch_ref, in_ref, qkv_ref, out_ref, vector_ref,
                  stream_ref, normed_ref, turned_ref, patch_turned_ref, in_full, qkv_full, out_full, vectors_ref,
                  sent_0, sent_1, sent_2,
                  patch_buf, in_buf, qkv_buf, out_buf, turn_buf, acc, v_c, v_x, v_z, sent_buf,
                  z_sem, x_sem, y_sem, c_sem, v_sem, own_sem, patch_sem, turn_sem, full_sem, last_sem):
    fsdp = lax.axis_index("fsdp")
    row = lax.axis_index("sp")
    z, x, core = fsdp // 4, (fsdp // 2) % 2, fsdp % 2
    block, width = in_ref.shape
    across_count = width // CUT_COLUMNS
    in_units = (block // CUT_ROWS) * across_count
    narrow = NARROW
    out_units = width // narrow
    units = in_units + qkv_ref.shape[1] // narrow + out_units

    def device(z_at, x_at, core_at, row_at):
        return ((z_at * 2 + x_at) * 2 + core_at, row_at)

    sibling = device(z, x, 1 - core, row)
    beside = device(z, 1 - x, core, row)
    across = device(z, x, core, 1 - row)
    along = [device((z + step) % 4, x, core, row) for step in (1, 2, 3)]
    barrier = pltpu.get_barrier_semaphore()
    for peer in [sibling, beside, across] + along:
        pl.semaphore_signal(barrier, inc=1, device_id=peer, device_id_type=MESH)

    def remote(source, target, sems, index, peer):
        return pltpu.make_async_remote_copy(
            src_ref=source, dst_ref=target, send_sem=sems.at[(0,) + index], recv_sem=sems.at[(1,) + index],
            device_id=peer, device_id_type=MESH,
        )

    patch_copy = pltpu.make_async_copy(patch_ref, patch_buf, patch_sem)

    def span(first, size, step=None):
        return pl.ds(pl.multiple_of(first, step or size), size)

    def places(kind, unit, part):
        if kind == "in":
            j, column = unit // across_count, unit % across_count
            columns = span(column * CUT_COLUMNS, CUT_COLUMNS)
            base, rows, edge = j * CUT_ROWS, CUT_ROWS, 40
        else:
            rows, edge = out_ref.shape[0], 16
            first = in_units if kind == "qkv" else units - out_units
            base, columns = 0, span((unit - first) * narrow, narrow)
        if part is None:
            return span(base, rows, 8), columns
        which, side = part
        if which == 0:
            return span(base + side * (rows - edge), edge, 8), columns
        return span(base + side * edge, rows - edge, 8), columns

    sources = {"in": (in_ref, in_buf), "qkv": (qkv_ref, qkv_buf), "out": (out_ref, out_buf)}

    def each_kind(unit, act):
        ranges = (("in", 0, in_units), ("qkv", in_units, units - out_units), ("out", units - out_units, units))
        for kind, first, last in ranges:
            @pl.when((unit >= first) & (unit < last))
            def _(kind=kind):
                act(kind)

    own_copies = []
    for kind, firsts in (("in", range(0, block, CUT_ROWS)), ("qkv", (0,)), ("out", (0,))):
        source, buf = sources[kind]
        for first in firsts:
            rows = places(kind, first // CUT_ROWS * across_count if kind == "in" else in_units, (1, row))[0]
            own_copies.append(
                pltpu.make_async_copy(source.at[rows], buf.at[z, x, core, rows], own_sem.at[len(own_copies)])
            )

    def z_copy(kind, unit, step):
        source, buf = sources[kind]
        at = places(kind, unit, (1, row))
        return remote(source.at[at], buf.at[(z, x, core) + at], z_sem, (unit, step), along[step])

    def x_copy(kind, unit):
        ref = sources[kind][1].at[(slice(None), x, core) + places(kind, unit, (1, row))]
        return remote(ref, ref, x_sem, (unit,), beside)

    def y_copy(kind, unit):
        ref = sources[kind][1].at[(slice(None), slice(None), core) + places(kind, unit, (0, row))]
        return remote(ref, ref, y_sem, (unit,), across)

    def c_copy(kind, unit, index):
        part = (1, row) if index == 0 else (0, 1 - row)
        ref = sources[kind][1].at[(slice(None), slice(None), core) + places(kind, unit, part)]
        return remote(ref, ref, c_sem, (unit, index), sibling)

    def z_stage(unit):
        def act(kind):
            for step in range(3):
                z_copy(kind, unit, step).start()

        each_kind(unit, act)

    def x_stage(unit):
        def act(kind):
            for step in range(3):
                z_copy(kind, unit, step).wait_recv()
            x_copy(kind, unit).start()

        each_kind(unit, act)

    def spread_stage(unit):
        def act(kind):
            x_copy(kind, unit).wait_recv()
            y_copy(kind, unit).start()
            c_copy(kind, unit, 0).start()

        each_kind(unit, act)

    def y_stage(unit):
        def act(kind):
            y_copy(kind, unit).wait_recv()
            c_copy(kind, unit, 1).start()

        each_kind(unit, act)

    def ready(unit):
        def act(kind):
            c_copy(kind, unit, 0).wait_recv()
            c_copy(kind, unit, 1).wait_recv()
            full_copy(kind, unit).start()

        each_kind(unit, act)

    def full_copy(kind, unit):
        at = (slice(None), slice(None), slice(None)) + places(kind, unit, None)
        full = {"in": in_full, "qkv": qkv_full, "out": out_full}[kind]
        return pltpu.make_async_copy(sources[kind][1].at[at], full.at[at], full_sem.at[unit])

    def multiply(unit):
        j, column = unit // across_count, unit % across_count
        columns = span(column * CUT_COLUMNS, CUT_COLUMNS)
        rows = span(j * CUT_ROWS, CUT_ROWS)

        def step(pair, carry):
            first = pair * 2 * block + j * CUT_ROWS
            left = jnp.concatenate(
                [patch_buf[:, span(first, CUT_ROWS)], patch_buf[:, span(first + block, CUT_ROWS)]], axis=1
            )
            right = in_buf[pair // 2, pair % 2, :, rows, columns].reshape(2 * CUT_ROWS, CUT_COLUMNS)
            acc[:, columns] = acc[:, columns] + three(nn, split_bf(left), split_bf(right))
            return carry

        lax.fori_loop(0, 8, step, 0)

    tiles = patch_ref.shape[1] // LANES
    each = turn_buf.shape[0]

    def turn_copy(tile, slot):
        return pltpu.make_async_copy(turn_buf.at[slot], patch_turned_ref.at[span(tile * LANES, LANES)], turn_sem.at[slot])

    def turn(group):
        for slot in range(each):
            @pl.when(group > 0)
            def _(slot=slot):
                turn_copy((group - 1) * each + slot, slot).wait()

            turn_buf[slot] = jnp.transpose(patch_buf[:, span((group * each + slot) * LANES, LANES)])
            turn_copy(group * each + slot, slot).start()

    pl.semaphore_wait(barrier, 6)
    z_stage(jnp.int32(0))
    z_stage(jnp.int32(1))
    for copy in own_copies:
        copy.start()
    patch_copy.start()
    v_copies = [
        remote(vector_ref, v_c, v_sem, (0,), sibling),
        remote(v_c, v_x, v_sem, (1,), beside),
    ] + [remote(v_x, v_z.at[step], v_sem, (2 + step,), along[step]) for step in range(3)]
    v_copies[0].start()
    acc[...] = jnp.zeros_like(acc)
    for copy in own_copies:
        copy.wait()

    def iteration(t, carry):
        z_stage(t + 2)
        x_stage(t)
        spread_stage(t - 2)
        y_stage(t - 4)

        @pl.when(t == 0)
        def _():
            patch_copy.wait()
            v_copies[0].wait_recv()
            v_c[...] = v_c[...] + vector_ref[...]
            v_copies[1].start()

        @pl.when(t == 1)
        def _():
            v_copies[1].wait_recv()
            v_x[...] = v_x[...] + v_c[...]
            for step in range(3):
                v_copies[2 + step].start()

        @pl.when(t == 2)
        def _():
            for step in range(3):
                v_copies[2 + step].wait_recv()
            vectors_ref[...] = v_x[...] + v_z[0] + v_z[1] + v_z[2]

        @pl.when(t < tiles // each)
        def _():
            turn(t)

        ready(t - 5)

        @pl.when((t >= 5) & (t < in_units + 5))
        def _():
            multiply(t - 5)

        @pl.when(t == in_units + 5)
        def _():
            stream = acc[...]
            stream_ref[...] = stream
            zhat, _ = normalized(stream)
            acc[...] = zhat * vectors_ref[0:1, :] + vectors_ref[1:2, :]
            normed_ref[...] = acc[...]
            turned_ref[...] = jnp.transpose(acc[...])

        return carry

    lax.fori_loop(0, units + 5, iteration, 0)
    left = split_bf(acc[...])
    last = []
    for group, ref in enumerate((sent_0, sent_1, sent_2)):
        right = jnp.concatenate(
            [
                qkv_buf[:, :, :, :, span(which * width + (1 - row) * (width // 2) + group * LANES, LANES)].reshape(width, LANES)
                for which in range(3)
            ],
            axis=1,
        )
        sent_buf[group] = three(nn, left, split_bf(right))
        copy = pltpu.make_async_copy(sent_buf.at[group], ref, last_sem.at[group])
        copy.start()
        last.append(copy)

    def finish(unit, carry):
        def act(kind):
            for step in range(3):
                z_copy(kind, unit, step).wait_send()
            x_copy(kind, unit).wait_send()
            y_copy(kind, unit).wait_send()
            c_copy(kind, unit, 0).wait_send()
            c_copy(kind, unit, 1).wait_send()
            full_copy(kind, unit).wait()

        each_kind(unit, act)
        return carry

    lax.fori_loop(0, units, finish, 0)
    for copy in v_copies:
        copy.wait_send()
    for slot in range(each):
        turn_copy(tiles - each + slot, slot).wait()
    for copy in last:
        copy.wait()


def gather_stream(patch_rows, w_in, w_qkv, w_out, vectors):
    rows, patch_width = patch_rows.shape
    block, width = w_in.shape
    piece, columns = w_qkv.shape
    group = columns // 6
    any_space = pl.BlockSpec(memory_space=pl.ANY)
    vmem = pl.BlockSpec(memory_space=pltpu.VMEM)
    dma = pltpu.SemaphoreType.DMA
    units = (block // CUT_ROWS) * (width // CUT_COLUMNS) + (columns + width) // NARROW
    owners = (4, 2, 2)

    def array(*shape):
        return jax.ShapeDtypeStruct(shape, F32)

    return pl.pallas_call(
        gather_kernel,
        out_shape=[
            array(rows, width), array(rows, width), array(width, rows), array(patch_width, rows),
            array(*owners, block, width), array(*owners, piece, columns), array(*owners, piece, width),
            array(*vectors.shape), array(rows, group), array(rows, group), array(rows, group),
        ],
        in_specs=[any_space] * 4 + [vmem],
        out_specs=[vmem, vmem, vmem] + [any_space] * 4 + [vmem] + [any_space] * 3,
        scratch_shapes=[
            pltpu.VMEM((rows, patch_width), F32),
            pltpu.VMEM(owners + (block, width), F32),
            pltpu.VMEM(owners + (piece, columns), F32),
            pltpu.VMEM(owners + (piece, width), F32),
            pltpu.VMEM((4, LANES, rows), F32),
            pltpu.VMEM((rows, width), F32),
            pltpu.VMEM(vectors.shape, F32),
            pltpu.VMEM(vectors.shape, F32),
            pltpu.VMEM((3,) + vectors.shape, F32),
            pltpu.VMEM((3, rows, group), F32),
            dma((2, units, 3)), dma((2, units)), dma((2, units)), dma((2, units, 2)), dma((2, 5)),
            dma((block // CUT_ROWS + 2,)), dma, dma((4,)), dma((units,)), dma((3,)),
        ],
        cost_estimate=pl.CostEstimate(flops=6 * rows * patch_width * width, bytes_accessed=90 * 10**6, transcendentals=0),
        compiler_params=pltpu.CompilerParams(collective_id=1, has_side_effects=True, vmem_limit_bytes=67043328),
        name="gather_stream",
    )(patch_rows, w_in, w_qkv, w_out, vectors)


def own_kernel(pos_ref, normed_ref, q_ref, k_ref, v_ref, *outs):
    step = pl.program_id(0)
    weight = jnp.concatenate([ref[...].reshape(normed_ref.shape[1], LANES) for ref in (q_ref, k_ref, v_ref)], axis=1)
    product = three(nn, split_bf(normed_ref[...]), split_bf(weight))
    for i, ref in enumerate(outs):
        @pl.when(step == i)
        def _(ref=ref):
            ref[...] = product


def project_own(position, normed, qkv_full):
    rows, width = normed.shape
    owners, columns = qkv_full.shape[:4], qkv_full.shape[4]
    group = columns // 6
    return pl.pallas_call(
        own_kernel,
        grid_spec=pltpu.PrefetchScalarGridSpec(
            num_scalar_prefetch=1,
            grid=(3,),
            in_specs=[
                pl.BlockSpec((rows, width), lambda g, pos: (0, 0)),
                pl.BlockSpec(owners + (LANES,), lambda g, pos: (0, 0, 0, 0, pos[0] * 3 + g)),
                pl.BlockSpec(owners + (LANES,), lambda g, pos: (0, 0, 0, 0, 6 + pos[0] * 3 + g)),
                pl.BlockSpec(owners + (LANES,), lambda g, pos: (0, 0, 0, 0, 12 + pos[0] * 3 + g)),
            ],
            out_specs=[pl.BlockSpec((rows, group), lambda g, pos: (0, 0))] * 3,
        ),
        out_shape=[jax.ShapeDtypeStruct((rows, group), F32)] * 3,
        cost_estimate=pl.CostEstimate(flops=3 * rows * width * columns, bytes_accessed=8 * 10**6, transcendentals=0),
        compiler_params=pltpu.CompilerParams(vmem_limit_bytes=40 * 1024 * 1024),
        name="project_own",
    )(position, normed, qkv_full, qkv_full, qkv_full)


def gelu_and_slope(values):
    root = 0.7978845608028654
    square = values * values
    bent = jnp.tanh(root * (values + 0.044715 * values * square))
    half = 0.5 + 0.5 * bent
    slope = half + 0.5 * values * (1.0 - bent * bent) * (root * (1.0 + 0.134145 * square))
    return values * half, slope


def norm_back(grad, values, gain):
    zhat, scale = normalized(values)
    scaled = grad * gain
    back = scale * (
        scaled - jnp.mean(scaled, axis=-1, keepdims=True) - zhat * jnp.mean(scaled * zhat, axis=-1, keepdims=True)
    )
    return back, jnp.sum(grad * zhat, axis=0, keepdims=True), jnp.sum(grad, axis=0, keepdims=True)


def middle_kernel(pos_ref, *refs):
    own_parts, in_parts = refs[0:3], refs[3:6]
    (stream_ref, cot_ref, out_ref, vectors_ref, up_ref, down_ref,
     block_ref, grad_pre_ref, grad_down_ref, grad_resid_ref, turned_ref, attended_ref) = refs[6:18]
    sent_refs, own_refs, sums_ref = refs[18:21], refs[21:24], refs[24]
    residual, norm_high, norm_low, cot_high, cot_low, grad_norm = refs[25:]
    step = pl.program_id(0)
    width = out_ref.shape[0]
    half = width // 2
    own = pl.ds(pl.multiple_of(pos_ref[0] * half, half), half)
    other = pl.ds(pl.multiple_of((1 - pos_ref[0]) * half, half), half)

    @pl.when(step == 0)
    def _():
        total = stream_ref[...]
        for span, parts in ((own, own_parts), (other, in_parts)):
            left = jnp.concatenate([part[...] for part in parts], axis=1)
            attended_ref[span, :] = jnp.transpose(left)
            total = total + three(nn, split_bf(left), split_bf(out_ref[span, :]))
        residual[...] = total
        block_ref[...] = total
        zhat, _ = normalized(total)
        normed = zhat * vectors_ref[2:3, :] + vectors_ref[3:4, :]
        turned_ref[...] = jnp.transpose(normed)
        norm_high[...], norm_low[...] = split_bf(normed)
        cot_high[...], cot_low[...] = split_bf(cot_ref[...])
        grad_norm[...] = jnp.zeros_like(grad_norm)

    up = split_bf(up_ref[...].reshape(width, width))
    hidden, slope = gelu_and_slope(three(nn, (norm_high[...], norm_low[...]), up))
    down = split_bf(down_ref[...].reshape(width, width))
    cot = (cot_high[...], cot_low[...])
    grad_pre = three(nt, cot, down) * slope
    grad_pre_ref[...] = grad_pre
    parts = split_bf(hidden)
    block_ref[...] = block_ref[...] + three(nn, parts, down)
    grad_down_ref[...] = three(tn, parts, cot).reshape(grad_down_ref.shape)
    grad_norm[...] = grad_norm[...] + three(nt, split_bf(grad_pre), up)

    @pl.when(step == pl.num_programs(0) - 1)
    def _():
        back, gain, offset = norm_back(grad_norm[...], residual[...], vectors_ref[2:3, :])
        grad = cot_ref[...] + back
        grad_resid_ref[...] = grad
        sums_ref[...] = jnp.zeros_like(sums_ref)
        sums_ref[2:3, :] = gain
        sums_ref[3:4, :] = offset
        left = split_bf(grad)
        for span, outs in ((other, sent_refs), (own, own_refs)):
            product = three(nt, left, split_bf(out_ref[span, :]))
            for i, ref in enumerate(outs):
                ref[...] = product[:, i * LANES:(i + 1) * LANES]


def middle(position, out_own, out_in, stream, cotangent, w_out, vectors, weights):
    rows, width = stream.shape
    owners, stacked = weights.shape[0], weights.shape[1]
    piece = width // owners
    steps = stacked // piece // 2
    whole = lambda *shape: pl.BlockSpec(shape, lambda j, *_: (0,) * len(shape))
    array = lambda *shape: jax.ShapeDtypeStruct(shape, F32)
    head = whole(rows, LANES)
    return pl.pallas_call(
        middle_kernel,
        grid_spec=pltpu.PrefetchScalarGridSpec(
            num_scalar_prefetch=1,
            grid=(steps,),
            in_specs=[head] * 6 + [
                whole(rows, width), whole(rows, width), whole(width, width), whole(*vectors.shape),
                pl.BlockSpec((owners, piece, width), lambda j, *_: (0, j, 0)),
                pl.BlockSpec((owners // steps, steps * piece, width), lambda j, *_: (j, 1, 0)),
            ],
            out_specs=[
                whole(rows, width),
                pl.BlockSpec((rows, width), lambda j, *_: (0, j)),
                pl.BlockSpec((owners // steps, steps * piece, width), lambda j, *_: (j, 0, 0)),
                whole(rows, width), whole(width, rows), whole(width, rows),
            ] + [head] * 6 + [whole(*vectors.shape)],
            scratch_shapes=[
                pltpu.VMEM((rows, width), F32),
                pltpu.VMEM((rows, width), BF), pltpu.VMEM((rows, width), BF),
                pltpu.VMEM((rows, width), BF), pltpu.VMEM((rows, width), BF),
                pltpu.VMEM((rows, width), F32),
            ],
        ),
        out_shape=[
            array(rows, width), array(rows, steps * width), array(owners, steps * piece, width),
            array(rows, width), array(width, rows), array(width, rows),
        ] + [array(rows, LANES)] * 6 + [array(*vectors.shape)],
        cost_estimate=pl.CostEstimate(
            flops=6 * rows * width * width * (5 * steps + 2), bytes_accessed=60 * 10**6, transcendentals=rows * steps * width
        ),
        compiler_params=pltpu.CompilerParams(vmem_limit_bytes=62 * 1024 * 1024),
        name="feed_forward",
    )(position, *out_own, *out_in, stream, cotangent, w_out, vectors, weights, weights)


def fast_shards(
    patches, segments, w_in, norm1_gain, norm1_bias, w_qkv, w_out, norm2_gain, norm2_bias, w_up, w_down, cotangent
):
    _, rows, patch_width = patches.shape
    piece, width = w_out.shape
    hidden = w_up.shape[1]
    owners = lax.axis_size("fsdp")
    position = lax.axis_index("sp")
    index = lax.axis_index("fsdp")
    places = position[None].astype(jnp.int32)
    labels = segments[0]
    length = labels.shape[0]
    labels_wide = jnp.broadcast_to(labels[:, None], (length, LANES))
    labels_row = labels.reshape(length // BLOCK, 1, BLOCK)
    blocks = hidden // width
    swap = [(0, 1), (1, 0)]

    vectors_own = jnp.tile(jnp.stack([norm1_gain, norm1_bias, norm2_gain, norm2_bias] + [norm1_gain] * 4), (1, owners))
    vectors_own = jnp.where(jnp.arange(width)[None, :] // piece == index, vectors_own, 0.0)
    (stream, normed, normed_turned, patches_turned, in_full, qkv_full, out_full, vectors, *sent) = gather_stream(
        patches[0], w_in, w_qkv, w_out, vectors_own
    )
    up_own = w_up.reshape(piece, blocks, width).transpose(1, 0, 2).reshape(blocks * piece, width)
    stacked = jnp.concatenate([up_own, w_down], axis=0)
    stacked, _ = lax.optimization_barrier((stacked, vectors))
    weights = lax.all_gather(stacked, "fsdp", axis=0, tiled=True).reshape(owners, 2 * blocks * piece, width)
    received = [lax.ppermute(part, "sp", swap) for part in sent]
    own = project_own(places, normed, qkv_full)
    attended = [attend_forward(a, b, places, labels, labels_wide, labels_row) for a, b in zip(own, received)]
    out_in = [lax.ppermute(part[1], "sp", swap) for part in attended]
    (block_out, grad_pre, grad_down, grad_resid, normed_two_turned, attended_turned,
     *grads) = middle(
        places, [part[0] for part in attended], out_in, stream, cotangent[0], out_full.reshape(width, width), vectors, weights
    )
    grad_sent, grad_own, sums = grads[:3], grads[3:6], grads[6]
    down_part = lax.psum_scatter(
        grad_down.reshape(hidden, width), ("fsdp", "sp"), scatter_dimension=0, tiled=True
    )
    grad_in = [lax.ppermute(part, "sp", swap) for part in grad_sent]
    both = [
        attend_backward(own[i], received[i], attended[i][0], attended[i][1], grad_own[i], grad_in[i], attended[i][2],
                        places, labels, labels_wide, labels_row)
        for i in range(3)
    ]
    mine = [pair[0] for pair in both]
    got = lax.ppermute(both[0][1], "sp", swap)
    grad_up, grad_out, grad_qkv, grad_w_in, grad_patch, vector_sums = back_and_reduce(
        [normed_two_turned, attended_turned, normed_turned, patches_turned], grad_pre, grad_resid,
        mine, got, [both[1][1], both[2][1]], qkv_full, stream, in_full.reshape(owners, in_full.shape[3], width), vectors, sums,
    )
    vector_sums = lax.dynamic_slice(vector_sums, (0, index * piece), (4, piece))
    down_part, _ = lax.optimization_barrier((down_part, vector_sums))
    down_other = lax.ppermute(down_part, "sp", swap)
    total_down = jnp.where(
        position == 0, jnp.concatenate([down_part, down_other]), jnp.concatenate([down_other, down_part])
    )
    return (
        block_out[None], grad_patch[None], grad_w_in, vector_sums[0], vector_sums[1],
        grad_qkv, grad_out, vector_sums[2], vector_sums[3], grad_up, total_down,
    )


def solution(mesh):
    sharded = P("fsdp", "sp", None)
    matrix = P("fsdp", None)
    vector = P("fsdp")
    fast = mesh.shape["fsdp"] == 16 and mesh.shape["sp"] == 2
    return jax.shard_map(
        fast_shards if fast else shards,
        mesh=mesh,
        in_specs=(sharded, matrix, matrix, vector, vector, matrix, matrix, vector, vector, matrix, matrix, sharded),
        out_specs=(sharded, sharded, matrix, vector, vector, matrix, matrix, vector, vector, matrix, matrix),
        check_vma=False,
    )
```

```python
import functools

import jax
import jax.numpy as jnp
from jax import lax
from jax.experimental import pallas as pl
from jax.experimental.pallas import tpu as pltpu
from jax.sharding import PartitionSpec as P

HEADS = 12


EPSILON = 1e-05


def matmul(left_side, right_side):
    return jnp.dot(
        left_side, right_side, precision=lax.Precision.HIGH, preferred_element_type=jnp.float32
    )


def matmul_tn(left_side, right_side):
    return lax.dot_general(
        left_side,
        right_side,
        (((0,), (0,)), ((), ())),
        precision=lax.Precision.HIGH,
        preferred_element_type=jnp.float32,
    )


def matmul_nt(left_side, right_side):
    return lax.dot_general(
        left_side,
        right_side,
        (((1,), (1,)), ((), ())),
        precision=lax.Precision.HIGH,
        preferred_element_type=jnp.float32,
    )


def layer_norm(values, scaling, offset):
    average = jnp.mean(values, axis=-1, keepdims=True)
    centred = values - average
    spread = jnp.mean(centred * centred, axis=-1, keepdims=True)
    return centred * lax.rsqrt(spread + EPSILON) * scaling + offset


def gelu_tanh(values):
    return jax.nn.gelu(values, approximate=True)


def scored(queries, key_rows, labels):
    length = labels.shape[0]
    factor = queries.shape[-1] ** (-0.5)
    raw_scores = matmul_nt(queries, key_rows) * factor
    places = jnp.arange(length, dtype=jnp.int32)
    allowed = (labels[:, None] == labels[None, :]) & (places[None, :] <= places[:, None])
    return (raw_scores, allowed, factor)


def attend_one(packed):
    queries, key_rows, value_rows, labels = packed
    raw_scores, allowed, factor = scored(queries, key_rows, labels)
    masked = jnp.where(allowed, raw_scores, -1e30)
    row_max = jnp.max(masked, axis=1, keepdims=True)
    exponent = jnp.exp(masked - row_max)
    summed = jnp.sum(exponent, axis=1, keepdims=True)
    attended = matmul(exponent / summed, value_rows)
    return (attended, (row_max + jnp.log(summed))[:, 0])


def attend_back(packed):
    queries, key_rows, value_rows, attended, log_total, grad_attended, labels = packed
    raw_scores, allowed, factor = scored(queries, key_rows, labels)
    weights = jnp.where(
        allowed, jnp.exp(jnp.where(allowed, raw_scores - log_total[:, None], -1e30)), 0.0
    )
    grad_values = matmul_tn(weights, grad_attended)
    grad_weights = matmul_nt(grad_attended, value_rows)
    row_dot = jnp.sum(grad_attended * attended, axis=1, keepdims=True)
    grad_scores = weights * (grad_weights - row_dot) * factor
    grad_queries = matmul(grad_scores, key_rows)
    grad_keys = matmul_tn(grad_scores, queries)
    return (grad_queries, grad_keys, grad_values)


def to_batch(blocked, heads_local):
    seq_count, length, columns = blocked.shape
    head_dim = columns // heads_local
    return (
        blocked.reshape(seq_count, length, heads_local, head_dim)
        .transpose(0, 2, 1, 3)
        .reshape(seq_count * heads_local, length, head_dim)
    )


def from_batch(blocked, seq_count):
    batch_size, length, head_dim = blocked.shape
    heads_local = batch_size // seq_count
    return (
        blocked.reshape(seq_count, heads_local, length, head_dim)
        .transpose(0, 2, 1, 3)
        .reshape(seq_count, length, heads_local * head_dim)
    )


def shards(
    patches,
    segments,
    w_in,
    norm1_gain,
    norm1_bias,
    w_qkv,
    w_out,
    norm2_gain,
    norm2_bias,
    w_up,
    w_down,
    cotangent,
):
    seq_count, local_len, patch_width = patches.shape
    model_width = w_out.shape[1]
    heads_local = HEADS // lax.axis_size("sp")
    row_count = seq_count * local_len
    norm_params = jnp.stack([norm1_gain, norm1_bias, norm2_gain, norm2_bias])
    gathered = (
        lax.all_gather(w_in, "fsdp", axis=0, tiled=True),
        lax.all_gather(w_qkv, "fsdp", axis=0, tiled=True),
        lax.all_gather(w_out, "fsdp", axis=0, tiled=True),
        lax.all_gather(w_up, "fsdp", axis=0, tiled=True),
        lax.all_gather(w_down, "fsdp", axis=0, tiled=True),
        lax.all_gather(norm_params, "fsdp", axis=1, tiled=True),
    )
    in_full, qkv_full, out_full, up_full, down_full, norm_full = gathered
    patch_rows = patches.reshape(row_count, patch_width)
    stream = matmul(patch_rows, in_full)
    normed, norm1_pull = jax.vjp(layer_norm, stream, norm_full[0], norm_full[1])
    projected = matmul(normed, qkv_full)
    query_tok = projected[:, :model_width].reshape(seq_count, local_len, model_width)
    key_tok = projected[:, model_width : 2 * model_width].reshape(seq_count, local_len, model_width)
    value_tok = projected[:, 2 * model_width :].reshape(seq_count, local_len, model_width)
    query_seq, key_seq, value_seq = (
        lax.all_to_all(query_tok, "sp", split_axis=2, concat_axis=1, tiled=True),
        lax.all_to_all(key_tok, "sp", split_axis=2, concat_axis=1, tiled=True),
        lax.all_to_all(value_tok, "sp", split_axis=2, concat_axis=1, tiled=True),
    )
    labels = jnp.repeat(segments, heads_local, axis=0)
    query_batch = to_batch(query_seq, heads_local)
    key_batch = to_batch(key_seq, heads_local)
    value_batch = to_batch(value_seq, heads_local)
    attended, log_total = lax.map(attend_one, (query_batch, key_batch, value_batch, labels))
    attended_tok = lax.all_to_all(
        from_batch(attended, seq_count), "sp", split_axis=1, concat_axis=2, tiled=True
    )
    attended_rows = attended_tok.reshape(row_count, model_width)
    residual = stream + matmul(attended_rows, out_full)
    normed_two, norm2_pull = jax.vjp(layer_norm, residual, norm_full[2], norm_full[3])
    hidden_pre = matmul(normed_two, up_full)
    hidden, gelu_pull = jax.vjp(gelu_tanh, hidden_pre)
    result = residual + matmul(hidden, down_full)
    block_out = result.reshape(seq_count, local_len, model_width)
    in_back, qkv_back, out_back, up_back, down_back = (
        lax.all_gather(w_in, "fsdp", axis=0, tiled=True),
        lax.all_gather(w_qkv, "fsdp", axis=0, tiled=True),
        lax.all_gather(w_out, "fsdp", axis=0, tiled=True),
        lax.all_gather(w_up, "fsdp", axis=0, tiled=True),
        lax.all_gather(w_down, "fsdp", axis=0, tiled=True),
    )
    grad_rows = cotangent.reshape(row_count, model_width)
    grad_down = matmul_tn(hidden, grad_rows)
    (grad_pre,) = gelu_pull(matmul_nt(grad_rows, down_back))
    grad_up = matmul_tn(normed_two, grad_pre)
    grad_resid_norm, grad_gain_two, grad_offset_two = norm2_pull(matmul_nt(grad_pre, up_back))
    grad_resid = grad_rows + grad_resid_norm
    grad_out = matmul_tn(attended_rows, grad_resid)
    grad_att = matmul_nt(grad_resid, out_back).reshape(seq_count, local_len, model_width)
    grad_att_seq = lax.all_to_all(grad_att, "sp", split_axis=2, concat_axis=1, tiled=True)
    grad_query, grad_key, grad_value = lax.map(
        attend_back,
        (
            query_batch,
            key_batch,
            value_batch,
            attended,
            log_total,
            to_batch(grad_att_seq, heads_local),
            labels,
        ),
    )
    back_query, back_key, back_value = (
        lax.all_to_all(
            from_batch(grad_query, seq_count), "sp", split_axis=1, concat_axis=2, tiled=True
        ),
        lax.all_to_all(
            from_batch(grad_key, seq_count), "sp", split_axis=1, concat_axis=2, tiled=True
        ),
        lax.all_to_all(
            from_batch(grad_value, seq_count), "sp", split_axis=1, concat_axis=2, tiled=True
        ),
    )
    grad_proj = jnp.concatenate([back_query, back_key, back_value], axis=2).reshape(
        row_count, 3 * model_width
    )
    grad_qkv = matmul_tn(normed, grad_proj)
    grad_stream_norm, grad_gain_one, grad_offset_one = norm1_pull(matmul_nt(grad_proj, qkv_back))
    grad_stream = grad_resid + grad_stream_norm
    grad_in = matmul_tn(patch_rows, grad_stream)
    grad_patch = matmul_nt(grad_stream, in_back).reshape(seq_count, local_len, patch_width)
    every_part = (
        lax.psum_scatter(grad_in, "fsdp", scatter_dimension=0, tiled=True),
        lax.psum_scatter(grad_qkv, "fsdp", scatter_dimension=0, tiled=True),
        lax.psum_scatter(grad_out, "fsdp", scatter_dimension=0, tiled=True),
        lax.psum_scatter(grad_up, "fsdp", scatter_dimension=0, tiled=True),
        lax.psum_scatter(grad_down, "fsdp", scatter_dimension=0, tiled=True),
        lax.psum_scatter(
            jnp.stack([grad_gain_one, grad_offset_one, grad_gain_two, grad_offset_two]),
            "fsdp",
            scatter_dimension=1,
            tiled=True,
        ),
    )
    total_in, total_qkv, total_out, total_up, total_down, norm_total = lax.psum(
        (every_part[0], every_part[1], every_part[2], every_part[3], every_part[4], every_part[5]),
        "sp",
    )
    norm_first = norm_total[0:2]
    norm_second = norm_total[2:4]
    return (
        block_out,
        grad_patch,
        total_in,
        norm_first[0],
        norm_first[1],
        total_qkv,
        total_out,
        norm_second[0],
        norm_second[1],
        total_up,
        total_down,
    )


LANES = 128
BLOCK = 256
BF = jnp.bfloat16
F32 = jnp.float32


def halves(values):
    high = values.astype(BF).astype(F32)
    return high, values - high


def roll_half(values):
    return pltpu.roll(values, LANES // 2, 1)


def low_lanes(rows):
    return lax.broadcasted_iota(jnp.int32, (rows, LANES), 1) < LANES // 2


def pair_tiles(values):
    high, low = halves(values)
    first = low_lanes(values.shape[0])
    return (
        jnp.where(first, high, roll_half(low)).astype(BF),
        jnp.where(first, roll_half(high), low).astype(BF),
    )


def spread_tiles(values):
    high, low = halves(values)
    first = low_lanes(values.shape[0])
    high_r, low_r = roll_half(high), roll_half(low)
    return (
        jnp.concatenate([jnp.where(first, high, high_r), jnp.where(first, low, low_r)], axis=1).astype(BF),
        jnp.concatenate([jnp.where(first, high_r, high), jnp.where(first, low_r, low)], axis=1).astype(BF),
    )


def nt(left, right):
    return lax.dot_general(left, right, (((1,), (1,)), ((), ())), preferred_element_type=F32)


def nn(left, right):
    return lax.dot_general(left, right, (((1,), (0,)), ((), ())), preferred_element_type=F32)


def tn(left, right):
    return lax.dot_general(left, right, (((0,), (0,)), ((), ())), preferred_element_type=F32)


def split_bf(values):
    high = values.astype(BF)
    return high, (values - high.astype(F32)).astype(BF)


def forward_kernel(pos_ref, seg_ref, *refs):
    (own_ref, in_ref, seg_col, seg_row,
     o_own, o_out, lse_ref, tq, hk, tv, out_s) = refs
    rows = own_ref.shape[0]
    own = pl.multiple_of(pos_ref[0] * rows, rows)
    other = pl.multiple_of((1 - pos_ref[0]) * rows, rows)
    for place, ref in ((own, own_ref), (other, in_ref)):
        span = pl.ds(place, rows)
        q, k, v = (ref.at[:, i * LANES:(i + 1) * LANES] for i in range(3))
        for head, tile in enumerate(pair_tiles(q[...] * 0.125)):
            tq[head, span, :] = jnp.concatenate([tile, tile], axis=1)
        for head, tile in enumerate(spread_tiles(k[...])):
            hk[head, span, :] = tile
        for head, tile in enumerate(pair_tiles(v[...])):
            tv[head, span, :] = tile
    blocks = 2 * rows // BLOCK
    first = low_lanes(BLOCK)

    def query_block(i, carry):
        q_span = pl.ds(pl.multiple_of(i * BLOCK, BLOCK), BLOCK)
        first_label = seg_ref[i * BLOCK]
        start = jnp.int32(0)
        for j in range(blocks):
            start = start + jnp.where((j < i) & (seg_ref[j * BLOCK + BLOCK - 1] < first_label), 1, 0)
        label = seg_col[q_span, :1]
        q_place = i * BLOCK + lax.broadcasted_iota(jnp.int32, (BLOCK, BLOCK), 0)

        def key_block(step, state):
            j = i - step
            k_span = pl.ds(pl.multiple_of(j * BLOCK, BLOCK), BLOCK)
            k_place = j * BLOCK + lax.broadcasted_iota(jnp.int32, (BLOCK, BLOCK), 1)
            allowed = (label == seg_row[j]) & (k_place <= q_place)
            new_state = []
            for head in range(2):
                top, total, acc = state[head]
                scores = nt(tq[head, q_span, :], hk[head, k_span, :])
                scores = jnp.where(allowed, scores, -1e30)
                new_top = jnp.maximum(top, jnp.max(scores, axis=1, keepdims=True))
                weight = jnp.exp(scores - new_top)
                keep = jnp.exp(top - new_top)
                high, low = split_bf(weight)
                values = tv[head, k_span, :]
                new_state.append((
                    new_top,
                    total * keep + jnp.sum(weight, axis=1, keepdims=True),
                    acc * keep + nn(high, values) + nn(low, values),
                ))
            return tuple(new_state)

        init = (
            jnp.full((BLOCK, 1), -1e30, F32),
            jnp.zeros((BLOCK, 1), F32),
            jnp.zeros((BLOCK, LANES), F32),
        )
        state = lax.fori_loop(0, i - start + 1, key_block, (init, init))
        outs, logs = [], []
        for top, total, acc in state:
            outs.append((acc + roll_half(acc)) / total)
            logs.append(jnp.broadcast_to(top + jnp.log(total), (BLOCK, LANES)))
        out_s[q_span, :] = jnp.where(first, outs[0], outs[1])
        lse_ref[q_span, :] = jnp.where(first, logs[0], logs[1])
        return carry

    lax.fori_loop(0, blocks, query_block, 0)
    o_own[...] = out_s[pl.ds(own, rows), :]
    o_out[...] = out_s[pl.ds(other, rows), :]


def attend_forward(own, received, position, labels, labels_wide, labels_row):
    rows = own.shape[0]
    length = 2 * rows
    smem = pl.BlockSpec(memory_space=pltpu.SMEM)
    vmem = pl.BlockSpec(memory_space=pltpu.VMEM)
    return pl.pallas_call(
        forward_kernel,
        in_specs=[smem, smem] + [vmem] * 4,
        out_specs=[vmem] * 3,
        scratch_shapes=[
            pltpu.VMEM((2, length, 2 * LANES), BF),
            pltpu.VMEM((2, length, 2 * LANES), BF),
            pltpu.VMEM((2, length, LANES), BF),
            pltpu.VMEM((length, LANES), F32),
        ],
        out_shape=[
            jax.ShapeDtypeStruct((rows, LANES), F32),
            jax.ShapeDtypeStruct((rows, LANES), F32),
            jax.ShapeDtypeStruct((length, LANES), F32),
        ],
        cost_estimate=pl.CostEstimate(flops=6 * 10**9, bytes_accessed=28 * rows * LANES, transcendentals=length * length),
        compiler_params=pltpu.CompilerParams(vmem_limit_bytes=32 * 1024 * 1024),
        name="attend_forward",
    )(position, labels, own, received, labels_wide, labels_row)


def backward_kernel(pos_ref, seg_ref, *refs):
    (own_ref, in_ref, o_own, o_in, g_own, g_in, lse_ref, seg_col, seg_row,
     grad_own, grad_out,
     tq, hk, tk, hv, tg, lse_t, delta_t, gq_s, gk_s, gv_s) = refs
    rows = own_ref.shape[0]
    length = 2 * rows
    own = pl.multiple_of(pos_ref[0] * rows, rows)
    other = pl.multiple_of((1 - pos_ref[0]) * rows, rows)
    half = LANES // 2
    for place, ref, o, g in ((own, own_ref, o_own, g_own), (other, in_ref, o_in, g_in)):
        span = pl.ds(place, rows)
        q, k, v = (ref.at[:, i * LANES:(i + 1) * LANES] for i in range(3))
        for head, tile in enumerate(pair_tiles(q[...] * 0.125)):
            tq[head, span, :] = jnp.concatenate([tile, tile], axis=1)
        for head, tile in enumerate(pair_tiles(g[...])):
            tg[head, span, :] = jnp.concatenate([tile, tile], axis=1)
        for head, tile in enumerate(spread_tiles(k[...])):
            hk[head, span, :] = tile
        for head, tile in enumerate(spread_tiles(v[...])):
            hv[head, span, :] = tile
        for head, tile in enumerate(pair_tiles(k[...])):
            tk[head, span, :] = tile
        turned = jnp.transpose(o[...] * g[...])
        for head in range(2):
            delta_t[head, 0:1, span] = jnp.sum(turned[head * half:(head + 1) * half], axis=0, keepdims=True)
    turned = jnp.transpose(lse_ref[...])
    for head in range(2):
        lse_t[head, 0:1, :] = turned[head * half:head * half + 1]
    blocks = length // BLOCK
    first = low_lanes(BLOCK)
    gq_s[...] = jnp.zeros_like(gq_s)

    def key_block(j, carry):
        k_span = pl.ds(pl.multiple_of(j * BLOCK, BLOCK), BLOCK)
        last_label = seg_ref[j * BLOCK + BLOCK - 1]
        count = jnp.int32(1)
        for i in range(blocks):
            count = count + jnp.where((i > j) & (seg_ref[i * BLOCK] <= last_label), 1, 0)
        label = seg_col[k_span, :1]
        k_place = j * BLOCK + lax.broadcasted_iota(jnp.int32, (BLOCK, BLOCK), 0)

        def query_block(step, state):
            i = j + step
            q_span = pl.ds(pl.multiple_of(i * BLOCK, BLOCK), BLOCK)
            q_place = i * BLOCK + lax.broadcasted_iota(jnp.int32, (BLOCK, BLOCK), 1)
            allowed = (label == seg_row[i]) & (k_place <= q_place)
            new_state = []
            for head in range(2):
                grad_k, grad_v = state[head]
                query = tq[head, q_span, :]
                grad = tg[head, q_span, :]
                scores = nt(hk[head, k_span, :], query)
                weight = jnp.exp(jnp.where(allowed, scores - lse_t[head, 0:1, q_span], -1e30))
                grad_weight = nt(hv[head, k_span, :], grad)
                grad_score = weight * (grad_weight - delta_t[head, 0:1, q_span])
                w_high, w_low = split_bf(weight)
                s_high, s_low = split_bf(grad_score)
                grad_v = grad_v + nn(w_high, grad[:, :LANES]) + nn(w_low, grad[:, :LANES])
                grad_k = grad_k + nn(s_high, query[:, :LANES]) + nn(s_low, query[:, :LANES])
                keys = tk[head, k_span, :]
                gq_s[head, q_span, :] += tn(s_high, keys) + tn(s_low, keys)
                new_state.append((grad_k, grad_v))
            return tuple(new_state)

        zero = jnp.zeros((BLOCK, LANES), F32)
        state = lax.fori_loop(0, count, query_block, ((zero, zero), (zero, zero)))
        for slot, store in ((0, gk_s), (1, gv_s)):
            left, right = state[0][slot], state[1][slot]
            store[k_span, :] = jnp.where(first, left + roll_half(left), right + roll_half(right))
        return carry

    lax.fori_loop(0, blocks, key_block, 0)
    wide = low_lanes(rows)
    for place, ref in ((own, grad_own), (other, grad_out)):
        span = pl.ds(place, rows)
        left, right = gq_s[0, span, :], gq_s[1, span, :]
        ref[:, :LANES] = jnp.where(wide, left + roll_half(left), right + roll_half(right)) * 0.125
        ref[:, LANES:2 * LANES] = gk_s[span, :]
        ref[:, 2 * LANES:] = gv_s[span, :]


def attend_backward(own, received, out_own, out_in, grad_own, grad_in, logs, position, labels, labels_wide, labels_row):
    rows = own.shape[0]
    length = 2 * rows
    smem = pl.BlockSpec(memory_space=pltpu.SMEM)
    vmem = pl.BlockSpec(memory_space=pltpu.VMEM)
    return pl.pallas_call(
        backward_kernel,
        in_specs=[smem, smem] + [vmem] * 9,
        out_specs=[vmem] * 2,
        scratch_shapes=[
            pltpu.VMEM((2, length, 2 * LANES), BF),
            pltpu.VMEM((2, length, 2 * LANES), BF),
            pltpu.VMEM((2, length, LANES), BF),
            pltpu.VMEM((2, length, 2 * LANES), BF),
            pltpu.VMEM((2, length, 2 * LANES), BF),
            pltpu.VMEM((2, 8, length), F32),
            pltpu.VMEM((2, 8, length), F32),
            pltpu.VMEM((2, length, LANES), F32),
            pltpu.VMEM((length, LANES), F32),
            pltpu.VMEM((length, LANES), F32),
        ],
        out_shape=[jax.ShapeDtypeStruct((rows, 3 * LANES), F32)] * 2,
        cost_estimate=pl.CostEstimate(flops=13 * 10**9, bytes_accessed=60 * rows * LANES, transcendentals=length * length),
        compiler_params=pltpu.CompilerParams(vmem_limit_bytes=40 * 1024 * 1024),
        name="attend_backward",
    )(position, labels, own, received, out_own, out_in, grad_own, grad_in, logs, labels_wide, labels_row)


MESH = pl.DeviceIdType.MESH
PIECE = 48
FLAT_PAIRS = 2


def back_kernel(plan, *refs):
    up_units, out_units, qkv_units, in_units = plan
    units = sum(plan)
    pairs = units // 2
    first_qkv = up_units + out_units
    first_in = first_qkv + qkv_units
    (up_turned, out_turned, qkv_turned, in_turned, grad_pre, grad_resid, mine_0, mine_1, mine_2, got_0, sent_1, sent_2,
     qkv_ref, stream_ref, weight_ref, vectors_ref, sums_ref,
     up_total, out_total, qkv_total, in_total, patch_ref, norm_total_ref, got_1, got_2,
     t_buf, g_buf, g_high, g_low, part, s_high, s_low, w_buf, p_buf, q_buf, acc, land_a, n_x, n_z, n_y, y_y, y_x, y_z, done,
     v_own, v_c, v_x, v_y, v_z,
     load_sem, w_sem, p_sem, q_sem, norm_sem, swap_sem,
     a_sem, nx_sem, nz_sem, ny_sem, yy_sem, yx_sem, yz_sem, ye_sem, v_sem, o_sem) = refs
    mine, got = (mine_0, mine_1, mine_2), (got_0, got_1, got_2)
    width = g_buf.shape[2]
    fsdp = lax.axis_index("fsdp")
    row = lax.axis_index("sp")
    z, x, core = fsdp // 4, (fsdp // 2) % 2, fsdp % 2
    half = PIECE // 2

    def device(z_at, x_at, core_at, row_at):
        return ((z_at * 2 + x_at) * 2 + core_at, row_at)

    sibling = device(z, x, 1 - core, row)
    beside = device(z, 1 - x, core, row)
    across = device(z, x, core, 1 - row)
    along = [device((z + step) % 4, x, core, row) for step in (1, 2, 3)]

    barrier = pltpu.get_barrier_semaphore()
    for peer in [sibling, beside, across] + along:
        pl.semaphore_signal(barrier, inc=1, device_id=peer, device_id_type=MESH)

    def remote(source, target, sems, index, peer):
        return pltpu.make_async_remote_copy(
            src_ref=source, dst_ref=target, send_sem=sems.at[(0,) + index], recv_sem=sems.at[(1,) + index],
            device_id=peer, device_id_type=MESH,
        )

    def span(first, size):
        return pl.ds(pl.multiple_of(first, size), size)

    def loop(number, body):
        def step(i, carry):
            body(i)
            return carry

        lax.fori_loop(0, number, step, 0)

    def start(copy):
        copy.start()

    def wait(copy):
        copy.wait()

    def loads(unit, slot, act):
        def left(view):
            for side in range(2):
                act(pltpu.make_async_copy(view.at[:, side], t_buf.at[slot, side], load_sem.at[slot, side]))

        def right(source):
            act(pltpu.make_async_copy(source, g_buf.at[slot], load_sem.at[slot, 2]))

        @pl.when(unit < up_units)
        def _():
            left(up_turned)
            right(grad_pre.at[:, span(unit * width, width)])

        @pl.when((unit >= up_units) & (unit < first_qkv))
        def _():
            left(out_turned)
            right(grad_resid.at[:, span((unit - up_units) * width, width)])

        @pl.when((unit >= first_qkv) & (unit < first_in))
        def _():
            left(qkv_turned)
            for j in range(qkv_units):
                kind, side = divmod(j, 2)
                for sources, own in ((mine, True), (got, False)):
                    @pl.when((unit == first_qkv + j) & ((row == side) == own))
                    def _(kind=kind, sources=sources):
                        for i, source in enumerate(sources):
                            act(pltpu.make_async_copy(
                                source.at[:, kind * LANES:(kind + 1) * LANES],
                                g_buf.at[slot, :, i * LANES:(i + 1) * LANES],
                                load_sem.at[slot, 2 + i],
                            ))

        @pl.when(unit >= first_in)
        def _():
            j = (unit - first_in) // 2
            for side in range(2):
                act(pltpu.make_async_copy(in_turned.at[:, side, j], t_buf.at[slot, side], load_sem.at[slot, side]))

    def weight_copy(block, slot):
        return pltpu.make_async_copy(weight_ref.at[block], w_buf.at[slot], w_sem.at[slot])

    def patch_copy(block, slot):
        columns = w_buf.shape[1]
        return pltpu.make_async_copy(p_buf.at[slot], patch_ref.at[:, span(block * columns, columns)], p_sem.at[slot])

    def q_copy(j):
        return pltpu.make_async_copy(qkv_ref.at[:, :, :, :, span(j * width, width)], q_buf, q_sem)

    rows = stream_ref.shape[0]
    cut = w_buf.shape[1]
    norm_copies = [
        pltpu.make_async_copy(stream_ref.at[:, 0:width], p_buf.at[0], norm_sem.at[0]),
        pltpu.make_async_copy(stream_ref.at[:, width:], p_buf.at[1], norm_sem.at[1]),
        pltpu.make_async_copy(grad_resid.at[0:cut], w_buf.at[0], norm_sem.at[2]),
        pltpu.make_async_copy(grad_resid.at[cut:], w_buf.at[1, 0:rows - cut], norm_sem.at[3]),
    ]
    swap_copies = [
        remote(sent_1, got_1, swap_sem, (0,), across),
        remote(sent_2, got_2, swap_sem, (1,), across),
    ]

    def core_copy(unit, slot):
        return remote(part.at[slot, 1 - core], land_a.at[unit], a_sem, (unit,), sibling)

    def nx_copy(unit, n):
        return remote(land_a.at[unit, :, 1 - x], n_x.at[n], nx_sem, (n,), beside)

    def nz_copy(n, step):
        return remote(n_x.at[n, (z + step + 1) % 4], n_z.at[n, step], nz_sem, (n, step), along[step])

    def ny_copy(n):
        return remote(n_x.at[n, z], n_y.at[n], ny_sem, (n,), across)

    def yy_copy(unit, p):
        return remote(land_a.at[unit, :, :, span((1 - row) * half, half)], y_y.at[p], yy_sem, (p,), across)

    def yx_copy(p):
        return remote(y_y.at[p, :, 1 - x], y_x.at[p], yx_sem, (p,), beside)

    def yz_copy(p, step):
        return remote(y_x.at[p, (z + step + 1) % 4], y_z.at[p, step], yz_sem, (p, step), along[step])

    def ye_copy(unit, p):
        return remote(y_x.at[p, z], done.at[unit, span(row * half, half)], ye_sem, (p,), across)

    def flat_number(pair):
        return pairs + pair

    def other_number(pair):
        return pair - FLAT_PAIRS

    def odd(pair, flat, other):
        @pl.when(pair < FLAT_PAIRS)
        def _():
            flat(2 * pair + 1, flat_number(pair))

        @pl.when(pair >= FLAT_PAIRS)
        def _():
            other(2 * pair + 1, other_number(pair))

    v_copies = [
        remote(v_own, v_c, v_sem, (0,), sibling),
        remote(v_c, v_x, v_sem, (1,), beside),
        remote(v_x, v_y, v_sem, (2,), across),
    ] + [remote(v_y, v_z.at[step], v_sem, (3 + step,), along[step]) for step in range(3)]

    loads(jnp.int32(0), 0, start)
    q_copy(0).start()
    for copy in norm_copies:
        copy.start()
    pl.semaphore_wait(barrier, 6)
    for copy in swap_copies:
        copy.start()

    def norm_backward():
        for copy in norm_copies:
            copy.wait()
        values = jnp.concatenate([p_buf[0], p_buf[1]], axis=1)
        back, gain, offset = norm_back(acc[...], values, vectors_ref[0:1, :])
        v_own[...] = sums_ref[...]
        v_own[0:1, :] = gain
        v_own[1:2, :] = offset
        acc[...] = back
        acc[0:cut, :] = acc[0:cut, :] + w_buf[0]
        acc[cut:, :] = acc[cut:, :] + w_buf[1, 0:rows - cut]
        s_high[...] = acc[...].astype(BF)
        s_low[...] = (acc[...] - s_high[...].astype(F32)).astype(BF)
        weight_copy(0, 0).start()
        v_copies[0].start()

    def compute(unit, slot):
        loads(unit, slot, wait)

        @pl.when(unit + 1 < units)
        def _():
            loads(unit + 1, 1 - slot, start)

        @pl.when(unit >= 2)
        def _():
            core_copy(unit - 2, slot).wait_send()

        @pl.when(unit < first_in)
        def _():
            grad = g_buf[slot]
            g_high[...] = grad.astype(BF)
            g_low[...] = (grad - g_high[...].astype(F32)).astype(BF)

        @pl.when(unit >= first_in)
        def _():
            columns = span(((unit - first_in) % 2) * width, width)
            g_high[...] = s_high[:, columns]
            g_low[...] = s_low[:, columns]

        def side_of(turn, carry):
            side = jnp.where(turn == 0, 1 - core, core)
            high, low = split_bf(t_buf[slot, side].reshape(8 * PIECE, t_buf.shape[4]))
            product = nn(high, g_high[...]) + nn(high, g_low[...]) + nn(low, g_high[...])
            part[slot, side] = product.reshape(4, 2, PIECE, product.shape[1])

            @pl.when(turn == 0)
            def _():
                core_copy(unit, slot).start()

            return carry

        lax.fori_loop(0, 2, side_of, 0)

        @pl.when((unit >= first_qkv) & (unit < first_in))
        def _():
            j = unit - first_qkv
            q_copy(j).wait()
            weight = split_bf(q_buf[...].reshape(acc.shape[1], width))
            acc[...] = acc[...] + three(nt, (g_high[...], g_low[...]), weight)

            @pl.when(j + 1 < qkv_units)
            def _():
                q_copy(j + 1).start()

    def patch_block(block, slot):
        weight_copy(block, slot).wait()

        @pl.when(block + 1 < weight_ref.shape[0])
        def _():
            weight_copy(block + 1, 1 - slot).start()

        @pl.when(block >= 2)
        def _():
            patch_copy(block - 2, slot).wait()

        p_buf[slot] = three(nt, (s_high[...], s_low[...]), split_bf(w_buf[slot]))
        patch_copy(block, slot).start()

    def after_core(unit, slot):
        core_copy(unit, slot).wait_recv()

        def add(i):
            for b in range(2):
                land_a[unit, i, b] = land_a[unit, i, b] + part[slot, core, i, b]

        loop(4, add)

    def flat_x(unit, n):
        nx_copy(unit, n).wait_recv()

        def add(i):
            n_x[n, i] = n_x[n, i] + land_a[unit, i, x]

        loop(4, add)
        for step in range(3):
            nz_copy(n, step).start()

    def flat_z(unit, n):
        for step in range(3):
            nz_copy(n, step).wait_recv()
        n_x[n, z] = n_x[n, z] + n_z[n, 0] + n_z[n, 1] + n_z[n, 2]
        ny_copy(n).start()

    def flat_y(unit, n):
        ny_copy(n).wait_recv()
        done[unit] = n_x[n, z] + n_y[n]

    def other_y(unit, p):
        yy_copy(unit, p).wait_recv()
        own = span(row * half, half)

        def add(i):
            for b in range(2):
                y_y[p, i, b] = y_y[p, i, b] + land_a[unit, i, b, own]

        loop(4, add)
        yx_copy(p).start()

    def other_x(unit, p):
        yx_copy(p).wait_recv()

        def add(i):
            y_x[p, i] = y_x[p, i] + y_y[p, i, x]

        loop(4, add)
        for step in range(3):
            yz_copy(p, step).start()

    def other_z(unit, p):
        for step in range(3):
            yz_copy(p, step).wait_recv()
        total = y_x[p, z] + y_z[p, 0] + y_z[p, 1] + y_z[p, 2]
        y_x[p, z] = total
        done[unit, span(row * half, half)] = total
        ye_copy(unit, p).start()

    acc[...] = jnp.zeros_like(acc)

    def iteration(p, carry):
        @pl.when(p == first_qkv // 2 - 1)
        def _():
            for copy in swap_copies:
                copy.wait_recv()

        @pl.when(p < pairs)
        def _():
            compute(2 * p, 0)
            compute(2 * p + 1, 1)
            after_core(2 * p, 0)
            nx_copy(2 * p, p).start()
            after_core(2 * p + 1, 1)
            odd(p, lambda unit, n: nx_copy(unit, n).start(), lambda unit, i: yy_copy(unit, i).start())

        @pl.when(p == first_in // 2 - 1)
        def _():
            norm_backward()

        q = p - 1

        @pl.when((q >= 0) & (q < pairs))
        def _():
            flat_x(2 * q, q)
            odd(q, flat_x, other_y)

        @pl.when((p >= first_in // 2) & (p < pairs))
        def _():
            patch_block(2 * p - first_in, 0)
            patch_block(2 * p - first_in + 1, 1)

        r = p - 2

        @pl.when((r >= 0) & (r < pairs))
        def _():
            flat_z(2 * r, r)
            odd(r, flat_z, other_x)

        s = p - 3

        @pl.when((s >= 0) & (s < pairs))
        def _():
            flat_y(2 * s, s)
            odd(s, flat_y, other_z)

        turn = p - first_in // 2

        @pl.when(turn == 0)
        def _():
            v_copies[0].wait_recv()
            v_c[...] = v_c[...] + v_own[...]
            v_copies[1].start()

        @pl.when(turn == 1)
        def _():
            v_copies[1].wait_recv()
            v_x[...] = v_x[...] + v_c[...]
            v_copies[2].start()

        @pl.when(turn == 2)
        def _():
            v_copies[2].wait_recv()
            v_y[...] = v_y[...] + v_x[...]
            for step in range(3):
                v_copies[3 + step].start()

        @pl.when(turn == 3)
        def _():
            for step in range(3):
                v_copies[3 + step].wait_recv()
            norm_total_ref[...] = v_y[...] + v_z[0] + v_z[1] + v_z[2]

        return carry

    lax.fori_loop(0, pairs + 3, iteration, 0)

    def flat_end(unit, n):
        nx_copy(unit, n).wait_send()
        ny_copy(n).wait_send()
        for step in range(3):
            nz_copy(n, step).wait_send()

    def other_end(unit, p):
        ye_copy(unit, p).wait()
        yy_copy(unit, p).wait_send()
        yx_copy(p).wait_send()
        for step in range(3):
            yz_copy(p, step).wait_send()

    def finish(p):
        flat_end(2 * p, p)
        odd(p, flat_end, other_end)

    loop(pairs, finish)

    def out_copy(unit, act):
        @pl.when(unit < up_units)
        def _():
            act(pltpu.make_async_copy(done.at[unit], up_total.at[:, span(unit * width, width)], o_sem.at[unit]))

        @pl.when((unit >= up_units) & (unit < first_qkv))
        def _():
            act(pltpu.make_async_copy(done.at[unit], out_total.at[:, span((unit - up_units) * width, width)], o_sem.at[unit]))

        @pl.when((unit >= first_qkv) & (unit < first_in))
        def _():
            act(pltpu.make_async_copy(done.at[unit], qkv_total.at[:, span((unit - first_qkv) * width, width)], o_sem.at[unit]))

        @pl.when(unit >= first_in)
        def _():
            j = unit - first_in
            act(pltpu.make_async_copy(
                done.at[unit], in_total.at[span((j // 2) * PIECE, PIECE), span((j % 2) * width, width)], o_sem.at[unit]
            ))

    loop(units, lambda unit: out_copy(unit, start))
    for copy in v_copies + swap_copies:
        copy.wait_send()
    core_copy(units - 2, 0).wait_send()
    core_copy(units - 1, 1).wait_send()
    blocks = weight_ref.shape[0]
    patch_copy(blocks - 2, 0).wait()
    patch_copy(blocks - 1, 1).wait()
    loop(units, lambda unit: out_copy(unit, wait))


def back_and_reduce(turned, grad_pre, grad_resid, mine, got, sent, qkv_full, stream, weights, vectors, sums):
    rows, full = stream.shape
    width = full // 2
    owners, block, _ = weights.shape
    piece = full // owners
    columns = [grad_pre.shape[1], full, qkv_full.shape[4], full]
    plan = [c // width for c in columns]
    plan[3] *= block // piece
    views = [left.reshape(8, 2, piece, rows) for left in turned[:3]] + [turned[3].reshape(8, 2, block // piece, piece, rows)]
    units = sum(plan)
    pairs = units // 2
    flats, others = pairs + FLAT_PAIRS, pairs - FLAT_PAIRS
    assert piece == PIECE and plan[3] == owners and (plan[0] + plan[1]) % 2 == 0 and plan[2] == 6
    half = PIECE // 2
    dma = pltpu.SemaphoreType.DMA
    any_space = pl.BlockSpec(memory_space=pl.ANY)
    vmem = pl.BlockSpec(memory_space=pltpu.VMEM)

    def array(*shape):
        return jax.ShapeDtypeStruct(shape, F32)

    return pl.pallas_call(
        functools.partial(back_kernel, tuple(plan)),
        out_shape=[
            array(piece, columns[0]), array(piece, full), array(piece, columns[2]), array(block, full),
            array(rows, owners * block), array(*vectors.shape), array(*got.shape), array(*got.shape),
        ],
        in_specs=[any_space] * 15 + [vmem, vmem],
        out_specs=[any_space] * 5 + [vmem, any_space, any_space],
        scratch_shapes=[
            pltpu.VMEM((2, 2, 8, PIECE, rows), F32),
            pltpu.VMEM((2, rows, width), F32),
            pltpu.VMEM((rows, width), BF),
            pltpu.VMEM((rows, width), BF),
            pltpu.VMEM((2, 2, 4, 2, PIECE, width), F32),
            pltpu.VMEM((rows, full), BF),
            pltpu.VMEM((rows, full), BF),
            pltpu.VMEM((2, block, full), F32),
            pltpu.VMEM((2, rows, block), F32),
            pltpu.VMEM((4, 2, 2, PIECE, width), F32),
            pltpu.VMEM((rows, full), F32),
            pltpu.VMEM((units, 4, 2, PIECE, width), F32),
            pltpu.VMEM((flats, 4, PIECE, width), F32),
            pltpu.VMEM((flats, 3, PIECE, width), F32),
            pltpu.VMEM((flats, PIECE, width), F32),
            pltpu.VMEM((others, 4, 2, half, width), F32),
            pltpu.VMEM((others, 4, half, width), F32),
            pltpu.VMEM((others, 3, half, width), F32),
            pltpu.VMEM((units, PIECE, width), F32),
            pltpu.VMEM(vectors.shape, F32),
            pltpu.VMEM(vectors.shape, F32),
            pltpu.VMEM(vectors.shape, F32),
            pltpu.VMEM(vectors.shape, F32),
            pltpu.VMEM((3,) + vectors.shape, F32),
            dma((2, 5)), dma((2,)), dma((2,)), dma, dma((4,)), dma((2, 2)),
            dma((2, units)), dma((2, flats)), dma((2, flats, 3)), dma((2, flats)),
            dma((2, others)), dma((2, others)), dma((2, others, 3)), dma((2, others)),
            dma((2, 6)), dma((units,)),
        ],
        cost_estimate=pl.CostEstimate(
            flops=6 * rows * full * (units * 8 * PIECE + owners * block), bytes_accessed=130 * 10**6, transcendentals=0
        ),
        compiler_params=pltpu.CompilerParams(
            collective_id=0, has_side_effects=True, vmem_limit_bytes=67043328
        ),
        name="back_and_reduce",
    )(*views, grad_pre, grad_resid, *mine, got, *sent, qkv_full, stream, weights, vectors, sums)[:6]


CUT_ROWS = 128
CUT_COLUMNS = 128
NARROW = 384


def three(product, left, right):
    return product(left[0], right[0]) + product(left[0], right[1]) + product(left[1], right[0])


def normalized(values):
    average = jnp.mean(values, axis=-1, keepdims=True)
    centred = values - average
    spread = jnp.mean(centred * centred, axis=-1, keepdims=True)
    scale = lax.rsqrt(spread + EPSILON)
    return centred * scale, scale


def gather_kernel(patch_ref, in_ref, qkv_ref, out_ref, vector_ref,
                  stream_ref, normed_ref, turned_ref, patch_turned_ref, in_full, qkv_full, out_full, vectors_ref,
                  sent_0, sent_1, sent_2,
                  patch_buf, in_buf, qkv_buf, out_buf, turn_buf, acc, v_c, v_x, v_z, sent_buf,
                  z_sem, x_sem, y_sem, c_sem, v_sem, own_sem, patch_sem, turn_sem, full_sem, last_sem):
    fsdp = lax.axis_index("fsdp")
    row = lax.axis_index("sp")
    z, x, core = fsdp // 4, (fsdp // 2) % 2, fsdp % 2
    block, width = in_ref.shape
    across_count = width // CUT_COLUMNS
    in_units = (block // CUT_ROWS) * across_count
    narrow = NARROW
    out_units = width // narrow
    units = in_units + qkv_ref.shape[1] // narrow + out_units

    def device(z_at, x_at, core_at, row_at):
        return ((z_at * 2 + x_at) * 2 + core_at, row_at)

    sibling = device(z, x, 1 - core, row)
    beside = device(z, 1 - x, core, row)
    across = device(z, x, core, 1 - row)
    along = [device((z + step) % 4, x, core, row) for step in (1, 2, 3)]
    barrier = pltpu.get_barrier_semaphore()
    for peer in [sibling, beside, across] + along:
        pl.semaphore_signal(barrier, inc=1, device_id=peer, device_id_type=MESH)

    def remote(source, target, sems, index, peer):
        return pltpu.make_async_remote_copy(
            src_ref=source, dst_ref=target, send_sem=sems.at[(0,) + index], recv_sem=sems.at[(1,) + index],
            device_id=peer, device_id_type=MESH,
        )

    patch_copy = pltpu.make_async_copy(patch_ref, patch_buf, patch_sem)

    def span(first, size, step=None):
        return pl.ds(pl.multiple_of(first, step or size), size)

    def places(kind, unit, part):
        if kind == "in":
            j, column = unit // across_count, unit % across_count
            columns = span(column * CUT_COLUMNS, CUT_COLUMNS)
            base, rows, edge = j * CUT_ROWS, CUT_ROWS, 40
        else:
            rows, edge = out_ref.shape[0], 16
            first = in_units if kind == "qkv" else units - out_units
            base, columns = 0, span((unit - first) * narrow, narrow)
        if part is None:
            return span(base, rows, 8), columns
        which, side = part
        if which == 0:
            return span(base + side * (rows - edge), edge, 8), columns
        return span(base + side * edge, rows - edge, 8), columns

    sources = {"in": (in_ref, in_buf), "qkv": (qkv_ref, qkv_buf), "out": (out_ref, out_buf)}

    def each_kind(unit, act):
        ranges = (("in", 0, in_units), ("qkv", in_units, units - out_units), ("out", units - out_units, units))
        for kind, first, last in ranges:
            @pl.when((unit >= first) & (unit < last))
            def _(kind=kind):
                act(kind)

    own_copies = []
    for kind, firsts in (("in", range(0, block, CUT_ROWS)), ("qkv", (0,)), ("out", (0,))):
        source, buf = sources[kind]
        for first in firsts:
            rows = places(kind, first // CUT_ROWS * across_count if kind == "in" else in_units, (1, row))[0]
            own_copies.append(
                pltpu.make_async_copy(source.at[rows], buf.at[z, x, core, rows], own_sem.at[len(own_copies)])
            )

    def z_copy(kind, unit, step):
        source, buf = sources[kind]
        at = places(kind, unit, (1, row))
        return remote(source.at[at], buf.at[(z, x, core) + at], z_sem, (unit, step), along[step])

    def x_copy(kind, unit):
        ref = sources[kind][1].at[(slice(None), x, core) + places(kind, unit, (1, row))]
        return remote(ref, ref, x_sem, (unit,), beside)

    def y_copy(kind, unit):
        ref = sources[kind][1].at[(slice(None), slice(None), core) + places(kind, unit, (0, row))]
        return remote(ref, ref, y_sem, (unit,), across)

    def c_copy(kind, unit, index):
        part = (1, row) if index == 0 else (0, 1 - row)
        ref = sources[kind][1].at[(slice(None), slice(None), core) + places(kind, unit, part)]
        return remote(ref, ref, c_sem, (unit, index), sibling)

    def z_stage(unit):
        def act(kind):
            for step in range(3):
                z_copy(kind, unit, step).start()

        each_kind(unit, act)

    def x_stage(unit):
        def act(kind):
            for step in range(3):
                z_copy(kind, unit, step).wait_recv()
            x_copy(kind, unit).start()

        each_kind(unit, act)

    def spread_stage(unit):
        def act(kind):
            x_copy(kind, unit).wait_recv()
            y_copy(kind, unit).start()
            c_copy(kind, unit, 0).start()

        each_kind(unit, act)

    def y_stage(unit):
        def act(kind):
            y_copy(kind, unit).wait_recv()
            c_copy(kind, unit, 1).start()

        each_kind(unit, act)

    def ready(unit):
        def act(kind):
            c_copy(kind, unit, 0).wait_recv()
            c_copy(kind, unit, 1).wait_recv()
            full_copy(kind, unit).start()

        each_kind(unit, act)

    def full_copy(kind, unit):
        at = (slice(None), slice(None), slice(None)) + places(kind, unit, None)
        full = {"in": in_full, "qkv": qkv_full, "out": out_full}[kind]
        return pltpu.make_async_copy(sources[kind][1].at[at], full.at[at], full_sem.at[unit])

    def multiply(unit):
        j, column = unit // across_count, unit % across_count
        columns = span(column * CUT_COLUMNS, CUT_COLUMNS)
        rows = span(j * CUT_ROWS, CUT_ROWS)

        def step(pair, carry):
            first = pair * 2 * block + j * CUT_ROWS
            left = jnp.concatenate(
                [patch_buf[:, span(first, CUT_ROWS)], patch_buf[:, span(first + block, CUT_ROWS)]], axis=1
            )
            right = in_buf[pair // 2, pair % 2, :, rows, columns].reshape(2 * CUT_ROWS, CUT_COLUMNS)
            acc[:, columns] = acc[:, columns] + three(nn, split_bf(left), split_bf(right))
            return carry

        lax.fori_loop(0, 8, step, 0)

    tiles = patch_ref.shape[1] // LANES
    each = turn_buf.shape[0]

    def turn_copy(tile, slot):
        return pltpu.make_async_copy(turn_buf.at[slot], patch_turned_ref.at[span(tile * LANES, LANES)], turn_sem.at[slot])

    def turn(group):
        for slot in range(each):
            @pl.when(group > 0)
            def _(slot=slot):
                turn_copy((group - 1) * each + slot, slot).wait()

            turn_buf[slot] = jnp.transpose(patch_buf[:, span((group * each + slot) * LANES, LANES)])
            turn_copy(group * each + slot, slot).start()

    pl.semaphore_wait(barrier, 6)
    z_stage(jnp.int32(0))
    z_stage(jnp.int32(1))
    for copy in own_copies:
        copy.start()
    patch_copy.start()
    v_copies = [
        remote(vector_ref, v_c, v_sem, (0,), sibling),
        remote(v_c, v_x, v_sem, (1,), beside),
    ] + [remote(v_x, v_z.at[step], v_sem, (2 + step,), along[step]) for step in range(3)]
    v_copies[0].start()
    acc[...] = jnp.zeros_like(acc)
    for copy in own_copies:
        copy.wait()

    sent_copies = [
        pltpu.make_async_copy(sent_buf.at[group], ref, last_sem.at[group])
        for group, ref in enumerate((sent_0, sent_1, sent_2))
    ]

    def iteration(t, carry):
        z_stage(t + 2)
        x_stage(t)
        spread_stage(t - 2)
        y_stage(t - 4)

        @pl.when(t == 0)
        def _():
            patch_copy.wait()
            v_copies[0].wait_recv()
            v_c[...] = v_c[...] + vector_ref[...]
            v_copies[1].start()

        @pl.when(t == 1)
        def _():
            v_copies[1].wait_recv()
            v_x[...] = v_x[...] + v_c[...]
            for step in range(3):
                v_copies[2 + step].start()

        @pl.when(t == 2)
        def _():
            for step in range(3):
                v_copies[2 + step].wait_recv()
            vectors_ref[...] = v_x[...] + v_z[0] + v_z[1] + v_z[2]

        @pl.when(t < tiles // each)
        def _():
            turn(t)

        ready(t - 5)

        @pl.when((t >= 5) & (t < in_units + 5))
        def _():
            multiply(t - 5)

        @pl.when(t == in_units + 5)
        def _():
            stream = acc[...]
            stream_ref[...] = stream
            zhat, _ = normalized(stream)
            acc[...] = zhat * vectors_ref[0:1, :] + vectors_ref[1:2, :]
            normed_ref[...] = acc[...]
            turned_ref[...] = jnp.transpose(acc[...])

        @pl.when(t == units - out_units + 4)
        def _():
            left = split_bf(acc[...])
            for group in range(3):
                right = jnp.concatenate(
                    [
                        qkv_buf[:, :, :, :, span(which * width + (1 - row) * (width // 2) + group * LANES, LANES)].reshape(
                            width, LANES
                        )
                        for which in range(3)
                    ],
                    axis=1,
                )
                sent_buf[group] = three(nn, left, split_bf(right))
                sent_copies[group].start()

        return carry

    lax.fori_loop(0, units + 5, iteration, 0)
    def finish(unit, carry):
        def act(kind):
            for step in range(3):
                z_copy(kind, unit, step).wait_send()
            x_copy(kind, unit).wait_send()
            y_copy(kind, unit).wait_send()
            c_copy(kind, unit, 0).wait_send()
            c_copy(kind, unit, 1).wait_send()
            full_copy(kind, unit).wait()

        each_kind(unit, act)
        return carry

    lax.fori_loop(0, units, finish, 0)
    for copy in v_copies:
        copy.wait_send()
    for slot in range(each):
        turn_copy(tiles - each + slot, slot).wait()
    for copy in sent_copies:
        copy.wait()


def gather_stream(patch_rows, w_in, w_qkv, w_out, vectors):
    rows, patch_width = patch_rows.shape
    block, width = w_in.shape
    piece, columns = w_qkv.shape
    group = columns // 6
    any_space = pl.BlockSpec(memory_space=pl.ANY)
    vmem = pl.BlockSpec(memory_space=pltpu.VMEM)
    dma = pltpu.SemaphoreType.DMA
    units = (block // CUT_ROWS) * (width // CUT_COLUMNS) + (columns + width) // NARROW
    owners = (4, 2, 2)

    def array(*shape):
        return jax.ShapeDtypeStruct(shape, F32)

    return pl.pallas_call(
        gather_kernel,
        out_shape=[
            array(rows, width), array(rows, width), array(width, rows), array(patch_width, rows),
            array(*owners, block, width), array(*owners, piece, columns), array(*owners, piece, width),
            array(*vectors.shape), array(rows, group), array(rows, group), array(rows, group),
        ],
        in_specs=[any_space] * 4 + [vmem],
        out_specs=[vmem, vmem, vmem] + [any_space] * 4 + [vmem] + [any_space] * 3,
        scratch_shapes=[
            pltpu.VMEM((rows, patch_width), F32),
            pltpu.VMEM(owners + (block, width), F32),
            pltpu.VMEM(owners + (piece, columns), F32),
            pltpu.VMEM(owners + (piece, width), F32),
            pltpu.VMEM((4, LANES, rows), F32),
            pltpu.VMEM((rows, width), F32),
            pltpu.VMEM(vectors.shape, F32),
            pltpu.VMEM(vectors.shape, F32),
            pltpu.VMEM((3,) + vectors.shape, F32),
            pltpu.VMEM((3, rows, group), F32),
            dma((2, units, 3)), dma((2, units)), dma((2, units)), dma((2, units, 2)), dma((2, 5)),
            dma((block // CUT_ROWS + 2,)), dma, dma((4,)), dma((units,)), dma((3,)),
        ],
        cost_estimate=pl.CostEstimate(flops=6 * rows * patch_width * width, bytes_accessed=90 * 10**6, transcendentals=0),
        compiler_params=pltpu.CompilerParams(collective_id=1, has_side_effects=True, vmem_limit_bytes=67043328),
        name="gather_stream",
    )(patch_rows, w_in, w_qkv, w_out, vectors)


def own_kernel(pos_ref, normed_ref, q_ref, k_ref, v_ref, *outs):
    step = pl.program_id(0)
    weight = jnp.concatenate([ref[...].reshape(normed_ref.shape[1], LANES) for ref in (q_ref, k_ref, v_ref)], axis=1)
    product = three(nn, split_bf(normed_ref[...]), split_bf(weight))
    for i, ref in enumerate(outs):
        @pl.when(step == i)
        def _(ref=ref):
            ref[...] = product


def project_own(position, normed, qkv_full):
    rows, width = normed.shape
    owners, columns = qkv_full.shape[:4], qkv_full.shape[4]
    group = columns // 6
    return pl.pallas_call(
        own_kernel,
        grid_spec=pltpu.PrefetchScalarGridSpec(
            num_scalar_prefetch=1,
            grid=(3,),
            in_specs=[
                pl.BlockSpec((rows, width), lambda g, pos: (0, 0)),
                pl.BlockSpec(owners + (LANES,), lambda g, pos: (0, 0, 0, 0, pos[0] * 3 + g)),
                pl.BlockSpec(owners + (LANES,), lambda g, pos: (0, 0, 0, 0, 6 + pos[0] * 3 + g)),
                pl.BlockSpec(owners + (LANES,), lambda g, pos: (0, 0, 0, 0, 12 + pos[0] * 3 + g)),
            ],
            out_specs=[pl.BlockSpec((rows, group), lambda g, pos: (0, 0))] * 3,
        ),
        out_shape=[jax.ShapeDtypeStruct((rows, group), F32)] * 3,
        cost_estimate=pl.CostEstimate(flops=3 * rows * width * columns, bytes_accessed=8 * 10**6, transcendentals=0),
        compiler_params=pltpu.CompilerParams(vmem_limit_bytes=40 * 1024 * 1024),
        name="project_own",
    )(position, normed, qkv_full, qkv_full, qkv_full)


def gelu_and_slope(values):
    root = 0.7978845608028654
    square = values * values
    bent = jnp.tanh(root * (values + 0.044715 * values * square))
    half = 0.5 + 0.5 * bent
    slope = half + 0.5 * values * (1.0 - bent * bent) * (root * (1.0 + 0.134145 * square))
    return values * half, slope


def norm_back(grad, values, gain):
    zhat, scale = normalized(values)
    scaled = grad * gain
    back = scale * (
        scaled - jnp.mean(scaled, axis=-1, keepdims=True) - zhat * jnp.mean(scaled * zhat, axis=-1, keepdims=True)
    )
    return back, jnp.sum(grad * zhat, axis=0, keepdims=True), jnp.sum(grad, axis=0, keepdims=True)


def residual_kernel(pos_ref, *refs):
    own_parts, in_parts = refs[0:3], refs[3:6]
    (stream_ref, cot_ref, out_ref, vectors_ref,
     residual_ref, norm_high, norm_low, cot_high, cot_low, turned_ref, attended_ref) = refs[6:]
    half = out_ref.shape[0] // 2
    own = pl.ds(pl.multiple_of(pos_ref[0] * half, half), half)
    other = pl.ds(pl.multiple_of((1 - pos_ref[0]) * half, half), half)
    total = stream_ref[...]
    for span, parts in ((own, own_parts), (other, in_parts)):
        left = jnp.concatenate([part[...] for part in parts], axis=1)
        attended_ref[span, :] = jnp.transpose(left)
        total = total + three(nn, split_bf(left), split_bf(out_ref[span, :]))
    residual_ref[...] = total
    zhat, _ = normalized(total)
    normed = zhat * vectors_ref[2:3, :] + vectors_ref[3:4, :]
    turned_ref[...] = jnp.transpose(normed)
    norm_high[...], norm_low[...] = split_bf(normed)
    cot_high[...], cot_low[...] = split_bf(cot_ref[...])


def residual_norm(position, out_own, out_in, stream, cotangent, w_out, vectors):
    rows, width = stream.shape
    vmem = pl.BlockSpec(memory_space=pltpu.VMEM)

    def array(*shape, kind=F32):
        return jax.ShapeDtypeStruct(shape, kind)

    return pl.pallas_call(
        residual_kernel,
        in_specs=[pl.BlockSpec(memory_space=pltpu.SMEM)] + [vmem] * 10,
        out_specs=[vmem] * 7,
        out_shape=[array(rows, width)] + [array(rows, width, kind=BF)] * 4 + [array(width, rows)] * 2,
        cost_estimate=pl.CostEstimate(flops=6 * rows * width * width, bytes_accessed=18 * 10**6, transcendentals=0),
        compiler_params=pltpu.CompilerParams(vmem_limit_bytes=40 * 1024 * 1024),
        name="residual_norm",
    )(position, *out_own, *out_in, stream, cotangent, w_out, vectors)


def middle_kernel(pos_ref, *refs):
    (residual, norm_high, norm_low, cot_high, cot_low, cot_ref, out_ref, vectors_ref, up_ref, down_ref,
     block_ref, grad_pre_ref, grad_down_ref, grad_resid_ref) = refs[:14]
    sent_refs, own_refs, sums_ref, grad_norm = refs[14:17], refs[17:20], refs[20], refs[21]
    step = pl.program_id(0)
    width = out_ref.shape[0]
    half = width // 2
    own = pl.ds(pl.multiple_of(pos_ref[0] * half, half), half)
    other = pl.ds(pl.multiple_of((1 - pos_ref[0]) * half, half), half)

    @pl.when(step == 0)
    def _():
        block_ref[...] = residual[...]
        grad_norm[...] = jnp.zeros_like(grad_norm)

    up = split_bf(up_ref[...].reshape(width, width))
    hidden, slope = gelu_and_slope(three(nn, (norm_high[...], norm_low[...]), up))
    down = split_bf(down_ref[...].reshape(width, width))
    cot = (cot_high[...], cot_low[...])
    grad_pre = three(nt, cot, down) * slope
    grad_pre_ref[...] = grad_pre
    parts = split_bf(hidden)
    block_ref[...] = block_ref[...] + three(nn, parts, down)
    grad_down_ref[...] = three(tn, parts, cot).reshape(grad_down_ref.shape)
    grad_norm[...] = grad_norm[...] + three(nt, split_bf(grad_pre), up)

    @pl.when(step == pl.num_programs(0) - 1)
    def _():
        back, gain, offset = norm_back(grad_norm[...], residual[...], vectors_ref[2:3, :])
        grad = cot_ref[...] + back
        grad_resid_ref[...] = grad
        sums_ref[...] = jnp.zeros_like(sums_ref)
        sums_ref[2:3, :] = gain
        sums_ref[3:4, :] = offset
        left = split_bf(grad)
        for span, outs in ((other, sent_refs), (own, own_refs)):
            product = three(nt, left, split_bf(out_ref[span, :]))
            for i, ref in enumerate(outs):
                ref[...] = product[:, i * LANES:(i + 1) * LANES]


def middle(position, residual, norm, cot, cotangent, w_out, vectors, weights):
    rows, width = residual.shape
    owners, stacked = weights.shape[0], weights.shape[1]
    piece = width // owners
    steps = stacked // piece // 2
    whole = lambda *shape: pl.BlockSpec(shape, lambda j, *_: (0,) * len(shape))
    array = lambda *shape: jax.ShapeDtypeStruct(shape, F32)
    head = whole(rows, LANES)
    return pl.pallas_call(
        middle_kernel,
        grid_spec=pltpu.PrefetchScalarGridSpec(
            num_scalar_prefetch=1,
            grid=(steps,),
            in_specs=[whole(rows, width)] * 6 + [
                whole(width, width), whole(*vectors.shape),
                pl.BlockSpec((owners, piece, width), lambda j, *_: (0, j, 0)),
                pl.BlockSpec((owners // steps, steps * piece, width), lambda j, *_: (j, 1, 0)),
            ],
            out_specs=[
                whole(rows, width),
                pl.BlockSpec((rows, width), lambda j, *_: (0, j)),
                pl.BlockSpec((owners // steps, steps * piece, width), lambda j, *_: (j, 0, 0)),
                whole(rows, width),
            ] + [head] * 6 + [whole(*vectors.shape)],
            scratch_shapes=[pltpu.VMEM((rows, width), F32)],
        ),
        out_shape=[
            array(rows, width), array(rows, steps * width), array(owners, steps * piece, width), array(rows, width),
        ] + [array(rows, LANES)] * 6 + [array(*vectors.shape)],
        cost_estimate=pl.CostEstimate(
            flops=6 * rows * width * width * (5 * steps + 1), bytes_accessed=60 * 10**6, transcendentals=rows * steps * width
        ),
        compiler_params=pltpu.CompilerParams(vmem_limit_bytes=62 * 1024 * 1024),
        name="feed_forward",
    )(position, residual, *norm, *cot, cotangent, w_out, vectors, weights, weights)


def fast_shards(
    patches, segments, w_in, norm1_gain, norm1_bias, w_qkv, w_out, norm2_gain, norm2_bias, w_up, w_down, cotangent
):
    _, rows, patch_width = patches.shape
    piece, width = w_out.shape
    hidden = w_up.shape[1]
    owners = lax.axis_size("fsdp")
    position = lax.axis_index("sp")
    index = lax.axis_index("fsdp")
    places = position[None].astype(jnp.int32)
    labels = segments[0]
    length = labels.shape[0]
    labels_wide = jnp.broadcast_to(labels[:, None], (length, LANES))
    labels_row = labels.reshape(length // BLOCK, 1, BLOCK)
    blocks = hidden // width
    swap = [(0, 1), (1, 0)]

    vectors_own = jnp.tile(jnp.stack([norm1_gain, norm1_bias, norm2_gain, norm2_bias] + [norm1_gain] * 4), (1, owners))
    vectors_own = jnp.where(jnp.arange(width)[None, :] // piece == index, vectors_own, 0.0)
    (stream, normed, normed_turned, patches_turned, in_full, qkv_full, out_full, vectors, *sent) = gather_stream(
        patches[0], w_in, w_qkv, w_out, vectors_own
    )
    up_own = w_up.reshape(piece, blocks, width).transpose(1, 0, 2).reshape(blocks * piece, width)
    stacked = jnp.concatenate([up_own, w_down], axis=0)
    stacked, _ = lax.optimization_barrier((stacked, vectors))
    weights = lax.all_gather(stacked, "fsdp", axis=0, tiled=True).reshape(owners, 2 * blocks * piece, width)
    received = [lax.ppermute(part, "sp", swap) for part in sent]
    own = project_own(places, normed, qkv_full)
    attended = [attend_forward(a, b, places, labels, labels_wide, labels_row) for a, b in zip(own, received)]
    out_in = [lax.ppermute(part[1], "sp", swap) for part in attended]
    w_out_full = out_full.reshape(width, width)
    residual, *split, normed_two_turned, attended_turned = residual_norm(
        places, [part[0] for part in attended], out_in, stream, cotangent[0], w_out_full, vectors
    )
    block_out, grad_pre, grad_down, grad_resid, *grads = middle(
        places, residual, split[:2], split[2:], cotangent[0], w_out_full, vectors, weights
    )
    grad_sent, grad_own, sums = grads[:3], grads[3:6], grads[6]
    down_part = lax.psum_scatter(
        grad_down.reshape(hidden, width), "fsdp", scatter_dimension=0, tiled=True
    )
    grad_in = [lax.ppermute(part, "sp", swap) for part in grad_sent]
    both = [
        attend_backward(own[i], received[i], attended[i][0], attended[i][1], grad_own[i], grad_in[i], attended[i][2],
                        places, labels, labels_wide, labels_row)
        for i in range(3)
    ]
    mine = [pair[0] for pair in both]
    got = lax.ppermute(both[0][1], "sp", swap)
    grad_up, grad_out, grad_qkv, grad_w_in, grad_patch, vector_sums = back_and_reduce(
        [normed_two_turned, attended_turned, normed_turned, patches_turned], grad_pre, grad_resid,
        mine, got, [both[1][1], both[2][1]], qkv_full, stream, in_full.reshape(owners, in_full.shape[3], width), vectors, sums,
    )
    vector_sums = lax.dynamic_slice(vector_sums, (0, index * piece), (4, piece))
    down_part, _ = lax.optimization_barrier((down_part, grad_out))
    total_down = down_part + lax.ppermute(down_part, "sp", swap)
    grad_patch = grad_patch * lax.optimization_barrier(jnp.float32(1.0))
    return (
        block_out[None], grad_patch[None], grad_w_in, vector_sums[0], vector_sums[1],
        grad_qkv, grad_out, vector_sums[2], vector_sums[3], grad_up, total_down,
    )


def solution(mesh):
    sharded = P("fsdp", "sp", None)
    matrix = P("fsdp", None)
    vector = P("fsdp")
    fast = mesh.shape["fsdp"] == 16 and mesh.shape["sp"] == 2
    return jax.shard_map(
        fast_shards if fast else shards,
        mesh=mesh,
        in_specs=(sharded, matrix, matrix, vector, vector, matrix, matrix, vector, vector, matrix, matrix, sharded),
        out_specs=(sharded, sharded, matrix, vector, vector, matrix, matrix, vector, vector, matrix, matrix),
        check_vma=False,
    )
```

```python
import functools

import jax
import jax.numpy as jnp
from jax import lax
from jax.experimental import pallas as pl
from jax.experimental.pallas import tpu as pltpu
from jax.sharding import PartitionSpec as P

HEADS = 12


EPSILON = 1e-05


def matmul(left_side, right_side):
    return jnp.dot(
        left_side, right_side, precision=lax.Precision.HIGH, preferred_element_type=jnp.float32
    )


def matmul_tn(left_side, right_side):
    return lax.dot_general(
        left_side,
        right_side,
        (((0,), (0,)), ((), ())),
        precision=lax.Precision.HIGH,
        preferred_element_type=jnp.float32,
    )


def matmul_nt(left_side, right_side):
    return lax.dot_general(
        left_side,
        right_side,
        (((1,), (1,)), ((), ())),
        precision=lax.Precision.HIGH,
        preferred_element_type=jnp.float32,
    )


def layer_norm(values, scaling, offset):
    average = jnp.mean(values, axis=-1, keepdims=True)
    centred = values - average
    spread = jnp.mean(centred * centred, axis=-1, keepdims=True)
    return centred * lax.rsqrt(spread + EPSILON) * scaling + offset


def gelu_tanh(values):
    return jax.nn.gelu(values, approximate=True)


def scored(queries, key_rows, labels):
    length = labels.shape[0]
    factor = queries.shape[-1] ** (-0.5)
    raw_scores = matmul_nt(queries, key_rows) * factor
    places = jnp.arange(length, dtype=jnp.int32)
    allowed = (labels[:, None] == labels[None, :]) & (places[None, :] <= places[:, None])
    return (raw_scores, allowed, factor)


def attend_one(packed):
    queries, key_rows, value_rows, labels = packed
    raw_scores, allowed, factor = scored(queries, key_rows, labels)
    masked = jnp.where(allowed, raw_scores, -1e30)
    row_max = jnp.max(masked, axis=1, keepdims=True)
    exponent = jnp.exp(masked - row_max)
    summed = jnp.sum(exponent, axis=1, keepdims=True)
    attended = matmul(exponent / summed, value_rows)
    return (attended, (row_max + jnp.log(summed))[:, 0])


def attend_back(packed):
    queries, key_rows, value_rows, attended, log_total, grad_attended, labels = packed
    raw_scores, allowed, factor = scored(queries, key_rows, labels)
    weights = jnp.where(
        allowed, jnp.exp(jnp.where(allowed, raw_scores - log_total[:, None], -1e30)), 0.0
    )
    grad_values = matmul_tn(weights, grad_attended)
    grad_weights = matmul_nt(grad_attended, value_rows)
    row_dot = jnp.sum(grad_attended * attended, axis=1, keepdims=True)
    grad_scores = weights * (grad_weights - row_dot) * factor
    grad_queries = matmul(grad_scores, key_rows)
    grad_keys = matmul_tn(grad_scores, queries)
    return (grad_queries, grad_keys, grad_values)


def to_batch(blocked, heads_local):
    seq_count, length, columns = blocked.shape
    head_dim = columns // heads_local
    return (
        blocked.reshape(seq_count, length, heads_local, head_dim)
        .transpose(0, 2, 1, 3)
        .reshape(seq_count * heads_local, length, head_dim)
    )


def from_batch(blocked, seq_count):
    batch_size, length, head_dim = blocked.shape
    heads_local = batch_size // seq_count
    return (
        blocked.reshape(seq_count, heads_local, length, head_dim)
        .transpose(0, 2, 1, 3)
        .reshape(seq_count, length, heads_local * head_dim)
    )


def shards(
    patches,
    segments,
    w_in,
    norm1_gain,
    norm1_bias,
    w_qkv,
    w_out,
    norm2_gain,
    norm2_bias,
    w_up,
    w_down,
    cotangent,
):
    seq_count, local_len, patch_width = patches.shape
    model_width = w_out.shape[1]
    heads_local = HEADS // lax.axis_size("sp")
    row_count = seq_count * local_len
    norm_params = jnp.stack([norm1_gain, norm1_bias, norm2_gain, norm2_bias])
    gathered = (
        lax.all_gather(w_in, "fsdp", axis=0, tiled=True),
        lax.all_gather(w_qkv, "fsdp", axis=0, tiled=True),
        lax.all_gather(w_out, "fsdp", axis=0, tiled=True),
        lax.all_gather(w_up, "fsdp", axis=0, tiled=True),
        lax.all_gather(w_down, "fsdp", axis=0, tiled=True),
        lax.all_gather(norm_params, "fsdp", axis=1, tiled=True),
    )
    in_full, qkv_full, out_full, up_full, down_full, norm_full = gathered
    patch_rows = patches.reshape(row_count, patch_width)
    stream = matmul(patch_rows, in_full)
    normed, norm1_pull = jax.vjp(layer_norm, stream, norm_full[0], norm_full[1])
    projected = matmul(normed, qkv_full)
    query_tok = projected[:, :model_width].reshape(seq_count, local_len, model_width)
    key_tok = projected[:, model_width : 2 * model_width].reshape(seq_count, local_len, model_width)
    value_tok = projected[:, 2 * model_width :].reshape(seq_count, local_len, model_width)
    query_seq, key_seq, value_seq = (
        lax.all_to_all(query_tok, "sp", split_axis=2, concat_axis=1, tiled=True),
        lax.all_to_all(key_tok, "sp", split_axis=2, concat_axis=1, tiled=True),
        lax.all_to_all(value_tok, "sp", split_axis=2, concat_axis=1, tiled=True),
    )
    labels = jnp.repeat(segments, heads_local, axis=0)
    query_batch = to_batch(query_seq, heads_local)
    key_batch = to_batch(key_seq, heads_local)
    value_batch = to_batch(value_seq, heads_local)
    attended, log_total = lax.map(attend_one, (query_batch, key_batch, value_batch, labels))
    attended_tok = lax.all_to_all(
        from_batch(attended, seq_count), "sp", split_axis=1, concat_axis=2, tiled=True
    )
    attended_rows = attended_tok.reshape(row_count, model_width)
    residual = stream + matmul(attended_rows, out_full)
    normed_two, norm2_pull = jax.vjp(layer_norm, residual, norm_full[2], norm_full[3])
    hidden_pre = matmul(normed_two, up_full)
    hidden, gelu_pull = jax.vjp(gelu_tanh, hidden_pre)
    result = residual + matmul(hidden, down_full)
    block_out = result.reshape(seq_count, local_len, model_width)
    in_back, qkv_back, out_back, up_back, down_back = (
        lax.all_gather(w_in, "fsdp", axis=0, tiled=True),
        lax.all_gather(w_qkv, "fsdp", axis=0, tiled=True),
        lax.all_gather(w_out, "fsdp", axis=0, tiled=True),
        lax.all_gather(w_up, "fsdp", axis=0, tiled=True),
        lax.all_gather(w_down, "fsdp", axis=0, tiled=True),
    )
    grad_rows = cotangent.reshape(row_count, model_width)
    grad_down = matmul_tn(hidden, grad_rows)
    (grad_pre,) = gelu_pull(matmul_nt(grad_rows, down_back))
    grad_up = matmul_tn(normed_two, grad_pre)
    grad_resid_norm, grad_gain_two, grad_offset_two = norm2_pull(matmul_nt(grad_pre, up_back))
    grad_resid = grad_rows + grad_resid_norm
    grad_out = matmul_tn(attended_rows, grad_resid)
    grad_att = matmul_nt(grad_resid, out_back).reshape(seq_count, local_len, model_width)
    grad_att_seq = lax.all_to_all(grad_att, "sp", split_axis=2, concat_axis=1, tiled=True)
    grad_query, grad_key, grad_value = lax.map(
        attend_back,
        (
            query_batch,
            key_batch,
            value_batch,
            attended,
            log_total,
            to_batch(grad_att_seq, heads_local),
            labels,
        ),
    )
    back_query, back_key, back_value = (
        lax.all_to_all(
            from_batch(grad_query, seq_count), "sp", split_axis=1, concat_axis=2, tiled=True
        ),
        lax.all_to_all(
            from_batch(grad_key, seq_count), "sp", split_axis=1, concat_axis=2, tiled=True
        ),
        lax.all_to_all(
            from_batch(grad_value, seq_count), "sp", split_axis=1, concat_axis=2, tiled=True
        ),
    )
    grad_proj = jnp.concatenate([back_query, back_key, back_value], axis=2).reshape(
        row_count, 3 * model_width
    )
    grad_qkv = matmul_tn(normed, grad_proj)
    grad_stream_norm, grad_gain_one, grad_offset_one = norm1_pull(matmul_nt(grad_proj, qkv_back))
    grad_stream = grad_resid + grad_stream_norm
    grad_in = matmul_tn(patch_rows, grad_stream)
    grad_patch = matmul_nt(grad_stream, in_back).reshape(seq_count, local_len, patch_width)
    every_part = (
        lax.psum_scatter(grad_in, "fsdp", scatter_dimension=0, tiled=True),
        lax.psum_scatter(grad_qkv, "fsdp", scatter_dimension=0, tiled=True),
        lax.psum_scatter(grad_out, "fsdp", scatter_dimension=0, tiled=True),
        lax.psum_scatter(grad_up, "fsdp", scatter_dimension=0, tiled=True),
        lax.psum_scatter(grad_down, "fsdp", scatter_dimension=0, tiled=True),
        lax.psum_scatter(
            jnp.stack([grad_gain_one, grad_offset_one, grad_gain_two, grad_offset_two]),
            "fsdp",
            scatter_dimension=1,
            tiled=True,
        ),
    )
    total_in, total_qkv, total_out, total_up, total_down, norm_total = lax.psum(
        (every_part[0], every_part[1], every_part[2], every_part[3], every_part[4], every_part[5]),
        "sp",
    )
    norm_first = norm_total[0:2]
    norm_second = norm_total[2:4]
    return (
        block_out,
        grad_patch,
        total_in,
        norm_first[0],
        norm_first[1],
        total_qkv,
        total_out,
        norm_second[0],
        norm_second[1],
        total_up,
        total_down,
    )


LANES = 128
BLOCK = 256
BF = jnp.bfloat16
F32 = jnp.float32


def halves(values):
    high = values.astype(BF).astype(F32)
    return high, values - high


def roll_half(values):
    return pltpu.roll(values, LANES // 2, 1)


def low_lanes(rows):
    return lax.broadcasted_iota(jnp.int32, (rows, LANES), 1) < LANES // 2


def pair_tiles(values):
    high, low = halves(values)
    first = low_lanes(values.shape[0])
    return (
        jnp.where(first, high, roll_half(low)).astype(BF),
        jnp.where(first, roll_half(high), low).astype(BF),
    )


def spread_tiles(values):
    high, low = halves(values)
    first = low_lanes(values.shape[0])
    high_r, low_r = roll_half(high), roll_half(low)
    return (
        jnp.concatenate([jnp.where(first, high, high_r), jnp.where(first, low, low_r)], axis=1).astype(BF),
        jnp.concatenate([jnp.where(first, high_r, high), jnp.where(first, low_r, low)], axis=1).astype(BF),
    )


def nt(left, right):
    return lax.dot_general(left, right, (((1,), (1,)), ((), ())), preferred_element_type=F32)


def nn(left, right):
    return lax.dot_general(left, right, (((1,), (0,)), ((), ())), preferred_element_type=F32)


def tn(left, right):
    return lax.dot_general(left, right, (((0,), (0,)), ((), ())), preferred_element_type=F32)


def split_bf(values):
    high = values.astype(BF)
    return high, (values - high.astype(F32)).astype(BF)


def forward_kernel(pos_ref, seg_ref, *refs):
    (own_ref, in_ref, seg_col, seg_row,
     o_own, o_out, lse_ref, tq, hk, tv, out_s) = refs
    rows = own_ref.shape[0]
    own = pl.multiple_of(pos_ref[0] * rows, rows)
    other = pl.multiple_of((1 - pos_ref[0]) * rows, rows)
    for place, ref in ((own, own_ref), (other, in_ref)):
        span = pl.ds(place, rows)
        q, k, v = (ref.at[:, i * LANES:(i + 1) * LANES] for i in range(3))
        for head, tile in enumerate(pair_tiles(q[...] * 0.125)):
            tq[head, span, :] = jnp.concatenate([tile, tile], axis=1)
        for head, tile in enumerate(spread_tiles(k[...])):
            hk[head, span, :] = tile
        for head, tile in enumerate(pair_tiles(v[...])):
            tv[head, span, :] = tile
    blocks = 2 * rows // BLOCK
    first = low_lanes(BLOCK)

    def query_block(i, carry):
        q_span = pl.ds(pl.multiple_of(i * BLOCK, BLOCK), BLOCK)
        first_label = seg_ref[i * BLOCK]
        start = jnp.int32(0)
        for j in range(blocks):
            start = start + jnp.where((j < i) & (seg_ref[j * BLOCK + BLOCK - 1] < first_label), 1, 0)
        label = seg_col[q_span, :1]
        q_place = i * BLOCK + lax.broadcasted_iota(jnp.int32, (BLOCK, BLOCK), 0)

        def key_block(step, state):
            j = i - step
            k_span = pl.ds(pl.multiple_of(j * BLOCK, BLOCK), BLOCK)
            k_place = j * BLOCK + lax.broadcasted_iota(jnp.int32, (BLOCK, BLOCK), 1)
            allowed = (label == seg_row[j]) & (k_place <= q_place)
            new_state = []
            for head in range(2):
                top, total, acc = state[head]
                scores = nt(tq[head, q_span, :], hk[head, k_span, :])
                scores = jnp.where(allowed, scores, -1e30)
                new_top = jnp.maximum(top, jnp.max(scores, axis=1, keepdims=True))
                weight = jnp.exp(scores - new_top)
                keep = jnp.exp(top - new_top)
                high, low = split_bf(weight)
                values = tv[head, k_span, :]
                new_state.append((
                    new_top,
                    total * keep + jnp.sum(weight, axis=1, keepdims=True),
                    acc * keep + nn(high, values) + nn(low, values),
                ))
            return tuple(new_state)

        init = (
            jnp.full((BLOCK, 1), -1e30, F32),
            jnp.zeros((BLOCK, 1), F32),
            jnp.zeros((BLOCK, LANES), F32),
        )
        state = lax.fori_loop(0, i - start + 1, key_block, (init, init))
        outs, logs = [], []
        for top, total, acc in state:
            outs.append((acc + roll_half(acc)) / total)
            logs.append(jnp.broadcast_to(top + jnp.log(total), (BLOCK, LANES)))
        out_s[q_span, :] = jnp.where(first, outs[0], outs[1])
        lse_ref[q_span, :] = jnp.where(first, logs[0], logs[1])
        return carry

    lax.fori_loop(0, blocks, query_block, 0)
    o_own[...] = out_s[pl.ds(own, rows), :]
    o_out[...] = out_s[pl.ds(other, rows), :]


def attend_forward(own, received, position, labels, labels_wide, labels_row):
    rows = own.shape[0]
    length = 2 * rows
    smem = pl.BlockSpec(memory_space=pltpu.SMEM)
    whole = lambda *shape: pl.BlockSpec(shape, lambda i: (0,) * len(shape))
    return pl.pallas_call(
        forward_kernel,
        grid=(1,),
        in_specs=[smem, smem, whole(rows, 3 * LANES), whole(rows, 3 * LANES), whole(length, LANES), whole(length // BLOCK, 1, BLOCK)],
        out_specs=[whole(rows, LANES), whole(rows, LANES), whole(length, LANES)],
        scratch_shapes=[
            pltpu.VMEM((2, length, 2 * LANES), BF),
            pltpu.VMEM((2, length, 2 * LANES), BF),
            pltpu.VMEM((2, length, LANES), BF),
            pltpu.VMEM((length, LANES), F32),
        ],
        out_shape=[
            jax.ShapeDtypeStruct((rows, LANES), F32),
            jax.ShapeDtypeStruct((rows, LANES), F32),
            jax.ShapeDtypeStruct((length, LANES), F32),
        ],
        cost_estimate=pl.CostEstimate(flops=6 * 10**9, bytes_accessed=28 * rows * LANES, transcendentals=length * length),
        compiler_params=pltpu.CompilerParams(vmem_limit_bytes=32 * 1024 * 1024),
        name="attend_forward",
    )(position, labels, own, received, labels_wide, labels_row)


def backward_kernel(pos_ref, seg_ref, *refs):
    (own_ref, in_ref, o_own, o_in, g_own, g_in, lse_ref, seg_col, seg_row,
     grad_own, grad_out,
     tq, hk, tk, hv, tg, lse_t, delta_t, gq_s, gk_s, gv_s) = refs
    rows = own_ref.shape[0]
    length = 2 * rows
    own = pl.multiple_of(pos_ref[0] * rows, rows)
    other = pl.multiple_of((1 - pos_ref[0]) * rows, rows)
    half = LANES // 2
    for place, ref, o, g in ((own, own_ref, o_own, g_own), (other, in_ref, o_in, g_in)):
        span = pl.ds(place, rows)
        q, k, v = (ref.at[:, i * LANES:(i + 1) * LANES] for i in range(3))
        for head, tile in enumerate(pair_tiles(q[...] * 0.125)):
            tq[head, span, :] = jnp.concatenate([tile, tile], axis=1)
        for head, tile in enumerate(pair_tiles(g[...])):
            tg[head, span, :] = jnp.concatenate([tile, tile], axis=1)
        for head, tile in enumerate(spread_tiles(k[...])):
            hk[head, span, :] = tile
        for head, tile in enumerate(spread_tiles(v[...])):
            hv[head, span, :] = tile
        for head, tile in enumerate(pair_tiles(k[...])):
            tk[head, span, :] = tile
        turned = jnp.transpose(o[...] * g[...])
        for head in range(2):
            delta_t[head, 0:1, span] = jnp.sum(turned[head * half:(head + 1) * half], axis=0, keepdims=True)
    turned = jnp.transpose(lse_ref[...])
    for head in range(2):
        lse_t[head, 0:1, :] = turned[head * half:head * half + 1]
    blocks = length // BLOCK
    first = low_lanes(BLOCK)
    gq_s[...] = jnp.zeros_like(gq_s)

    def key_block(j, carry):
        k_span = pl.ds(pl.multiple_of(j * BLOCK, BLOCK), BLOCK)
        last_label = seg_ref[j * BLOCK + BLOCK - 1]
        count = jnp.int32(1)
        for i in range(blocks):
            count = count + jnp.where((i > j) & (seg_ref[i * BLOCK] <= last_label), 1, 0)
        label = seg_col[k_span, :1]
        k_place = j * BLOCK + lax.broadcasted_iota(jnp.int32, (BLOCK, BLOCK), 0)

        def query_block(step, state):
            i = j + step
            q_span = pl.ds(pl.multiple_of(i * BLOCK, BLOCK), BLOCK)
            q_place = i * BLOCK + lax.broadcasted_iota(jnp.int32, (BLOCK, BLOCK), 1)
            allowed = (label == seg_row[i]) & (k_place <= q_place)
            new_state = []
            for head in range(2):
                grad_k, grad_v = state[head]
                query = tq[head, q_span, :]
                grad = tg[head, q_span, :]
                scores = nt(hk[head, k_span, :], query)
                weight = jnp.exp(jnp.where(allowed, scores - lse_t[head, 0:1, q_span], -1e30))
                grad_weight = nt(hv[head, k_span, :], grad)
                grad_score = weight * (grad_weight - delta_t[head, 0:1, q_span])
                w_high, w_low = split_bf(weight)
                s_high, s_low = split_bf(grad_score)
                grad_v = grad_v + nn(w_high, grad[:, :LANES]) + nn(w_low, grad[:, :LANES])
                grad_k = grad_k + nn(s_high, query[:, :LANES]) + nn(s_low, query[:, :LANES])
                keys = tk[head, k_span, :]
                gq_s[head, q_span, :] += tn(s_high, keys) + tn(s_low, keys)
                new_state.append((grad_k, grad_v))
            return tuple(new_state)

        zero = jnp.zeros((BLOCK, LANES), F32)
        state = lax.fori_loop(0, count, query_block, ((zero, zero), (zero, zero)))
        for slot, store in ((0, gk_s), (1, gv_s)):
            left, right = state[0][slot], state[1][slot]
            store[k_span, :] = jnp.where(first, left + roll_half(left), right + roll_half(right))
        return carry

    lax.fori_loop(0, blocks, key_block, 0)
    wide = low_lanes(rows)
    for place, ref in ((own, grad_own), (other, grad_out)):
        span = pl.ds(place, rows)
        left, right = gq_s[0, span, :], gq_s[1, span, :]
        ref[:, :LANES] = jnp.where(wide, left + roll_half(left), right + roll_half(right)) * 0.125
        ref[:, LANES:2 * LANES] = gk_s[span, :]
        ref[:, 2 * LANES:] = gv_s[span, :]


def attend_backward(own, received, out_own, out_in, grad_own, grad_in, logs, position, labels, labels_wide, labels_row):
    rows = own.shape[0]
    length = 2 * rows
    smem = pl.BlockSpec(memory_space=pltpu.SMEM)
    whole = lambda *shape: pl.BlockSpec(shape, lambda i: (0,) * len(shape))
    return pl.pallas_call(
        backward_kernel,
        grid=(1,),
        in_specs=[smem, smem, whole(rows, 3 * LANES), whole(rows, 3 * LANES)] + [whole(rows, LANES)] * 4
        + [whole(length, LANES), whole(length, LANES), whole(length // BLOCK, 1, BLOCK)],
        out_specs=[whole(rows, 3 * LANES)] * 2,
        scratch_shapes=[
            pltpu.VMEM((2, length, 2 * LANES), BF),
            pltpu.VMEM((2, length, 2 * LANES), BF),
            pltpu.VMEM((2, length, LANES), BF),
            pltpu.VMEM((2, length, 2 * LANES), BF),
            pltpu.VMEM((2, length, 2 * LANES), BF),
            pltpu.VMEM((2, 8, length), F32),
            pltpu.VMEM((2, 8, length), F32),
            pltpu.VMEM((2, length, LANES), F32),
            pltpu.VMEM((length, LANES), F32),
            pltpu.VMEM((length, LANES), F32),
        ],
        out_shape=[pltpu.HBM((rows, 3 * LANES), F32)] * 2,
        cost_estimate=pl.CostEstimate(flops=13 * 10**9, bytes_accessed=60 * rows * LANES, transcendentals=length * length),
        compiler_params=pltpu.CompilerParams(vmem_limit_bytes=40 * 1024 * 1024),
        name="attend_backward",
    )(position, labels, own, received, out_own, out_in, grad_own, grad_in, logs, labels_wide, labels_row)


MESH = pl.DeviceIdType.MESH
PIECE = 48
FLAT_PAIRS = 2


def back_kernel(plan, *refs):
    up_units, out_units, qkv_units, in_units = plan
    units = sum(plan)
    pairs = units // 2
    first_qkv = up_units + out_units
    first_in = first_qkv + qkv_units
    (up_turned, out_turned, qkv_turned, in_turned, grad_pre, grad_resid, mine_0, mine_1, mine_2, got_0, sent_1, sent_2,
     qkv_ref, stream_ref, weight_ref, vectors_ref, sums_ref,
     up_total, out_total, qkv_total, in_total, patch_ref, norm_total_ref, got_1, got_2,
     t_buf, g_buf, g_high, g_low, part, s_high, s_low, w_buf, p_buf, q_buf, acc, land_a, n_x, n_z, n_y, y_y, y_x, y_z, done,
     v_own, v_c, v_x, v_y, v_z,
     load_sem, w_sem, p_sem, q_sem, norm_sem, swap_sem,
     a_sem, nx_sem, nz_sem, ny_sem, yy_sem, yx_sem, yz_sem, ye_sem, v_sem, o_sem) = refs
    mine, got = (mine_0, mine_1, mine_2), (got_0, got_1, got_2)
    width = g_buf.shape[2]
    fsdp = lax.axis_index("fsdp")
    row = lax.axis_index("sp")
    z, x, core = fsdp // 4, (fsdp // 2) % 2, fsdp % 2
    half = PIECE // 2

    def device(z_at, x_at, core_at, row_at):
        return ((z_at * 2 + x_at) * 2 + core_at, row_at)

    sibling = device(z, x, 1 - core, row)
    beside = device(z, 1 - x, core, row)
    across = device(z, x, core, 1 - row)
    along = [device((z + step) % 4, x, core, row) for step in (1, 2, 3)]

    barrier = pltpu.get_barrier_semaphore()
    for peer in [sibling, beside, across] + along:
        pl.semaphore_signal(barrier, inc=1, device_id=peer, device_id_type=MESH)

    def remote(source, target, sems, index, peer):
        return pltpu.make_async_remote_copy(
            src_ref=source, dst_ref=target, send_sem=sems.at[(0,) + index], recv_sem=sems.at[(1,) + index],
            device_id=peer, device_id_type=MESH,
        )

    def span(first, size):
        return pl.ds(pl.multiple_of(first, size), size)

    def loop(number, body):
        def step(i, carry):
            body(i)
            return carry

        lax.fori_loop(0, number, step, 0)

    def start(copy):
        copy.start()

    def wait(copy):
        copy.wait()

    def loads(unit, slot, act):
        def left(view):
            for side in range(2):
                act(pltpu.make_async_copy(view.at[:, side], t_buf.at[slot, side], load_sem.at[slot, side]))

        def right(source):
            act(pltpu.make_async_copy(source, g_buf.at[slot], load_sem.at[slot, 2]))

        @pl.when(unit < up_units)
        def _():
            left(up_turned)
            right(grad_pre.at[:, span(unit * width, width)])

        @pl.when((unit >= up_units) & (unit < first_qkv))
        def _():
            left(out_turned)
            right(grad_resid.at[:, span((unit - up_units) * width, width)])

        @pl.when((unit >= first_qkv) & (unit < first_in))
        def _():
            left(qkv_turned)
            for j in range(qkv_units):
                kind, side = divmod(j, 2)
                for sources, own in ((mine, True), (got, False)):
                    @pl.when((unit == first_qkv + j) & ((row == side) == own))
                    def _(kind=kind, sources=sources):
                        for i, source in enumerate(sources):
                            act(pltpu.make_async_copy(
                                source.at[:, kind * LANES:(kind + 1) * LANES],
                                g_buf.at[slot, :, i * LANES:(i + 1) * LANES],
                                load_sem.at[slot, 2 + i],
                            ))

        @pl.when(unit >= first_in)
        def _():
            j = (unit - first_in) // 2
            for side in range(2):
                act(pltpu.make_async_copy(in_turned.at[:, side, j], t_buf.at[slot, side], load_sem.at[slot, side]))

    def weight_copy(block, slot):
        return pltpu.make_async_copy(weight_ref.at[block], w_buf.at[slot], w_sem.at[slot])

    def patch_copy(block, slot):
        columns = w_buf.shape[1]
        return pltpu.make_async_copy(p_buf.at[slot], patch_ref.at[:, span(block * columns, columns)], p_sem.at[slot])

    def q_copy(j):
        return pltpu.make_async_copy(qkv_ref.at[:, :, :, :, span(j * width, width)], q_buf, q_sem)

    rows = stream_ref.shape[0]
    cut = w_buf.shape[1]
    norm_copies = [
        pltpu.make_async_copy(stream_ref.at[:, 0:width], p_buf.at[0], norm_sem.at[0]),
        pltpu.make_async_copy(stream_ref.at[:, width:], p_buf.at[1], norm_sem.at[1]),
        pltpu.make_async_copy(grad_resid.at[0:cut], w_buf.at[0], norm_sem.at[2]),
        pltpu.make_async_copy(grad_resid.at[cut:], w_buf.at[1, 0:rows - cut], norm_sem.at[3]),
    ]
    swap_copies = [
        remote(sent_1, got_1, swap_sem, (0,), across),
        remote(sent_2, got_2, swap_sem, (1,), across),
    ]

    def core_copy(unit, slot):
        return remote(part.at[slot, 1 - core], land_a.at[unit], a_sem, (unit,), sibling)

    def nx_copy(unit, n):
        return remote(land_a.at[unit, :, 1 - x], n_x.at[n], nx_sem, (n,), beside)

    def nz_copy(n, step):
        return remote(n_x.at[n, (z + step + 1) % 4], n_z.at[n, step], nz_sem, (n, step), along[step])

    def ny_copy(n):
        return remote(n_x.at[n, z], n_y.at[n], ny_sem, (n,), across)

    def yy_copy(unit, p):
        return remote(land_a.at[unit, :, :, span((1 - row) * half, half)], y_y.at[p], yy_sem, (p,), across)

    def yx_copy(p):
        return remote(y_y.at[p, :, 1 - x], y_x.at[p], yx_sem, (p,), beside)

    def yz_copy(p, step):
        return remote(y_x.at[p, (z + step + 1) % 4], y_z.at[p, step], yz_sem, (p, step), along[step])

    def ye_copy(unit, p):
        return remote(y_x.at[p, z], done.at[unit, span(row * half, half)], ye_sem, (p,), across)

    def flat_number(pair):
        return pairs + pair

    def other_number(pair):
        return pair - FLAT_PAIRS

    def odd(pair, flat, other):
        @pl.when(pair < FLAT_PAIRS)
        def _():
            flat(2 * pair + 1, flat_number(pair))

        @pl.when(pair >= FLAT_PAIRS)
        def _():
            other(2 * pair + 1, other_number(pair))

    v_copies = [
        remote(v_own, v_c, v_sem, (0,), sibling),
        remote(v_c, v_x, v_sem, (1,), beside),
        remote(v_x, v_y, v_sem, (2,), across),
    ] + [remote(v_y, v_z.at[step], v_sem, (3 + step,), along[step]) for step in range(3)]

    loads(jnp.int32(0), 0, start)
    q_copy(0).start()
    for copy in norm_copies:
        copy.start()
    pl.semaphore_wait(barrier, 6)
    for copy in swap_copies:
        copy.start()

    def norm_backward():
        for copy in norm_copies:
            copy.wait()
        values = jnp.concatenate([p_buf[0], p_buf[1]], axis=1)
        back, gain, offset = norm_back(acc[...], values, vectors_ref[0:1, :])
        v_own[...] = sums_ref[...]
        v_own[0:1, :] = gain
        v_own[1:2, :] = offset
        acc[...] = back
        acc[0:cut, :] = acc[0:cut, :] + w_buf[0]
        acc[cut:, :] = acc[cut:, :] + w_buf[1, 0:rows - cut]
        s_high[...] = acc[...].astype(BF)
        s_low[...] = (acc[...] - s_high[...].astype(F32)).astype(BF)
        weight_copy(0, 0).start()
        v_copies[0].start()

    def compute(unit, slot):
        loads(unit, slot, wait)

        @pl.when(unit + 1 < units)
        def _():
            loads(unit + 1, 1 - slot, start)

        @pl.when(unit >= 2)
        def _():
            core_copy(unit - 2, slot).wait_send()

        @pl.when(unit < first_in)
        def _():
            grad = g_buf[slot]
            g_high[...] = grad.astype(BF)
            g_low[...] = (grad - g_high[...].astype(F32)).astype(BF)

        @pl.when(unit >= first_in)
        def _():
            columns = span(((unit - first_in) % 2) * width, width)
            g_high[...] = s_high[:, columns]
            g_low[...] = s_low[:, columns]

        def side_of(turn, carry):
            side = jnp.where(turn == 0, 1 - core, core)
            high, low = split_bf(t_buf[slot, side].reshape(8 * PIECE, t_buf.shape[4]))
            product = nn(high, g_high[...]) + nn(high, g_low[...]) + nn(low, g_high[...])
            part[slot, side] = product.reshape(4, 2, PIECE, product.shape[1])

            @pl.when(turn == 0)
            def _():
                core_copy(unit, slot).start()

            return carry

        lax.fori_loop(0, 2, side_of, 0)

        @pl.when((unit >= first_qkv) & (unit < first_in))
        def _():
            j = unit - first_qkv
            q_copy(j).wait()
            weight = split_bf(q_buf[...].reshape(acc.shape[1], width))
            acc[...] = acc[...] + three(nt, (g_high[...], g_low[...]), weight)

            @pl.when(j + 1 < qkv_units)
            def _():
                q_copy(j + 1).start()

    def patch_block(block, slot):
        weight_copy(block, slot).wait()

        @pl.when(block + 1 < weight_ref.shape[0])
        def _():
            weight_copy(block + 1, 1 - slot).start()

        @pl.when(block >= 2)
        def _():
            patch_copy(block - 2, slot).wait()

        p_buf[slot] = three(nt, (s_high[...], s_low[...]), split_bf(w_buf[slot]))
        patch_copy(block, slot).start()

    def after_core(unit, slot):
        core_copy(unit, slot).wait_recv()

        def add(i):
            for b in range(2):
                land_a[unit, i, b] = land_a[unit, i, b] + part[slot, core, i, b]

        loop(4, add)

    def flat_x(unit, n):
        nx_copy(unit, n).wait_recv()

        def add(i):
            n_x[n, i] = n_x[n, i] + land_a[unit, i, x]

        loop(4, add)
        for step in range(3):
            nz_copy(n, step).start()

    def flat_z(unit, n):
        for step in range(3):
            nz_copy(n, step).wait_recv()
        n_x[n, z] = n_x[n, z] + n_z[n, 0] + n_z[n, 1] + n_z[n, 2]
        ny_copy(n).start()

    def flat_y(unit, n):
        ny_copy(n).wait_recv()
        done[unit] = n_x[n, z] + n_y[n]

    def other_y(unit, p):
        yy_copy(unit, p).wait_recv()
        own = span(row * half, half)

        def add(i):
            for b in range(2):
                y_y[p, i, b] = y_y[p, i, b] + land_a[unit, i, b, own]

        loop(4, add)
        yx_copy(p).start()

    def other_x(unit, p):
        yx_copy(p).wait_recv()

        def add(i):
            y_x[p, i] = y_x[p, i] + y_y[p, i, x]

        loop(4, add)
        for step in range(3):
            yz_copy(p, step).start()

    def other_z(unit, p):
        for step in range(3):
            yz_copy(p, step).wait_recv()
        total = y_x[p, z] + y_z[p, 0] + y_z[p, 1] + y_z[p, 2]
        y_x[p, z] = total
        done[unit, span(row * half, half)] = total
        ye_copy(unit, p).start()

    acc[...] = jnp.zeros_like(acc)

    def iteration(p, carry):
        @pl.when(p == first_qkv // 2 - 1)
        def _():
            for copy in swap_copies:
                copy.wait_recv()

        @pl.when(p < pairs)
        def _():
            compute(2 * p, 0)
            compute(2 * p + 1, 1)
            after_core(2 * p, 0)
            nx_copy(2 * p, p).start()
            after_core(2 * p + 1, 1)
            odd(p, lambda unit, n: nx_copy(unit, n).start(), lambda unit, i: yy_copy(unit, i).start())

        @pl.when(p == first_in // 2 - 1)
        def _():
            norm_backward()

        q = p - 1

        @pl.when((q >= 0) & (q < pairs))
        def _():
            flat_x(2 * q, q)
            odd(q, flat_x, other_y)

        @pl.when((p >= first_in // 2) & (p < pairs))
        def _():
            patch_block(2 * p - first_in, 0)
            patch_block(2 * p - first_in + 1, 1)

        r = p - 2

        @pl.when((r >= 0) & (r < pairs))
        def _():
            flat_z(2 * r, r)
            odd(r, flat_z, other_x)

        s = p - 3

        @pl.when((s >= 0) & (s < pairs))
        def _():
            flat_y(2 * s, s)
            odd(s, flat_y, other_z)

        turn = p - first_in // 2

        @pl.when(turn == 0)
        def _():
            v_copies[0].wait_recv()
            v_c[...] = v_c[...] + v_own[...]
            v_copies[1].start()

        @pl.when(turn == 1)
        def _():
            v_copies[1].wait_recv()
            v_x[...] = v_x[...] + v_c[...]
            v_copies[2].start()

        @pl.when(turn == 2)
        def _():
            v_copies[2].wait_recv()
            v_y[...] = v_y[...] + v_x[...]
            for step in range(3):
                v_copies[3 + step].start()

        @pl.when(turn == 3)
        def _():
            for step in range(3):
                v_copies[3 + step].wait_recv()
            norm_total_ref[...] = v_y[...] + v_z[0] + v_z[1] + v_z[2]

        return carry

    lax.fori_loop(0, pairs + 3, iteration, 0)

    def flat_end(unit, n):
        nx_copy(unit, n).wait_send()
        ny_copy(n).wait_send()
        for step in range(3):
            nz_copy(n, step).wait_send()

    def other_end(unit, p):
        ye_copy(unit, p).wait()
        yy_copy(unit, p).wait_send()
        yx_copy(p).wait_send()
        for step in range(3):
            yz_copy(p, step).wait_send()

    def finish(p):
        flat_end(2 * p, p)
        odd(p, flat_end, other_end)

    loop(pairs, finish)

    def out_copy(unit, act):
        @pl.when(unit < up_units)
        def _():
            act(pltpu.make_async_copy(done.at[unit], up_total.at[:, span(unit * width, width)], o_sem.at[unit]))

        @pl.when((unit >= up_units) & (unit < first_qkv))
        def _():
            act(pltpu.make_async_copy(done.at[unit], out_total.at[:, span((unit - up_units) * width, width)], o_sem.at[unit]))

        @pl.when((unit >= first_qkv) & (unit < first_in))
        def _():
            act(pltpu.make_async_copy(done.at[unit], qkv_total.at[:, span((unit - first_qkv) * width, width)], o_sem.at[unit]))

        @pl.when(unit >= first_in)
        def _():
            j = unit - first_in
            act(pltpu.make_async_copy(
                done.at[unit], in_total.at[span((j // 2) * PIECE, PIECE), span((j % 2) * width, width)], o_sem.at[unit]
            ))

    loop(units, lambda unit: out_copy(unit, start))
    for copy in v_copies + swap_copies:
        copy.wait_send()
    core_copy(units - 2, 0).wait_send()
    core_copy(units - 1, 1).wait_send()
    blocks = weight_ref.shape[0]
    patch_copy(blocks - 2, 0).wait()
    patch_copy(blocks - 1, 1).wait()
    loop(units, lambda unit: out_copy(unit, wait))


def back_and_reduce(turned, grad_pre, grad_resid, mine, got, sent, qkv_full, stream, weights, vectors, sums):
    rows, full = stream.shape
    width = full // 2
    owners, block, _ = weights.shape
    piece = full // owners
    columns = [grad_pre.shape[1], full, qkv_full.shape[4], full]
    plan = [c // width for c in columns]
    plan[3] *= block // piece
    views = [left.reshape(8, 2, piece, rows) for left in turned[:3]] + [turned[3].reshape(8, 2, block // piece, piece, rows)]
    units = sum(plan)
    pairs = units // 2
    flats, others = pairs + FLAT_PAIRS, pairs - FLAT_PAIRS
    assert piece == PIECE and plan[3] == owners and (plan[0] + plan[1]) % 2 == 0 and plan[2] == 6
    half = PIECE // 2
    dma = pltpu.SemaphoreType.DMA
    any_space = pl.BlockSpec(memory_space=pl.ANY)
    vmem = pl.BlockSpec(memory_space=pltpu.VMEM)

    def array(*shape):
        return jax.ShapeDtypeStruct(shape, F32)

    return pl.pallas_call(
        functools.partial(back_kernel, tuple(plan)),
        out_shape=[
            array(piece, columns[0]), array(piece, full), array(piece, columns[2]), array(block, full),
            array(rows, owners * block), array(*vectors.shape), array(*got.shape), array(*got.shape),
        ],
        in_specs=[any_space] * 15 + [vmem, vmem],
        out_specs=[any_space] * 5 + [vmem, any_space, any_space],
        scratch_shapes=[
            pltpu.VMEM((2, 2, 8, PIECE, rows), F32),
            pltpu.VMEM((2, rows, width), F32),
            pltpu.VMEM((rows, width), BF),
            pltpu.VMEM((rows, width), BF),
            pltpu.VMEM((2, 2, 4, 2, PIECE, width), F32),
            pltpu.VMEM((rows, full), BF),
            pltpu.VMEM((rows, full), BF),
            pltpu.VMEM((2, block, full), F32),
            pltpu.VMEM((2, rows, block), F32),
            pltpu.VMEM((4, 2, 2, PIECE, width), F32),
            pltpu.VMEM((rows, full), F32),
            pltpu.VMEM((units, 4, 2, PIECE, width), F32),
            pltpu.VMEM((flats, 4, PIECE, width), F32),
            pltpu.VMEM((flats, 3, PIECE, width), F32),
            pltpu.VMEM((flats, PIECE, width), F32),
            pltpu.VMEM((others, 4, 2, half, width), F32),
            pltpu.VMEM((others, 4, half, width), F32),
            pltpu.VMEM((others, 3, half, width), F32),
            pltpu.VMEM((units, PIECE, width), F32),
            pltpu.VMEM(vectors.shape, F32),
            pltpu.VMEM(vectors.shape, F32),
            pltpu.VMEM(vectors.shape, F32),
            pltpu.VMEM(vectors.shape, F32),
            pltpu.VMEM((3,) + vectors.shape, F32),
            dma((2, 5)), dma((2,)), dma((2,)), dma, dma((4,)), dma((2, 2)),
            dma((2, units)), dma((2, flats)), dma((2, flats, 3)), dma((2, flats)),
            dma((2, others)), dma((2, others)), dma((2, others, 3)), dma((2, others)),
            dma((2, 6)), dma((units,)),
        ],
        cost_estimate=pl.CostEstimate(
            flops=6 * rows * full * (units * 8 * PIECE + owners * block), bytes_accessed=130 * 10**6, transcendentals=0
        ),
        compiler_params=pltpu.CompilerParams(
            collective_id=0, has_side_effects=True, vmem_limit_bytes=67043328
        ),
        name="back_and_reduce",
    )(*views, grad_pre, grad_resid, *mine, got, *sent, qkv_full, stream, weights, vectors, sums)[:6]


CUT_ROWS = 128
CUT_COLUMNS = 128
NARROW = 384


def three(product, left, right):
    return product(left[0], right[0]) + product(left[0], right[1]) + product(left[1], right[0])


def normalized(values):
    average = jnp.mean(values, axis=-1, keepdims=True)
    centred = values - average
    spread = jnp.mean(centred * centred, axis=-1, keepdims=True)
    scale = lax.rsqrt(spread + EPSILON)
    return centred * scale, scale


def gather_kernel(patch_ref, in_ref, qkv_ref, out_ref, vector_ref,
                  stream_ref, normed_ref, turned_ref, patch_turned_ref, in_full, qkv_full, out_full, vectors_ref,
                  sent_0, sent_1, sent_2,
                  patch_buf, in_buf, qkv_buf, out_buf, turn_buf, acc, v_own, v_c, v_x, v_z, sent_buf,
                  z_sem, x_sem, y_sem, c_sem, v_sem, own_sem, patch_sem, turn_sem, full_sem, last_sem):
    fsdp = lax.axis_index("fsdp")
    row = lax.axis_index("sp")
    z, x, core = fsdp // 4, (fsdp // 2) % 2, fsdp % 2
    block, width = in_ref.shape
    across_count = width // CUT_COLUMNS
    in_units = (block // CUT_ROWS) * across_count
    narrow = NARROW
    out_units = width // narrow
    units = in_units + qkv_ref.shape[1] // narrow + out_units

    def device(z_at, x_at, core_at, row_at):
        return ((z_at * 2 + x_at) * 2 + core_at, row_at)

    sibling = device(z, x, 1 - core, row)
    beside = device(z, 1 - x, core, row)
    across = device(z, x, core, 1 - row)
    along = [device((z + step) % 4, x, core, row) for step in (1, 2, 3)]
    barrier = pltpu.get_barrier_semaphore()
    for peer in [sibling, beside, across] + along:
        pl.semaphore_signal(barrier, inc=1, device_id=peer, device_id_type=MESH)

    def remote(source, target, sems, index, peer):
        return pltpu.make_async_remote_copy(
            src_ref=source, dst_ref=target, send_sem=sems.at[(0,) + index], recv_sem=sems.at[(1,) + index],
            device_id=peer, device_id_type=MESH,
        )

    patch_copy = pltpu.make_async_copy(patch_ref, patch_buf, patch_sem)

    def span(first, size, step=None):
        return pl.ds(pl.multiple_of(first, step or size), size)

    def places(kind, unit, part):
        if kind == "in":
            j, column = unit // across_count, unit % across_count
            columns = span(column * CUT_COLUMNS, CUT_COLUMNS)
            base, rows, edge = j * CUT_ROWS, CUT_ROWS, 40
        else:
            rows, edge = out_ref.shape[0], 16
            first = in_units if kind == "qkv" else units - out_units
            base, columns = 0, span((unit - first) * narrow, narrow)
        if part is None:
            return span(base, rows, 8), columns
        which, side = part
        if which == 0:
            return span(base + side * (rows - edge), edge, 8), columns
        return span(base + side * edge, rows - edge, 8), columns

    sources = {"in": (in_ref, in_buf), "qkv": (qkv_ref, qkv_buf), "out": (out_ref, out_buf)}

    def each_kind(unit, act):
        ranges = (("in", 0, in_units), ("qkv", in_units, units - out_units), ("out", units - out_units, units))
        for kind, first, last in ranges:
            @pl.when((unit >= first) & (unit < last))
            def _(kind=kind):
                act(kind)

    own_copies = []
    for kind, firsts in (("in", range(0, block, CUT_ROWS)), ("qkv", (0,)), ("out", (0,))):
        source, buf = sources[kind]
        for first in firsts:
            rows = places(kind, first // CUT_ROWS * across_count if kind == "in" else in_units, (1, row))[0]
            own_copies.append(
                pltpu.make_async_copy(source.at[rows], buf.at[z, x, core, rows], own_sem.at[len(own_copies)])
            )

    def z_copy(kind, unit, step):
        source, buf = sources[kind]
        at = places(kind, unit, (1, row))
        return remote(source.at[at], buf.at[(z, x, core) + at], z_sem, (unit, step), along[step])

    def x_copy(kind, unit):
        ref = sources[kind][1].at[(slice(None), x, core) + places(kind, unit, (1, row))]
        return remote(ref, ref, x_sem, (unit,), beside)

    def y_copy(kind, unit):
        ref = sources[kind][1].at[(slice(None), slice(None), core) + places(kind, unit, (0, row))]
        return remote(ref, ref, y_sem, (unit,), across)

    def c_copy(kind, unit, index):
        part = (1, row) if index == 0 else (0, 1 - row)
        ref = sources[kind][1].at[(slice(None), slice(None), core) + places(kind, unit, part)]
        return remote(ref, ref, c_sem, (unit, index), sibling)

    def z_stage(unit):
        def act(kind):
            for step in range(3):
                z_copy(kind, unit, step).start()

        each_kind(unit, act)

    def x_stage(unit):
        def act(kind):
            for step in range(3):
                z_copy(kind, unit, step).wait_recv()
            x_copy(kind, unit).start()

        each_kind(unit, act)

    def spread_stage(unit):
        def act(kind):
            x_copy(kind, unit).wait_recv()
            y_copy(kind, unit).start()
            c_copy(kind, unit, 0).start()

        each_kind(unit, act)

    def y_stage(unit):
        def act(kind):
            y_copy(kind, unit).wait_recv()
            c_copy(kind, unit, 1).start()

        each_kind(unit, act)

    def ready(unit):
        def act(kind):
            c_copy(kind, unit, 0).wait_recv()
            c_copy(kind, unit, 1).wait_recv()
            full_copy(kind, unit).start()

        each_kind(unit, act)

    def full_copy(kind, unit):
        at = (slice(None), slice(None), slice(None)) + places(kind, unit, None)
        full = {"in": in_full, "qkv": qkv_full, "out": out_full}[kind]
        return pltpu.make_async_copy(sources[kind][1].at[at], full.at[at], full_sem.at[unit])

    def multiply(unit):
        j, column = unit // across_count, unit % across_count
        columns = span(column * CUT_COLUMNS, CUT_COLUMNS)
        rows = span(j * CUT_ROWS, CUT_ROWS)

        def step(pair, carry):
            first = pair * 2 * block + j * CUT_ROWS
            left = jnp.concatenate(
                [patch_buf[:, span(first, CUT_ROWS)], patch_buf[:, span(first + block, CUT_ROWS)]], axis=1
            )
            right = in_buf[pair // 2, pair % 2, :, rows, columns].reshape(2 * CUT_ROWS, CUT_COLUMNS)
            acc[:, columns] = acc[:, columns] + three(nn, split_bf(left), split_bf(right))
            return carry

        lax.fori_loop(0, 8, step, 0)

    tiles = patch_ref.shape[1] // LANES
    each = turn_buf.shape[0]

    def turn_copy(tile, slot):
        return pltpu.make_async_copy(turn_buf.at[slot], patch_turned_ref.at[span(tile * LANES, LANES)], turn_sem.at[slot])

    def turn(group):
        for slot in range(each):
            @pl.when(group > 0)
            def _(slot=slot):
                turn_copy((group - 1) * each + slot, slot).wait()

            turn_buf[slot] = jnp.transpose(patch_buf[:, span((group * each + slot) * LANES, LANES)])
            turn_copy(group * each + slot, slot).start()

    wide = jnp.concatenate([vector_ref[...], jnp.zeros((8, width - LANES), F32)], axis=1)
    v_own[...] = pltpu.roll(wide, fsdp * out_ref.shape[0], 1)
    pl.semaphore_wait(barrier, 6)
    z_stage(jnp.int32(0))
    z_stage(jnp.int32(1))
    for copy in own_copies:
        copy.start()
    patch_copy.start()
    v_copies = [
        remote(v_own, v_c, v_sem, (0,), sibling),
        remote(v_c, v_x, v_sem, (1,), beside),
    ] + [remote(v_x, v_z.at[step], v_sem, (2 + step,), along[step]) for step in range(3)]
    v_copies[0].start()
    acc[...] = jnp.zeros_like(acc)
    for copy in own_copies:
        copy.wait()

    sent_copies = [
        pltpu.make_async_copy(sent_buf.at[group], ref, last_sem.at[group])
        for group, ref in enumerate((sent_0, sent_1, sent_2))
    ]

    def iteration(t, carry):
        z_stage(t + 2)
        x_stage(t)
        spread_stage(t - 2)
        y_stage(t - 4)

        @pl.when(t == 0)
        def _():
            patch_copy.wait()
            v_copies[0].wait_recv()
            v_c[...] = v_c[...] + v_own[...]
            v_copies[1].start()

        @pl.when(t == 1)
        def _():
            v_copies[1].wait_recv()
            v_x[...] = v_x[...] + v_c[...]
            for step in range(3):
                v_copies[2 + step].start()

        @pl.when(t == 2)
        def _():
            for step in range(3):
                v_copies[2 + step].wait_recv()
            vectors_ref[...] = v_x[...] + v_z[0] + v_z[1] + v_z[2]

        @pl.when(t < tiles // each)
        def _():
            turn(t)

        ready(t - 5)

        @pl.when((t >= 5) & (t < in_units + 5))
        def _():
            multiply(t - 5)

        @pl.when(t == in_units + 5)
        def _():
            stream = acc[...]
            stream_ref[...] = stream
            zhat, _ = normalized(stream)
            acc[...] = zhat * vectors_ref[0:1, :] + vectors_ref[1:2, :]
            normed_ref[...] = acc[...]
            turned_ref[...] = jnp.transpose(acc[...])

        @pl.when(t == units - out_units + 4)
        def _():
            left = split_bf(acc[...])
            for group in range(3):
                right = jnp.concatenate(
                    [
                        qkv_buf[:, :, :, :, span(which * width + (1 - row) * (width // 2) + group * LANES, LANES)].reshape(
                            width, LANES
                        )
                        for which in range(3)
                    ],
                    axis=1,
                )
                sent_buf[group] = three(nn, left, split_bf(right))
                sent_copies[group].start()

        return carry

    lax.fori_loop(0, units + 5, iteration, 0)
    def finish(unit, carry):
        def act(kind):
            for step in range(3):
                z_copy(kind, unit, step).wait_send()
            x_copy(kind, unit).wait_send()
            y_copy(kind, unit).wait_send()
            c_copy(kind, unit, 0).wait_send()
            c_copy(kind, unit, 1).wait_send()
            full_copy(kind, unit).wait()

        each_kind(unit, act)
        return carry

    lax.fori_loop(0, units, finish, 0)
    for copy in v_copies:
        copy.wait_send()
    for slot in range(each):
        turn_copy(tiles - each + slot, slot).wait()
    for copy in sent_copies:
        copy.wait()


def gather_stream(patch_rows, w_in, w_qkv, w_out, vectors):
    rows, patch_width = patch_rows.shape
    block, width = w_in.shape
    piece, columns = w_qkv.shape
    group = columns // 6
    any_space = pl.BlockSpec(memory_space=pl.ANY)
    vmem = pl.BlockSpec(memory_space=pltpu.VMEM)
    dma = pltpu.SemaphoreType.DMA
    units = (block // CUT_ROWS) * (width // CUT_COLUMNS) + (columns + width) // NARROW
    owners = (4, 2, 2)

    def array(*shape):
        return jax.ShapeDtypeStruct(shape, F32)

    return pl.pallas_call(
        gather_kernel,
        out_shape=[
            array(rows, width), array(rows, width), array(width, rows), array(patch_width, rows),
            array(*owners, block, width), array(*owners, piece, columns), array(*owners, piece, width),
            array(8, width), array(rows, group), array(rows, group), array(rows, group),
        ],
        in_specs=[any_space] * 4 + [vmem],
        out_specs=[vmem, vmem, vmem] + [any_space] * 4 + [vmem] + [any_space] * 3,
        scratch_shapes=[
            pltpu.VMEM((rows, patch_width), F32),
            pltpu.VMEM(owners + (block, width), F32),
            pltpu.VMEM(owners + (piece, columns), F32),
            pltpu.VMEM(owners + (piece, width), F32),
            pltpu.VMEM((4, LANES, rows), F32),
            pltpu.VMEM((rows, width), F32),
            pltpu.VMEM((8, width), F32),
            pltpu.VMEM((8, width), F32),
            pltpu.VMEM((8, width), F32),
            pltpu.VMEM((3, 8, width), F32),
            pltpu.VMEM((3, rows, group), F32),
            dma((2, units, 3)), dma((2, units)), dma((2, units)), dma((2, units, 2)), dma((2, 5)),
            dma((block // CUT_ROWS + 2,)), dma, dma((4,)), dma((units,)), dma((3,)),
        ],
        cost_estimate=pl.CostEstimate(flops=6 * rows * patch_width * width, bytes_accessed=90 * 10**6, transcendentals=0),
        compiler_params=pltpu.CompilerParams(collective_id=1, has_side_effects=True, vmem_limit_bytes=67043328),
        name="gather_stream",
    )(patch_rows, w_in, w_qkv, w_out, vectors)


def own_kernel(pos_ref, normed_ref, q_ref, k_ref, v_ref, *outs):
    step = pl.program_id(0)
    weight = jnp.concatenate([ref[...].reshape(normed_ref.shape[1], LANES) for ref in (q_ref, k_ref, v_ref)], axis=1)
    product = three(nn, split_bf(normed_ref[...]), split_bf(weight))
    for i, ref in enumerate(outs):
        @pl.when(step == i)
        def _(ref=ref):
            ref[...] = product


def project_own(position, normed, qkv_full):
    rows, width = normed.shape
    owners, columns = qkv_full.shape[:4], qkv_full.shape[4]
    group = columns // 6
    return pl.pallas_call(
        own_kernel,
        grid_spec=pltpu.PrefetchScalarGridSpec(
            num_scalar_prefetch=1,
            grid=(3,),
            in_specs=[
                pl.BlockSpec((rows, width), lambda g, pos: (0, 0)),
                pl.BlockSpec(owners + (LANES,), lambda g, pos: (0, 0, 0, 0, pos[0] * 3 + g)),
                pl.BlockSpec(owners + (LANES,), lambda g, pos: (0, 0, 0, 0, 6 + pos[0] * 3 + g)),
                pl.BlockSpec(owners + (LANES,), lambda g, pos: (0, 0, 0, 0, 12 + pos[0] * 3 + g)),
            ],
            out_specs=[pl.BlockSpec((rows, group), lambda g, pos: (0, 0))] * 3,
        ),
        out_shape=[jax.ShapeDtypeStruct((rows, group), F32)] * 3,
        cost_estimate=pl.CostEstimate(flops=3 * rows * width * columns, bytes_accessed=8 * 10**6, transcendentals=0),
        compiler_params=pltpu.CompilerParams(vmem_limit_bytes=40 * 1024 * 1024),
        name="project_own",
    )(position, normed, qkv_full, qkv_full, qkv_full)


def gelu_and_slope(values):
    root = 0.7978845608028654
    square = values * values
    bent = jnp.tanh(root * (values + 0.044715 * values * square))
    half = 0.5 + 0.5 * bent
    slope = half + 0.5 * values * (1.0 - bent * bent) * (root * (1.0 + 0.134145 * square))
    return values * half, slope


def norm_back(grad, values, gain):
    zhat, scale = normalized(values)
    scaled = grad * gain
    back = scale * (
        scaled - jnp.mean(scaled, axis=-1, keepdims=True) - zhat * jnp.mean(scaled * zhat, axis=-1, keepdims=True)
    )
    return back, jnp.sum(grad * zhat, axis=0, keepdims=True), jnp.sum(grad, axis=0, keepdims=True)


def residual_kernel(pos_ref, *refs):
    own_parts, in_parts = refs[0:3], refs[3:6]
    (stream_ref, cot_ref, out_ref, vectors_ref,
     residual_ref, norm_high, norm_low, cot_high, cot_low, turned_ref, attended_ref) = refs[6:]
    half = out_ref.shape[0] // 2
    own = pl.ds(pl.multiple_of(pos_ref[0] * half, half), half)
    other = pl.ds(pl.multiple_of((1 - pos_ref[0]) * half, half), half)
    total = stream_ref[...]
    for span, parts in ((own, own_parts), (other, in_parts)):
        left = jnp.concatenate([part[...] for part in parts], axis=1)
        attended_ref[span, :] = jnp.transpose(left)
        total = total + three(nn, split_bf(left), split_bf(out_ref[span, :]))
    residual_ref[...] = total
    zhat, _ = normalized(total)
    normed = zhat * vectors_ref[2:3, :] + vectors_ref[3:4, :]
    turned_ref[...] = jnp.transpose(normed)
    norm_high[...], norm_low[...] = split_bf(normed)
    cot_high[...], cot_low[...] = split_bf(cot_ref[...])


def residual_norm(position, out_own, out_in, stream, cotangent, w_out, vectors):
    rows, width = stream.shape
    vmem = pl.BlockSpec(memory_space=pltpu.VMEM)

    def array(*shape, kind=F32):
        return jax.ShapeDtypeStruct(shape, kind)

    return pl.pallas_call(
        residual_kernel,
        in_specs=[pl.BlockSpec(memory_space=pltpu.SMEM)] + [vmem] * 10,
        out_specs=[vmem] * 7,
        out_shape=[array(rows, width)] + [array(rows, width, kind=BF)] * 4 + [array(width, rows)] * 2,
        cost_estimate=pl.CostEstimate(flops=6 * rows * width * width, bytes_accessed=18 * 10**6, transcendentals=0),
        compiler_params=pltpu.CompilerParams(vmem_limit_bytes=40 * 1024 * 1024),
        name="residual_norm",
    )(position, *out_own, *out_in, stream, cotangent, w_out, vectors)


def middle_kernel(pos_ref, *refs):
    (residual, norm_high, norm_low, cot_high, cot_low, cot_ref, out_ref, vectors_ref, up_ref, down_ref,
     block_ref, grad_pre_ref, grad_down_ref, grad_resid_ref) = refs[:14]
    sent_refs, own_refs, sums_ref, grad_norm = refs[14:17], refs[17:20], refs[20], refs[21]
    step = pl.program_id(0)
    width = out_ref.shape[0]
    half = width // 2
    own = pl.ds(pl.multiple_of(pos_ref[0] * half, half), half)
    other = pl.ds(pl.multiple_of((1 - pos_ref[0]) * half, half), half)

    @pl.when(step == 0)
    def _():
        block_ref[...] = residual[...]
        grad_norm[...] = jnp.zeros_like(grad_norm)

    up = split_bf(up_ref[...].reshape(width, width))
    hidden, slope = gelu_and_slope(three(nn, (norm_high[...], norm_low[...]), up))
    down = split_bf(down_ref[...].reshape(width, width))
    cot = (cot_high[...], cot_low[...])
    grad_pre = three(nt, cot, down) * slope
    grad_pre_ref[...] = grad_pre
    parts = split_bf(hidden)
    block_ref[...] = block_ref[...] + three(nn, parts, down)
    grad_down_ref[...] = three(tn, parts, cot).reshape(grad_down_ref.shape)
    grad_norm[...] = grad_norm[...] + three(nt, split_bf(grad_pre), up)

    @pl.when(step == pl.num_programs(0) - 1)
    def _():
        back, gain, offset = norm_back(grad_norm[...], residual[...], vectors_ref[2:3, :])
        grad = cot_ref[...] + back
        grad_resid_ref[...] = grad
        sums_ref[...] = jnp.zeros_like(sums_ref)
        sums_ref[2:3, :] = gain
        sums_ref[3:4, :] = offset
        left = split_bf(grad)
        for span, outs in ((other, sent_refs), (own, own_refs)):
            product = three(nt, left, split_bf(out_ref[span, :]))
            for i, ref in enumerate(outs):
                ref[...] = product[:, i * LANES:(i + 1) * LANES]


def middle(position, residual, norm, cot, cotangent, w_out, vectors, weights):
    rows, width = residual.shape
    owners, stacked = weights.shape[0], weights.shape[1]
    piece = width // owners
    steps = stacked // piece // 2
    whole = lambda *shape: pl.BlockSpec(shape, lambda j, *_: (0,) * len(shape))
    array = lambda *shape: jax.ShapeDtypeStruct(shape, F32)
    head = whole(rows, LANES)
    return pl.pallas_call(
        middle_kernel,
        grid_spec=pltpu.PrefetchScalarGridSpec(
            num_scalar_prefetch=1,
            grid=(steps,),
            in_specs=[whole(rows, width)] * 6 + [
                whole(width, width), whole(*vectors.shape),
                pl.BlockSpec((owners, piece, width), lambda j, *_: (0, j, 0)),
                pl.BlockSpec((owners // steps, steps * piece, width), lambda j, *_: (j, 1, 0)),
            ],
            out_specs=[
                whole(rows, width),
                pl.BlockSpec((rows, width), lambda j, *_: (0, j)),
                pl.BlockSpec((owners // steps, steps * piece, width), lambda j, *_: (j, 0, 0)),
                whole(rows, width),
            ] + [head] * 6 + [whole(*vectors.shape)],
            scratch_shapes=[pltpu.VMEM((rows, width), F32)],
        ),
        out_shape=[
            array(rows, width), array(rows, steps * width), array(owners, steps * piece, width), array(rows, width),
        ] + [array(rows, LANES)] * 6 + [array(*vectors.shape)],
        cost_estimate=pl.CostEstimate(
            flops=6 * rows * width * width * (5 * steps + 1), bytes_accessed=60 * 10**6, transcendentals=rows * steps * width
        ),
        compiler_params=pltpu.CompilerParams(vmem_limit_bytes=62 * 1024 * 1024),
        name="feed_forward",
    )(position, residual, *norm, *cot, cotangent, w_out, vectors, weights, weights)


def fast_shards(
    patches, segments, w_in, norm1_gain, norm1_bias, w_qkv, w_out, norm2_gain, norm2_bias, w_up, w_down, cotangent
):
    _, rows, patch_width = patches.shape
    piece, width = w_out.shape
    hidden = w_up.shape[1]
    owners = lax.axis_size("fsdp")
    position = lax.axis_index("sp")
    index = lax.axis_index("fsdp")
    places = position[None].astype(jnp.int32)
    labels = segments[0]
    length = labels.shape[0]
    labels_wide = jnp.broadcast_to(labels[:, None], (length, LANES))
    labels_row = labels.reshape(length // BLOCK, 1, BLOCK)
    blocks = hidden // width
    swap = [(0, 1), (1, 0)]

    vectors_own = jnp.pad(
        jnp.stack([norm1_gain, norm1_bias, norm2_gain, norm2_bias]), ((0, 4), (0, LANES - piece))
    )
    (stream, normed, normed_turned, patches_turned, in_full, qkv_full, out_full, vectors, *sent) = gather_stream(
        patches[0], w_in, w_qkv, w_out, vectors_own
    )
    up_own = w_up.reshape(piece, blocks, width).transpose(1, 0, 2).reshape(blocks * piece, width)
    stacked = jnp.concatenate([up_own, w_down], axis=0)
    stacked, _ = lax.optimization_barrier((stacked, vectors))
    weights = lax.all_gather(stacked, "fsdp", axis=0, tiled=True).reshape(owners, 2 * blocks * piece, width)
    received = [lax.ppermute(part, "sp", swap) for part in sent]
    own = project_own(places, normed, qkv_full)
    attended = [attend_forward(a, b, places, labels, labels_wide, labels_row) for a, b in zip(own, received)]
    out_in = [lax.ppermute(part[1], "sp", swap) for part in attended]
    w_out_full = out_full.reshape(width, width)
    residual, *split, normed_two_turned, attended_turned = residual_norm(
        places, [part[0] for part in attended], out_in, stream, cotangent[0], w_out_full, vectors
    )
    block_out, grad_pre, grad_down, grad_resid, *grads = middle(
        places, residual, split[:2], split[2:], cotangent[0], w_out_full, vectors, weights
    )
    grad_sent, grad_own, sums = grads[:3], grads[3:6], grads[6]
    down_part = lax.psum_scatter(
        grad_down.reshape(hidden, width), "fsdp", scatter_dimension=0, tiled=True
    )
    grad_in = [lax.ppermute(part, "sp", swap) for part in grad_sent]
    both = [
        attend_backward(own[i], received[i], attended[i][0], attended[i][1], grad_own[i], grad_in[i], attended[i][2],
                        places, labels, labels_wide, labels_row)
        for i in range(3)
    ]
    mine = [pair[0] for pair in both]
    got = lax.ppermute(both[0][1], "sp", swap)
    grad_up, grad_out, grad_qkv, grad_w_in, grad_patch, vector_sums = back_and_reduce(
        [normed_two_turned, attended_turned, normed_turned, patches_turned], grad_pre, grad_resid,
        mine, got, [both[1][1], both[2][1]], qkv_full, stream, in_full.reshape(owners, in_full.shape[3], width), vectors, sums,
    )
    vector_sums = lax.dynamic_slice(vector_sums, (0, index * piece), (4, piece))
    down_part, _ = lax.optimization_barrier((down_part, grad_out))
    total_down = down_part + lax.ppermute(down_part, "sp", swap)
    grad_patch = grad_patch * lax.optimization_barrier(jnp.float32(1.0))
    return (
        block_out[None], grad_patch[None], grad_w_in, vector_sums[0], vector_sums[1],
        grad_qkv, grad_out, vector_sums[2], vector_sums[3], grad_up, total_down,
    )


def solution(mesh):
    sharded = P("fsdp", "sp", None)
    matrix = P("fsdp", None)
    vector = P("fsdp")
    fast = mesh.shape["fsdp"] == 16 and mesh.shape["sp"] == 2
    return jax.shard_map(
        fast_shards if fast else shards,
        mesh=mesh,
        in_specs=(sharded, matrix, matrix, vector, vector, matrix, matrix, vector, vector, matrix, matrix, sharded),
        out_specs=(sharded, sharded, matrix, vector, vector, matrix, matrix, vector, vector, matrix, matrix),
        check_vma=False,
    )
```
